32 devices in a mesh: parts: 2 (over y), seq: 4 (over z), strand: 2 (over core), mp: 2 (over x).
Axes of the slice: x: 2, y: 2, z: 4, core: 2. Of those that a mesh axis runs over, the one named last changes fastest.
Arguments:
- hidden: bfloat16 [4096, 1024], P(('parts', 'seq'), 'mp'), parts along dimension 0, may hold values from -6 to 6
- breaks: int32 [4096], P('parts'), parts along dimension 0, may hold values 0 or 1
- cotangent: bfloat16 [4096, 1024], P(('parts', 'seq'), 'mp'), parts along dimension 0, may hold values from -0.059814453 to 0.059814453
- input_weight: bfloat16 [1024, 2048], P(('seq', 'strand'), 'mp'), may hold values from -0.1875 to 0.1875
- gate_weight: bfloat16 [1024, 2048], P(('seq', 'strand'), 'mp'), may hold values from -0.1875 to 0.1875
- key_weight: bfloat16 [1024, 1024], P(('seq', 'strand'), 'mp'), may hold values from -0.0625 to 0.0625
- query_weight: bfloat16 [1024, 1024], P(('seq', 'strand'), 'mp'), may hold values from -0.0625 to 0.0625
- step_weight: bfloat16 [1024, 32], P(('seq', 'strand'), 'mp'), may hold values from -0.1875 to 0.1875
- output_weight: bfloat16 [1024, 2048], P(('seq', 'strand'), 'mp'), may hold values from -0.125 to 0.125
- step_bias: float32 [32], P('mp'), may hold values from -4.5 to -2
- decay_log: float32 [32], P('mp'), may hold values from -13 to 0
- skip_gain: float32 [32], P('mp'), may hold values from 0.5 to 2
Outputs:
- combined: bfloat16 [4096, 1024], P(('parts', 'seq'), 'mp'), parts along dimension 0
- grad_input: float32 [2048, 2048], P(('parts', 'seq', 'strand'), 'mp'), parts along dimension 0
- grad_gate: float32 [2048, 2048], P(('parts', 'seq', 'strand'), 'mp'), parts along dimension 0
- grad_key: float32 [2048, 1024], P(('parts', 'seq', 'strand'), 'mp'), parts along dimension 0
- grad_query: float32 [2048, 1024], P(('parts', 'seq', 'strand'), 'mp'), parts along dimension 0
- grad_step: float32 [2048, 32], P(('parts', 'seq', 'strand'), 'mp'), parts along dimension 0
- grad_output: float32 [2048, 2048], P(('parts', 'seq', 'strand'), 'mp'), parts along dimension 0
The draws below stay inside these ranges and needn't reach their ends.
There are 2 independent parts, one for each index of `parts`. The reference program is written for one: setup_inputs(seed, part) draws one part's arguments, and reference() takes and returns one part's arrays. A program takes and returns all parts, laid end to end along the dimension named above; an argument that names none is the same for every part. Nothing has to cross between parts.
All inputs are finite; a program needn't handle non-finite values.
Results may differ from the reference program's by a relative error of at most 0.02.
Values may be sent and summed in bfloat16 or wider, within the bound.
A program may use at most 128 MiB of HBM per device.

```python
import math
from functools import partial
import jax
import jax.numpy as jnp
from jax import lax

D = 1024
HEADS = 32
HEAD_DIM = 64
STATE = 128
GROUPS = 8
STRETCH = 256
TOK_DEV = 512
INNER = 2048
SEQ_LEN = 2048
N_MP = 2


def draw_decay_log(key, part):
    key_pick, key_slow, key_fast = jax.random.split(key, 3)
    fast_share = 0.5
    is_fast = jax.random.uniform(key_pick, (HEADS,), jnp.float32) < fast_share
    slow_rate = jax.random.uniform(key_slow, (HEADS,), jnp.float32, math.log(0.2 / SEQ_LEN), math.log(5.0 / SEQ_LEN))
    fast_rate = jax.random.uniform(key_fast, (HEADS,), jnp.float32, math.log(0.15), math.log(0.6))
    return jnp.where(is_fast, fast_rate, slow_rate).astype(jnp.float32)


def set_ends(entries, stream_key, least, largest):
    longest = entries.shape.index(max(entries.shape))
    spots = []
    for shift in (0, 1):
        where = [jax.random.randint(jax.random.fold_in(stream_key, axis), (), 0, length) for axis, length in enumerate(entries.shape)]
        where[longest] = (where[longest] + shift) % entries.shape[longest]
        spots.append(tuple(where))
    return entries.at[spots[0]].set(least).at[spots[1]].set(largest)


def block_scale(rng, extent, cuts, least, top_value):
    factor_of, own = 1.0, jax.random.fold_in(rng, 6)
    for position, shards_of in cuts:
        heights = jnp.exp(jax.random.uniform(jax.random.fold_in(own, position), (shards_of,), jnp.float32, least / len(cuts), top_value / len(cuts)))
        factor_of = factor_of * jnp.repeat(heights, extent[position] // shards_of).reshape([-1 if axis == position else 1 for axis in range(len(extent))])
    return factor_of


def noise(rng, shape, deviation, limit, cuts=(), kind=jnp.bfloat16):
    gain = block_scale(rng, shape, cuts, -0.22, 0.18) if cuts else 1.0
    entries = jax.random.normal(rng, shape, jnp.float32) * deviation * gain
    return jnp.minimum(jnp.maximum(entries, -limit), limit).astype(kind)


def setup_inputs(seed: int = 0, part: int = 0) -> dict:
    key_list = jax.random.split(jax.random.key(seed), 13)
    part_keys = jax.random.split(jax.random.fold_in(key_list[12], part), 13)
    hidden = noise(part_keys[0], (SEQ_LEN, D), 1.0, 6.0, ((0, 4), (1, 2)))
    breaks = set_ends((jax.random.randint(part_keys[1], (SEQ_LEN,), 0, SEQ_LEN) < 5).astype(jnp.int32), jax.random.fold_in(part_keys[1], 1), 0, 1)
    cotangent = noise(part_keys[2], (SEQ_LEN, D), 0.01, 0.059814453, ((0, 4), (1, 2)))
    input_weight = noise(key_list[3], (D, INNER), D ** -0.5, 0.1875, ((0, 8), (1, 2)))
    gate_weight = noise(key_list[4], (D, INNER), D ** -0.5, 0.1875, ((0, 8), (1, 2)))
    key_weight = noise(key_list[5], (D, GROUPS * STATE), (8 * D) ** -0.5, 0.0625, ((0, 8), (1, 2)))
    query_weight = noise(key_list[6], (D, GROUPS * STATE), (8 * D) ** -0.5, 0.0625, ((0, 8), (1, 2)))
    step_weight = noise(key_list[7], (D, HEADS), D ** -0.5, 0.1875, ((0, 8), (1, 2)))
    output_weight = noise(key_list[8], (D, INNER), INNER ** -0.5, 0.125, ((0, 8), (1, 2)))
    step_bias = jnp.clip(-4.5 + 2.5 * jax.random.uniform(key_list[9], (HEADS,), jnp.float32) ** block_scale(key_list[9], (HEADS,), ((0, 2),), -0.2, 0.2), -4.5, -2.0)
    decay_log = draw_decay_log(jax.random.fold_in(key_list[12], 71), part)
    skip_gain = jnp.clip(0.5 + 1.5 * jax.random.uniform(key_list[11], (HEADS,), jnp.float32) ** block_scale(key_list[11], (HEADS,), ((0, 2),), -0.2, 0.2), 0.5, 2.0)
    return {"hidden": hidden, "breaks": breaks, "cotangent": cotangent, "input_weight": input_weight, "gate_weight": gate_weight, "key_weight": key_weight, "query_weight": query_weight, "step_weight": step_weight, "output_weight": output_weight, "step_bias": step_bias, "decay_log": decay_log, "skip_gain": skip_gain}


KEEP_LOG = -0.35667494393873245
EPSILON = 1e-05

def block_terms(step_bias, decay_log, break_marks, inner_vals, key_vals, query_vals, step_raw):
    length = inner_vals.shape[0]
    blocks = length // STRETCH
    head_count = inner_vals.shape[1]
    groups = key_vals.shape[1]
    per_group = head_count // groups
    step_size = jax.nn.softplus(step_raw + step_bias)
    log_rates = -jnp.exp(decay_log) * step_size + KEEP_LOG * break_marks[:, None]
    log_decay = jnp.cumsum(log_rates.reshape(blocks, STRETCH, head_count), axis=1)
    step_blocks = step_size.reshape(blocks, STRETCH, head_count)
    key_blocks = key_vals.reshape(blocks, STRETCH, groups, -1).astype(jnp.float32)
    query_blocks = query_vals.reshape(blocks, STRETCH, groups, -1).astype(jnp.float32)
    inner_blocks = inner_vals.reshape(blocks, STRETCH, groups, per_group, -1)
    scores = jnp.einsum('cqgn,ckgn->cgqk', query_blocks, key_blocks, precision=lax.Precision.HIGHEST)
    decay_rows = jnp.transpose(log_decay, (0, 2, 1)).reshape(blocks, groups, per_group, STRETCH)
    step_rows = jnp.transpose(step_blocks, (0, 2, 1)).reshape(blocks, groups, per_group, STRETCH)
    causal = lax.broadcasted_iota(jnp.int32, (STRETCH, STRETCH), 0) >= lax.broadcasted_iota(jnp.int32, (STRETCH, STRETCH), 1)
    spread = decay_rows[..., :, None] - decay_rows[..., None, :]
    within = jnp.where(causal, jnp.exp(jnp.where(causal, spread, 0.0)), 0.0)
    mixing = (scores[:, :, None] * within * step_rows[..., None, :]).astype(jnp.bfloat16)
    local_out = jnp.einsum('cghqk,ckghp->cqghp', mixing.astype(jnp.float32), inner_blocks.astype(jnp.float32), precision=lax.Precision.HIGHEST)
    to_end = (jnp.exp(log_decay[:, -1:, :] - log_decay) * step_blocks).reshape(blocks, STRETCH, groups, per_group)
    weighted = (inner_blocks * to_end[..., None]).astype(jnp.bfloat16)
    block_states = jnp.einsum('cqghp,cqgn->cghpn', weighted.astype(jnp.float32), key_blocks, precision=lax.Precision.HIGHEST)
    block_decay = jnp.exp(log_decay[:, -1, :]).reshape(blocks, groups, per_group)

    def advance(running, current):
        kept_decay, kept_state = running
        decay_now, state_now = current
        return ((kept_decay * decay_now, decay_now[..., None, None] * kept_state + state_now), (kept_decay, kept_state))
    initial = (jnp.ones(block_decay.shape[1:], jnp.float32), jnp.zeros(block_states.shape[1:], jnp.float32))
    totals, priors = lax.scan(advance, initial, (block_decay, block_states))
    return (local_out, priors[1], priors[0], log_decay, totals[0], totals[1])

def finish_terms(skip_gain, local_out, prior_state, prior_decay, log_decay, total_decay, total_state, query_vals, inner_vals, entering):
    blocks = log_decay.shape[0]
    groups = query_vals.shape[1]
    per_group = inner_vals.shape[1] // groups
    states = prior_state + prior_decay[..., None, None] * entering
    query_full = query_vals.reshape(blocks, STRETCH, groups, -1).astype(jnp.float32)
    carried = jnp.einsum('cqgn,cghpn->cqghp', query_full, states, precision=lax.Precision.HIGHEST)
    growth = jnp.exp(log_decay).reshape(blocks, STRETCH, groups, per_group)
    inner_full = inner_vals.reshape(blocks, STRETCH, groups, per_group, -1).astype(jnp.float32)
    mixer_out = local_out + growth[..., None] * carried + skip_gain.reshape(groups, per_group)[:, :, None] * inner_full
    leaving = total_decay[..., None, None] * entering + total_state
    return (mixer_out.reshape(blocks * STRETCH, groups, -1), leaving)

def gate_terms(mixer_out, gate_vals):
    product = mixer_out * jax.nn.silu(gate_vals.astype(jnp.float32))
    scaled = product * lax.rsqrt(lax.optimization_barrier(jnp.mean(product * product, axis=-1, keepdims=True)) + EPSILON)
    return scaled.astype(jnp.bfloat16)

def group_mixer(bias_part, log_part, skip_part, break_marks, inner_vals, gate_vals, key_vals, query_vals, step_raw):
    length = inner_vals.shape[0]
    inner_heads = inner_vals.reshape(length, -1, HEAD_DIM)
    key_heads = key_vals.reshape(length, 1, -1)
    query_heads = query_vals.reshape(length, 1, -1)
    local_terms = block_terms(bias_part, log_part, break_marks, inner_heads, key_heads, query_heads, step_raw)
    entering = jnp.zeros(local_terms[5].shape, jnp.float32)
    mixer_out, leaving = finish_terms(skip_part, *local_terms, query_heads, inner_heads, entering)
    return gate_terms(mixer_out, gate_vals.reshape(length, 1, -1)).reshape(length, -1)

def block_grad(left_side, right_side):
    block_count = left_side.shape[0] // TOK_DEV
    left_blocks = left_side.astype(jnp.float32).reshape(block_count, TOK_DEV, -1)
    right_blocks = right_side.astype(jnp.float32).reshape(block_count, TOK_DEV, -1)
    products = jnp.einsum('btd,btk->bdk', left_blocks, right_blocks, precision=lax.Precision.HIGHEST)
    rounded = lax.optimization_barrier(products.astype(jnp.bfloat16))
    return lax.optimization_barrier(jnp.sum(rounded.astype(jnp.float32), axis=0))

def reference(hidden, breaks, cotangent, input_weight, gate_weight, key_weight, query_weight, step_weight, output_weight, step_bias, decay_log, skip_gain):
    per_group = HEADS // GROUPS
    width_group = per_group * HEAD_DIM
    per_shard = GROUPS // N_MP
    all_marks = breaks.astype(jnp.float32)
    grad_input = jnp.zeros(input_weight.shape, jnp.float32)
    grad_gate = jnp.zeros(gate_weight.shape, jnp.float32)
    grad_key = jnp.zeros(key_weight.shape, jnp.float32)
    grad_query = jnp.zeros(query_weight.shape, jnp.float32)
    grad_step = jnp.zeros(step_weight.shape, jnp.float32)
    grad_output = jnp.zeros(output_weight.shape, jnp.float32)
    strand_totals = []
    for strand_index in range(2):
        if strand_index == 0:
            source = hidden
            break_marks = all_marks
            grads_in = cotangent
        else:
            source = jnp.flip(hidden, (0, 1))
            break_marks = jnp.flip(all_marks)
            grads_in = jnp.flip(cotangent, (0, 1))
        inner_all = jnp.dot(source, input_weight, preferred_element_type=jnp.float32).astype(jnp.bfloat16)
        gate_all = jnp.dot(source, gate_weight, preferred_element_type=jnp.float32).astype(jnp.bfloat16)
        key_all = jnp.dot(source, key_weight, preferred_element_type=jnp.float32).astype(jnp.bfloat16)
        query_all = jnp.dot(source, query_weight, preferred_element_type=jnp.float32).astype(jnp.bfloat16)
        step_all = jnp.dot(source, step_weight, preferred_element_type=jnp.float32)
        strand_total = jnp.zeros((SEQ_LEN, D), jnp.float32)
        shard_sum = jnp.zeros((SEQ_LEN, D), jnp.float32)
        for group_index in range(GROUPS):
            col_span = slice(group_index * width_group, (group_index + 1) * width_group)
            key_span = slice(group_index * STATE, (group_index + 1) * STATE)
            head_span = slice(group_index * per_group, (group_index + 1) * per_group)
            apply_group = partial(group_mixer, step_bias[head_span], decay_log[head_span], skip_gain[head_span], break_marks)
            gated, pullback = jax.vjp(apply_group, inner_all[:, col_span], gate_all[:, col_span], key_all[:, key_span], query_all[:, key_span], step_all[:, head_span])
            out_columns = output_weight[:, col_span]
            shard_sum = shard_sum + lax.dot_general(gated, out_columns, (((1,), (1,)), ((), ())), preferred_element_type=jnp.float32)
            if (group_index + 1) % per_shard == 0:
                strand_total = strand_total + lax.optimization_barrier(shard_sum.astype(jnp.bfloat16)).astype(jnp.float32)
                shard_sum = jnp.zeros((SEQ_LEN, D), jnp.float32)
            gated_back = jnp.dot(grads_in, out_columns, preferred_element_type=jnp.float32).astype(jnp.bfloat16)
            inner_back, gate_back, key_back, query_back, step_back = pullback(gated_back)
            grad_input = grad_input.at[:, col_span].add(block_grad(source, inner_back))
            grad_gate = grad_gate.at[:, col_span].add(block_grad(source, gate_back))
            grad_key = grad_key.at[:, key_span].add(block_grad(source, key_back))
            grad_query = grad_query.at[:, key_span].add(block_grad(source, query_back))
            grad_step = grad_step.at[:, head_span].add(block_grad(source, step_back))
            grad_output = grad_output.at[:, col_span].add(block_grad(grads_in, gated))
        strand_totals.append(strand_total)
    combined = (strand_totals[0] + jnp.flip(strand_totals[1], (0, 1))).astype(jnp.bfloat16)
    return (combined, grad_input, grad_gate, grad_key, grad_query, grad_step, grad_output)
```

```python
from functools import partial

import jax
import jax.numpy as jnp
from jax import lax
from jax.experimental import pallas as pl
from jax.experimental.pallas import tpu as pltpu
from jax.sharding import PartitionSpec as P

HEAD_DIM = 64
STATE = 128
STRETCH = 256


KEEP_LOG = -0.35667494393873245
EPSILON = 1e-05
HIGHEST = lax.Precision.HIGHEST


def swap(value, axis):
    size = lax.axis_size(axis)
    return lax.ppermute(value, axis, [(i, size - 1 - i) for i in range(size)])


def earlier_than(count, backward):
    row = lax.broadcasted_iota(jnp.int32, (count, count), 0)
    column = lax.broadcasted_iota(jnp.int32, (count, count), 1)
    return jnp.where(backward, column > row, column < row)


def chain_weights(before, logs):
    steps = before.astype(jnp.float32)
    between = steps[:, None, :] * jnp.transpose(steps)[None, :, :]
    spans = jnp.sum(between[..., None] * logs[None, None], axis=2)
    return jnp.where(before[..., None], jnp.exp(spans), 0.0)


def block_terms(
    backward, step_bias, decay_log, break_marks, inner_vals, key_vals, query_vals, step_raw
):
    length = inner_vals.shape[0]
    blocks = length // STRETCH
    head_count = inner_vals.shape[1]
    groups = key_vals.shape[1]
    per_group = head_count // groups
    before = earlier_than(STRETCH, backward)
    row = lax.broadcasted_iota(jnp.int32, (STRETCH, STRETCH), 0)
    column = lax.broadcasted_iota(jnp.int32, (STRETCH, STRETCH), 1)
    causal = before | (row == column)
    step_size = jax.nn.softplus(step_raw + step_bias)
    log_rates = -jnp.exp(decay_log) * step_size + KEEP_LOG * break_marks[:, None]
    rate_rows = jnp.transpose(log_rates.reshape(blocks, STRETCH, head_count), (0, 2, 1))
    step_rows = jnp.transpose(step_size.reshape(blocks, STRETCH, head_count), (0, 2, 1))
    log_rows = jnp.einsum("chj,ij->chi", rate_rows, causal.astype(jnp.float32), precision=HIGHEST)
    ends = jnp.sum(rate_rows, axis=-1)
    end_rows = jnp.exp(ends[..., None] - log_rows) * step_rows
    log_decay = jnp.transpose(log_rows, (0, 2, 1))
    key_blocks = key_vals.reshape(blocks, STRETCH, groups, -1)
    query_blocks = query_vals.reshape(blocks, STRETCH, groups, -1)
    inner_blocks = inner_vals.reshape(blocks, STRETCH, groups, per_group, -1)
    scores = jnp.einsum(
        "cqgn,ckgn->cgqk", query_blocks, key_blocks, preferred_element_type=jnp.float32
    )
    decay_rows = log_rows.reshape(blocks, groups, per_group, STRETCH)
    step_heads = step_rows.reshape(blocks, groups, per_group, STRETCH)
    spread = decay_rows[..., :, None] - decay_rows[..., None, :]
    within = jnp.where(causal, jnp.exp(jnp.where(causal, spread, 0.0)), 0.0)
    mixing = (scores[:, :, None] * within * step_heads[..., None, :]).astype(jnp.bfloat16)
    local_out = jnp.einsum(
        "cghqk,ckghp->cqghp", mixing, inner_blocks, preferred_element_type=jnp.float32
    )
    to_end = jnp.transpose(end_rows, (0, 2, 1)).reshape(blocks, STRETCH, groups, per_group)
    weighted = (inner_blocks * to_end[..., None]).astype(jnp.bfloat16)
    block_states = jnp.einsum(
        "cqghp,cqgn->cghpn", weighted, key_blocks, preferred_element_type=jnp.float32
    )
    order = earlier_than(blocks, backward)
    head_shape = (groups, per_group)
    weights = chain_weights(order, ends).reshape((blocks, blocks) + head_shape)
    prior_state = jnp.stack(
        [
            sum(
                weights[c, k][..., None, None] * block_states[k] for k in range(blocks) if k != c
            )
            if blocks > 1
            else jnp.zeros_like(block_states[0])
            for c in range(blocks)
        ]
    )
    order_f = order.astype(jnp.float32)
    prior_logs = jnp.sum(order_f[:, :, None] * ends[None], axis=1)
    later_logs = jnp.sum(jnp.transpose(order_f)[:, :, None] * ends[None], axis=1)
    prior_decay = jnp.exp(prior_logs).reshape((blocks,) + head_shape)
    later_decay = jnp.exp(later_logs).reshape((blocks,) + head_shape)
    total_state = sum(later_decay[c][..., None, None] * block_states[c] for c in range(blocks))
    total_log = jnp.sum(ends, axis=0)
    return (local_out, prior_state, prior_decay, log_decay, total_log, total_state)


def finish_terms(
    skip_gain,
    local_out,
    prior_state,
    prior_decay,
    log_decay,
    query_vals,
    inner_vals,
    entering,
):
    blocks = log_decay.shape[0]
    groups = query_vals.shape[1]
    per_group = inner_vals.shape[1] // groups
    states = prior_state + prior_decay[..., None, None] * entering
    query_full = query_vals.reshape(blocks, STRETCH, groups, -1).astype(jnp.float32)
    carried = jnp.einsum("cqgn,cghpn->cqghp", query_full, states, precision=HIGHEST)
    growth = jnp.exp(log_decay).reshape(blocks, STRETCH, groups, per_group)
    inner_full = inner_vals.reshape(blocks, STRETCH, groups, per_group, -1).astype(jnp.float32)
    mixer_out = (
        local_out
        + growth[..., None] * carried
        + skip_gain.reshape(groups, per_group)[:, :, None] * inner_full
    )
    return mixer_out.reshape(blocks * STRETCH, groups, -1)


def gate_terms(mixer_out, gate_vals):
    product = mixer_out * jax.nn.silu(gate_vals.astype(jnp.float32))
    scaled = product * lax.rsqrt(jnp.mean(product * product, axis=-1, keepdims=True) + EPSILON)
    return scaled.astype(jnp.bfloat16)


def gather_kernel(peers, halves, *refs):
    shards, rows, fulls, all_rows = refs[:2], refs[2], refs[3:5], refs[5]
    local_sem, z_send, z_recv, y_send, y_recv, s_send, s_recv, o_send, o_recv, x_send, x_recv = refs[6:]
    part = lax.axis_index("parts")
    seq = lax.axis_index("seq")
    strand = lax.axis_index("strand")
    model = lax.axis_index("mp")
    twin = {"parts": 1 - part}
    mate = {"strand": 1 - strand}
    others = [lax.rem(seq + d, peers) for d in range(1, peers)]
    models = [lax.rem(model + d, halves) for d in range(1, halves)]

    def remote(source, target, send, receive, device):
        return pltpu.make_async_remote_copy(
            src_ref=source,
            dst_ref=target,
            send_sem=send,
            recv_sem=receive,
            device_id=device,
            device_id_type=pl.DeviceIdType.MESH,
        )

    barrier = pltpu.get_barrier_semaphore()
    targets = [{"seq": t} for t in others] + [{"mp": m} for m in models] + [twin, mate]
    for target in targets:
        pl.semaphore_signal(
            barrier, inc=1, device_id=target, device_id_type=pl.DeviceIdType.MESH
        )
    pl.semaphore_wait(barrier, len(targets))

    sends = []
    locals_ = []

    def go(copy):
        copy.start()
        sends.append(copy)

    for w in range(2):
        for d, t in enumerate(others):
            go(
                remote(
                    shards[w].at[part],
                    fulls[w].at[0, seq, part],
                    z_send.at[w, d],
                    z_recv.at[w, seq],
                    {"seq": t},
                )
            )
    for d, m in enumerate(models):
        go(remote(rows, all_rows.at[model], x_send.at[d], x_recv.at[model], {"mp": m}))
    for w in range(2):
        go(remote(shards[w], fulls[w].at[1, seq], o_send.at[w], o_recv.at[w], mate))
        copy = pltpu.make_async_copy(shards[w], fulls[w].at[0, seq], local_sem.at[w])
        copy.start()
        locals_.append(copy)
    copy = pltpu.make_async_copy(rows, all_rows.at[model], local_sem.at[2])
    copy.start()
    locals_.append(copy)

    for w in range(2):
        full = fulls[w]
        for d, t in enumerate(others):
            mine = full.at[0, t, part]
            remote(mine, mine, z_send.at[w, d], z_recv.at[w, t], {"seq": t}).wait_recv()
            go(remote(mine, mine, y_send.at[w, d], y_recv.at[w, t], twin))
            go(remote(mine, full.at[1, t, part], s_send.at[w, d, 0], s_recv.at[w, t, part], mate))
    for w in range(2):
        full = fulls[w]
        for d, t in enumerate(others):
            theirs = full.at[0, t, 1 - part]
            remote(theirs, theirs, y_send.at[w, d], y_recv.at[w, t], twin).wait_recv()
            go(
                remote(
                    theirs,
                    full.at[1, t, 1 - part],
                    s_send.at[w, d, 1],
                    s_recv.at[w, t, 1 - part],
                    mate,
                )
            )
    for w in range(2):
        full = fulls[w]
        own = full.at[1, seq]
        remote(own, own, o_send.at[w], o_recv.at[w], mate).wait_recv()
        for d, t in enumerate(others):
            for h in range(2):
                block = full.at[1, t, h]
                remote(block, block, s_send.at[w, d, h], s_recv.at[w, t, h], mate).wait_recv()
    for d, m in enumerate(models):
        block = all_rows.at[m]
        remote(block, block, x_send.at[d], x_recv.at[m], {"mp": m}).wait_recv()
    for copy in sends:
        copy.wait_send()
    for copy in locals_:
        copy.wait()


def gather_all(first, second, rows):
    peers, halves = (lax.axis_size("seq"), lax.axis_size("mp"))
    depth = first.shape[0] // 2
    shards = tuple(a.reshape(2, depth, -1) for a in (first, second))
    anywhere = pl.BlockSpec(memory_space=pl.ANY)
    dma = pltpu.SemaphoreType.DMA
    out = pl.pallas_call(
        partial(gather_kernel, peers, halves),
        out_shape=tuple(
            jax.ShapeDtypeStruct((2, peers) + a.shape, a.dtype) for a in shards
        )
        + (jax.ShapeDtypeStruct((halves,) + rows.shape, rows.dtype),),
        in_specs=[anywhere] * 3,
        out_specs=(anywhere,) * 3,
        scratch_shapes=[
            dma((3,)),
            dma((2, peers)),
            dma((2, peers)),
            dma((2, peers)),
            dma((2, peers)),
            dma((2, peers, 2)),
            dma((2, peers, 2)),
            dma((2,)),
            dma((2,)),
            dma((halves,)),
            dma((halves,)),
        ],
        compiler_params=pltpu.CompilerParams(collective_id=0, has_side_effects=True),
    )(*shards, rows)
    return (
        out[0].reshape(4 * peers * depth, -1),
        out[1].reshape(4 * peers * depth, -1),
        out[2],
    )


def exchange_kernel(peers, count, *refs):
    sources, targets = refs[:count], refs[count : 2 * count]
    local_sem, send_sem, recv_sem = refs[2 * count :]
    seq = lax.axis_index("seq")
    others = [lax.rem(seq + d, peers) for d in range(1, peers)]

    barrier = pltpu.get_barrier_semaphore()
    for t in others:
        pl.semaphore_signal(
            barrier, inc=1, device_id={"seq": t}, device_id_type=pl.DeviceIdType.MESH
        )
    pl.semaphore_wait(barrier, len(others))

    started = []
    for w in range(count):
        for d, t in enumerate(others):
            copy = pltpu.make_async_remote_copy(
                src_ref=sources[w].at[t],
                dst_ref=targets[w].at[seq],
                send_sem=send_sem.at[w, d],
                recv_sem=recv_sem.at[w, seq],
                device_id={"seq": t},
                device_id_type=pl.DeviceIdType.MESH,
            )
            copy.start()
            started.append(copy)
    own = [
        pltpu.make_async_copy(sources[w].at[seq], targets[w].at[seq], local_sem.at[w])
        for w in range(count)
    ]
    for copy in own:
        copy.start()
    for w in range(count):
        for d, t in enumerate(others):
            block = targets[w].at[t]
            pltpu.make_async_remote_copy(
                src_ref=block,
                dst_ref=block,
                send_sem=send_sem.at[w, d],
                recv_sem=recv_sem.at[w, t],
                device_id={"seq": t},
                device_id_type=pl.DeviceIdType.MESH,
            ).wait_recv()
    for copy in started:
        copy.wait_send()
    for copy in own:
        copy.wait()


def exchange(values):
    peers = lax.axis_size("seq")
    count = len(values)
    blocks = tuple(v.reshape(peers, v.shape[0] // peers, -1) for v in values)
    anywhere = pl.BlockSpec(memory_space=pl.ANY)
    dma = pltpu.SemaphoreType.DMA
    arrived = pl.pallas_call(
        partial(exchange_kernel, peers, count),
        out_shape=tuple(jax.ShapeDtypeStruct(v.shape, v.dtype) for v in blocks),
        in_specs=[anywhere] * count,
        out_specs=(anywhere,) * count,
        scratch_shapes=[dma((count,)), dma((count, peers)), dma((count, peers))],
        compiler_params=pltpu.CompilerParams(collective_id=1, has_side_effects=True),
    )(*blocks)
    return tuple(jnp.sum(v.astype(jnp.float32), axis=0) for v in arrived)


def core_sum(own, other):
    arrived = swap(other, "strand")
    return (own.astype(jnp.float32) + arrived.astype(jnp.float32)).astype(jnp.bfloat16)


def share_sum(own, other):
    return lax.psum_scatter(core_sum(own, other), "seq", scatter_dimension=0, tiled=True)


def on_device(
    hidden,
    breaks,
    cotangent,
    input_weight,
    gate_weight,
    key_weight,
    query_weight,
    step_weight,
    output_weight,
    step_bias,
    decay_log,
    skip_gain,
):
    strand = lax.axis_index("strand")
    backward = strand == 1
    seq_index = lax.axis_index("seq")
    length = hidden.shape[0]
    shard_rows = input_weight.shape[0]
    peers = lax.axis_size("seq")
    halves = lax.axis_size("mp")
    width = shard_rows * peers * 2
    half = shard_rows * peers
    part_width = hidden.shape[1]

    target = lax.broadcasted_iota(jnp.int32, (width, width), 1)
    source = lax.broadcasted_iota(jnp.int32, (width, width), 0)
    local = target % half
    side = jnp.where(target < half, strand, 1 - strand)
    feature = (local // shard_rows) * (2 * shard_rows) + side * shard_rows + local % shard_rows
    feature = jnp.where(backward, width - 1 - feature, feature)
    moves = (source == feature).astype(jnp.bfloat16)
    moves = lax.optimization_barrier(moves)

    key_width = key_weight.shape[1]
    inner_width = input_weight.shape[1]
    ahead = jnp.concatenate(
        (input_weight, gate_weight, key_weight, query_weight, step_weight), axis=1
    )
    ahead_full, out_full, everything = gather_all(
        ahead, output_weight, jnp.stack((hidden, cotangent))
    )

    def permuted(which):
        return sum(
            jnp.dot(
                everything[m, which],
                moves[m * part_width : (m + 1) * part_width],
                preferred_element_type=jnp.float32,
            )
            for m in range(halves)
        ).astype(jnp.bfloat16)

    inputs = permuted(0)
    grads_in = permuted(1)
    break_marks = lax.dynamic_slice_in_dim(breaks, seq_index * length, length).astype(jnp.float32)

    def project(start, size):
        return jnp.dot(
            inputs, ahead_full[:, start : start + size], preferred_element_type=jnp.float32
        )

    groups = key_width // STATE
    key_start = 2 * inner_width
    key_vals = project(key_start, key_width).astype(jnp.bfloat16).reshape(length, groups, STATE)
    query_vals = (
        project(key_start + key_width, key_width)
        .astype(jnp.bfloat16)
        .reshape(length, groups, STATE)
    )
    step_raw = project(key_start + 2 * key_width, step_weight.shape[1])
    inner_vals = project(0, inner_width).astype(jnp.bfloat16).reshape(length, -1, HEAD_DIM)
    gate_vals = project(inner_width, inner_width).astype(jnp.bfloat16).reshape(length, groups, -1)

    local_terms, local_pull = jax.vjp(
        partial(block_terms, backward, step_bias, decay_log, break_marks),
        inner_vals,
        key_vals,
        query_vals,
        step_raw,
    )
    total_log, total_state = local_terms[4:]
    head_shape = total_state.shape[:2]
    heads = total_log.shape[0]
    log_pieces = []
    rest = total_log
    for _ in range(3):
        piece = lax.reduce_precision(rest, 8, 7)
        log_pieces.append(piece)
        rest = rest - piece
    log_rows = jnp.pad(jnp.stack(log_pieces), ((0, 13), (0, STATE - heads)))
    sent = jnp.concatenate(
        (total_state.reshape(-1, STATE).astype(jnp.bfloat16), log_rows.astype(jnp.bfloat16))
    )
    arrived = lax.all_gather(sent, "seq")
    state_rows = heads * HEAD_DIM
    all_logs = jnp.sum(arrived[:, state_rows : state_rows + 3, :heads].astype(jnp.float32), axis=1)
    order = earlier_than(peers, backward)
    chain = chain_weights(order, all_logs)
    here = lax.dynamic_index_in_dim(chain, seq_index, 0, keepdims=False)
    there = lax.dynamic_index_in_dim(chain, seq_index, 1, keepdims=False)

    def chained(everything, weights):
        weights = weights.reshape((peers,) + head_shape)
        return sum(
            weights[k][..., None, None]
            * everything[k].reshape(total_state.shape).astype(jnp.float32)
            for k in range(peers)
        )

    entering = chained(arrived[:, :state_rows], here)
    mixer_out, finish_pull = jax.vjp(
        partial(finish_terms, skip_gain), *local_terms[:4], query_vals, inner_vals, entering
    )
    gated, gate_pull = jax.vjp(gate_terms, mixer_out, gate_vals)
    gated_flat = gated.reshape(length, -1)

    gated_back = jnp.dot(grads_in, out_full, preferred_element_type=jnp.float32).astype(jnp.bfloat16).reshape(gated.shape)
    mixer_back, gate_back = gate_pull(gated_back)
    finish_back = finish_pull(mixer_back)
    carried_back = chained(lax.all_gather(finish_back[6].astype(jnp.bfloat16), "seq"), there)

    contract_rows = (((1,), (1,)), ((), ()))
    head_terms = tuple(
        lax.dot_general(
            gated_flat, part, contract_rows, preferred_element_type=jnp.float32
        ).astype(jnp.bfloat16)
        for part in (out_full[:half], out_full[half:])
    )
    head_terms = jnp.stack(
        [
            sum(
                lax.dot_general(
                    head_terms[s],
                    moves[m * part_width : (m + 1) * part_width, s * half : (s + 1) * half],
                    contract_rows,
                    preferred_element_type=jnp.float32,
                )
                for s in range(2)
            ).astype(jnp.bfloat16)
            for m in range(halves)
        ]
    )
    reduced = lax.psum_scatter(head_terms, "mp", scatter_dimension=0)
    combined = (
        reduced.astype(jnp.float32) + swap(reduced, "strand").astype(jnp.float32)
    ).astype(jnp.bfloat16)

    contract = (((0,), (0,)), ((), ()))

    def grad_pair(left, right):
        return tuple(
            lax.dot_general(part, right, contract, preferred_element_type=jnp.float32).astype(
                jnp.bfloat16
            )
            for part in (left[:, :half], left[:, half:])
        )

    grad_output = share_sum(*grad_pair(grads_in, gated_flat)).astype(jnp.float32)
    grad_gate = share_sum(*grad_pair(inputs, gate_back.reshape(length, -1))).astype(jnp.float32)

    log_back = jnp.sum(carried_back * entering, axis=(-2, -1)).reshape(
        total_log.shape
    ) * jnp.exp(total_log)
    local_back = local_pull((*finish_back[:4], log_back, carried_back))
    inner_back = (local_back[0] + finish_back[5]).reshape(length, -1)
    key_back = local_back[1].reshape(length, -1)
    query_back = (local_back[2] + finish_back[4]).reshape(length, -1)
    step_back = local_back[3]

    input_terms = grad_pair(inputs, inner_back)
    small_terms = tuple(
        jnp.concatenate(
            (
                lax.dot_general(
                    part, key_back, contract, preferred_element_type=jnp.float32
                ).astype(jnp.bfloat16),
                lax.dot_general(
                    part, query_back, contract, preferred_element_type=jnp.float32
                ).astype(jnp.bfloat16),
                lax.dot_general(
                    part.astype(jnp.float32), step_back, contract, precision=HIGHEST
                ).astype(jnp.bfloat16),
            ),
            axis=1,
        )
        for part in (inputs[:, :half], inputs[:, half:])
    )
    grad_input, small_share = exchange((core_sum(*input_terms), core_sum(*small_terms)))
    return (
        combined,
        grad_input,
        grad_gate,
        small_share[:, :key_width],
        small_share[:, key_width : 2 * key_width],
        small_share[:, 2 * key_width :],
        grad_output,
    )


NN = (((1,), (0,)), ((), ()))
NT = (((1,), (1,)), ((), ()))
TN = (((0,), (0,)), ((), ()))
F32 = jnp.float32
BF16 = jnp.bfloat16


def mm(left, right, dims=NN, **options):
    return lax.dot_general(left, right, dims, preferred_element_type=F32, **options)


def iota(shape, axis):
    return lax.broadcasted_iota(jnp.int32, shape, axis)


def per_head(columns, first):
    low = iota((columns.shape[0], 128), 1) < HEAD_DIM
    parts = []
    for pair in range(2):
        at = first + 2 * pair
        wide = [
            jnp.broadcast_to(columns[:, at + i : at + i + 1], (columns.shape[0], 128))
            for i in range(2)
        ]
        parts.append(jnp.where(low, *wide))
    return jnp.concatenate(parts, axis=1)


def head_rows(value, select):
    high = value.astype(BF16)
    low = (value - high.astype(F32)).astype(BF16)
    return (mm(select, high, NT) + mm(select, low, NT))[:8]


def mixer_kernel(
    u_ref,
    t_ref,
    w_ref,
    step_ref,
    marks_ref,
    params_ref,
    skip_ref,
    p_ref,
    grad_ref,
    grad_step_ref,
    weff,
    seff,
    xzbc,
    dxzbc,
    gated,
    dy_ref,
    r_rows,
    dt_rows,
    k_rows,
    dr_rows,
    entering,
    state,
):
    positions, width = u_ref.shape
    blocks = positions // STRETCH
    shards = step_ref.shape[0]
    shard = width // shards
    heads = 4
    inner = heads * HEAD_DIM
    backward = lax.axis_index("strand") == 1

    row = iota((shard, shard), 0)
    column = iota((shard, shard), 1)
    other = jnp.where(backward, shard - 1 - column, column)
    moves = jnp.where(row == other, 1.0, 0.0).astype(BF16)

    def mirrored(i, count):
        return jnp.where(backward, count - 1 - i, i)

    for b in range(shards):
        source = mirrored(b, shards)
        rows = pl.ds(pl.multiple_of(source * shard, shard), shard)
        weff[b * shard : (b + 1) * shard, :] = mm(moves, w_ref[rows, :]).astype(BF16)
        seff[:, b * shard : (b + 1) * shard] = mm(step_ref[source], moves).astype(BF16)

    lead = iota((STRETCH, STRETCH), 0) - iota((STRETCH, STRETCH), 1)
    lead = jnp.where(backward, -lead, lead)
    causal = lead >= 0
    sums_to = (lead <= 0).astype(F32)
    sums_from = (lead >= 0).astype(F32)
    sums_before = (lead < 0).astype(F32)
    low_lanes = iota((STRETCH, 128), 1) < HEAD_DIM
    select = jnp.where(
        iota((16, inner), 1) // HEAD_DIM == iota((16, inner), 0), 1.0, 0.0
    ).astype(BF16)
    rates = -jnp.exp(params_ref[1])
    bias = params_ref[0]
    skip = skip_ref[0:1, :]
    filler = jnp.zeros((128 - 24, STRETCH), F32)

    def columns_of(k, dt):
        ends = jnp.broadcast_to(jnp.sum(k[1], axis=1, keepdims=True), k[0].shape)
        return jnp.transpose(jnp.concatenate((k[0], dt, ends, filler), axis=0))

    state[...] = jnp.zeros_like(state)

    def forward(c, carry):
        blk = mirrored(c, blocks)
        at = pl.ds(pl.multiple_of(blk * STRETCH, STRETCH), STRETCH)
        u = u_ref[at, :]
        projected = mm(u, weff[:, : 3 * inner]).astype(BF16)
        xzbc[at, :] = projected
        x = projected[:, :inner]
        z = projected[:, inner : 2 * inner].astype(F32)
        b = projected[:, 2 * inner : 2 * inner + STATE]
        q = projected[:, 2 * inner + STATE :]
        r = mm(seff[...], u, NT)[:8] + jnp.concatenate([bias] * 2, axis=1)
        dt = jnp.maximum(r, 0.0) + jnp.log1p(jnp.exp(-jnp.abs(r)))
        a = jnp.concatenate([rates] * 2, axis=1) * dt + KEEP_LOG * marks_ref[blk]
        k = mm(a, sums_to, precision=HIGHEST)
        r_rows[blk] = r
        dt_rows[blk] = dt
        k_rows[blk] = jnp.concatenate((k, a), axis=0)
        cols = columns_of((k, a), dt)
        scores = mm(q, b, NT)
        parts = []
        for pair in range(2):
            outs = []
            for i in range(2):
                h = 2 * pair + i
                spread = jnp.where(causal, cols[:, h : h + 1] - k[h : h + 1, :], -1e30)
                mixing = (scores * jnp.exp(spread) * dt[h : h + 1, :]).astype(BF16)
                outs.append(mm(mixing, x[:, 128 * pair : 128 * (pair + 1)]))
            parts.append(jnp.where(low_lanes, *outs))
        y = jnp.concatenate(parts, axis=1)
        before = state[...]
        entering[blk] = before
        carried = mm(q, before.astype(BF16))
        wide_k = per_head(cols, 0)
        wide_dt = per_head(cols, 8)
        wide_end = per_head(cols, 16)
        xf = x.astype(F32)
        y = y + jnp.exp(wide_k) * carried + skip * xf
        e = (jnp.exp(wide_end - wide_k) * wide_dt * xf).astype(BF16)
        state[...] = jnp.exp(wide_end[0:1, :]) * before + mm(b, e, TN)

        sig = 1.0 / (1.0 + jnp.exp(-z))
        silu = z * sig
        v = y * silu
        scale = lax.rsqrt(jnp.mean(v * v, axis=1, keepdims=True) + EPSILON)
        g = (v * scale).astype(BF16)
        gated[at, :] = g
        out_weight = weff[:, 3 * inner :]
        p_ref[at, :] = mm(g, out_weight, NT).astype(BF16)

        dg = mm(t_ref[at, :], out_weight).astype(BF16).astype(F32)
        along = jnp.mean(dg * v, axis=1, keepdims=True)
        dv = scale * (dg - v * (scale * scale * along))
        dy_ref[at, :] = dv * silu
        dz = dv * y * (sig * (1.0 + z * (1.0 - sig)))
        dxzbc[at, inner : 2 * inner] = dz.astype(BF16)
        return carry

    lax.fori_loop(0, blocks, forward, 0)

    state[...] = jnp.zeros_like(state)

    def backwards(c, carry):
        blk = mirrored(blocks - 1 - c, blocks)
        at = pl.ds(pl.multiple_of(blk * STRETCH, STRETCH), STRETCH)
        x = xzbc[at, :inner]
        b = xzbc[at, 2 * inner : 2 * inner + STATE]
        q = xzbc[at, 2 * inner + STATE :]
        xf = x.astype(F32)
        dy = dy_ref[at, :]
        dyb = dy.astype(BF16)
        dt = dt_rows[blk]
        k = k_rows[blk, :8]
        cols = columns_of((k, k_rows[blk, 8:]), dt)
        wide_k = per_head(cols, 0)
        wide_dt = per_head(cols, 8)
        wide_end = per_head(cols, 16)
        before = entering[blk]
        before_b = before.astype(BF16)
        leaving = state[...]
        leaving_b = leaving.astype(BF16)

        keep = jnp.exp(wide_end - wide_k)
        keep_x = keep * xf
        de = mm(b, leaving_b)
        db = mm((keep_x * wide_dt).astype(BF16), leaving_b, NT)
        ddt = head_rows(de * keep_x, select)
        dx = de * (keep * wide_dt) + skip * dy

        grown = jnp.exp(wide_k) * dy
        grown_b = grown.astype(BF16)
        dq = mm(grown_b, before_b, NT)
        dk = head_rows(grown * mm(q, before_b), select)
        end_row = jnp.exp(wide_end[0:1, :])
        total = jnp.sum(before * leaving, axis=0, keepdims=True) * end_row
        total = head_rows(jnp.broadcast_to(total, (128, inner)), select)[:, 0:1]
        state[...] = end_row * leaving + mm(q, grown_b, TN)

        scores = mm(q, b, NT)
        dscores = jnp.zeros((STRETCH, STRETCH), F32)
        row_sums = jnp.zeros((STRETCH, 128), F32)
        lane = iota((STRETCH, 128), 1)
        dx_parts = []
        col_sums = []
        for pair in range(2):
            pair_at = slice(128 * pair, 128 * (pair + 1))
            outs = []
            for i in range(2):
                h = 2 * pair + i
                dt_row = dt[h : h + 1, :]
                spread = jnp.where(causal, cols[:, h : h + 1] - k[h : h + 1, :], -1e30)
                decay = jnp.exp(spread)
                mine = low_lanes if i == 0 else jnp.logical_not(low_lanes)
                dy_head = jnp.where(mine, dy[:, pair_at], 0.0).astype(BF16)
                dmix = mm(dy_head, x[:, pair_at], NT) * decay
                mixing = (scores * decay * dt_row).astype(BF16)
                outs.append(mm(mixing, dyb[:, pair_at], TN))
                dscores = dscores + dmix * dt_row
                dmix = dmix * scores
                col_sums.append(jnp.sum(dmix, axis=0, keepdims=True))
                summed = jnp.sum(dmix * dt_row, axis=1, keepdims=True)
                row_sums = jnp.where(lane == h, summed, row_sums)
            dx_parts.append(jnp.where(low_lanes, *outs))
        dx = dx + jnp.concatenate(dx_parts, axis=1)
        dscores_b = dscores.astype(BF16)
        dq = dq + mm(dscores_b, b)
        db = db + mm(dscores_b, q, TN)
        dxzbc[at, :inner] = dx.astype(BF16)
        dxzbc[at, 2 * inner : 2 * inner + STATE] = db.astype(BF16)
        dxzbc[at, 2 * inner + STATE :] = dq.astype(BF16)

        columns = jnp.concatenate(col_sums + [jnp.zeros((4, STRETCH), F32)], axis=0)
        dk = dk + jnp.transpose(row_sums)[:8] - dt * columns
        da = mm(dk, sums_from, precision=HIGHEST)
        da = da + mm(dt * ddt, sums_before, precision=HIGHEST) + total
        ddt = ddt + columns + jnp.concatenate([rates] * 2, axis=1) * da
        dr_rows[blk] = ddt / (1.0 + jnp.exp(-r_rows[blk]))
        return carry

    lax.fori_loop(0, blocks, backwards, 0)

    dr = jnp.concatenate([dr_rows[i] for i in range(blocks)], axis=1)
    dr_high = dr.astype(BF16)
    dr_low = (dr - dr_high.astype(F32)).astype(BF16)
    dr_both = jnp.concatenate((dr_high, dr_low), axis=0)

    def weigh(f, carry):
        target = mirrored(f, shards)
        lanes = pl.ds(pl.multiple_of(f * shard, shard), shard)
        rows = pl.ds(pl.multiple_of(target * shard, shard), shard)
        u = u_ref[:, lanes]
        found = mm(u, dxzbc[...], TN).astype(BF16)
        grad_ref[rows, : 3 * inner] = mm(moves, found).astype(BF16)
        found = mm(t_ref[:, lanes], gated[...], TN).astype(BF16)
        grad_ref[rows, 3 * inner :] = mm(moves, found).astype(BF16)
        both = mm(dr_both, u)
        both = jnp.concatenate((both[:8] + both[8:], jnp.zeros((8, shard), F32)), axis=0)
        grad_step_ref[target] = mm(both.astype(BF16), moves).astype(BF16)
        return carry

    lax.fori_loop(0, shards, weigh, 0)


def mix(u, t, w, step, marks, params, skip):
    positions, width = u.shape
    blocks = positions // STRETCH
    columns = w.shape[1]
    inner = skip.shape[1]
    vmem = pl.BlockSpec(memory_space=pltpu.VMEM)
    return pl.pallas_call(
        mixer_kernel,
        out_shape=(
            jax.ShapeDtypeStruct((positions, width), BF16),
            jax.ShapeDtypeStruct((width, columns), BF16),
            jax.ShapeDtypeStruct(step.shape, BF16),
        ),
        in_specs=[vmem] * 7,
        out_specs=(vmem,) * 3,
        scratch_shapes=[
            pltpu.VMEM((width, columns), BF16),
            pltpu.VMEM((16, width), BF16),
            pltpu.VMEM((positions, 3 * inner), BF16),
            pltpu.VMEM((positions, 3 * inner), BF16),
            pltpu.VMEM((positions, inner), BF16),
            pltpu.VMEM((positions, inner), F32),
            pltpu.VMEM((blocks, 8, STRETCH), F32),
            pltpu.VMEM((blocks, 8, STRETCH), F32),
            pltpu.VMEM((blocks, 16, STRETCH), F32),
            pltpu.VMEM((blocks, 8, STRETCH), F32),
            pltpu.VMEM((blocks, STATE, inner), F32),
            pltpu.VMEM((STATE, inner), F32),
        ],
        compiler_params=pltpu.CompilerParams(vmem_limit_bytes=60 * 1024 * 1024),
    )(u, t, w, step, marks, params, skip)


class Places:
    def __init__(self, peers):
        self.part = lax.axis_index("parts")
        self.seq = lax.axis_index("seq")
        self.strand = lax.axis_index("strand")
        self.model = lax.axis_index("mp")
        self.peers = peers
        self.twin = {"parts": 1 - self.part}
        self.mate = {"strand": 1 - self.strand}
        self.side = {"mp": 1 - self.model}
        self.others = [lax.rem(self.seq + d, peers) for d in range(1, peers)]


def remote(source, target, send, receive, device):
    return pltpu.make_async_remote_copy(
        src_ref=source,
        dst_ref=target,
        send_sem=send,
        recv_sem=receive,
        device_id=device,
        device_id_type=pl.DeviceIdType.MESH,
    )


def greet(place):
    barrier = pltpu.get_barrier_semaphore()
    targets = [{"seq": t} for t in place.others] + [place.twin, place.mate, place.side]
    for target in targets:
        pl.semaphore_signal(
            barrier, inc=1, device_id=target, device_id_type=pl.DeviceIdType.MESH
        )
    pl.semaphore_wait(barrier, len(targets))


def collect_kernel(
    peers,
    hidden,
    cotangent,
    packed,
    steps,
    u_ref,
    t_ref,
    w_ref,
    step_ref,
    local_sem,
    z_send,
    z_recv,
    x_send,
    x_recv,
    m_send,
    m_recv,
    w_send,
    w_recv,
    s_send,
    s_recv,
):
    place = Places(peers)
    seq, strand, model, part = place.seq, place.strand, place.model, place.part
    length, features = hidden.shape
    half = length // 2
    shard = packed.shape[1]
    thin = shard // 2
    sources = (hidden, cotangent)
    fulls = (u_ref, t_ref)
    greet(place)

    def piece(a, block, side, core):
        rows = pl.ds(pl.multiple_of(block * length + core * half, half), half)
        return fulls[a].at[rows, pl.ds(pl.multiple_of(side * features, features), features)]

    def own(a):
        return sources[a].at[pl.ds(pl.multiple_of(strand * half, half), half), :]

    def up(a, block, source):
        return remote(
            source,
            piece(a, block, model, strand),
            z_send.at[a, 0, block],
            z_recv.at[a, block],
            {"seq": jnp.minimum(seq + 1, peers - 1)},
        )

    def down(a, block, source):
        return remote(
            source,
            piece(a, block, model, strand),
            z_send.at[a, 1, block],
            z_recv.at[a, block],
            {"seq": jnp.maximum(seq - 1, 0)},
        )

    def across(a, block, source):
        return remote(
            source,
            piece(a, block, model, strand),
            x_send.at[a, block],
            x_recv.at[a, block],
            place.side,
        )

    def to_mate(a, block, side):
        mine = piece(a, block, side, strand)
        return remote(mine, mine, m_send.at[a, block, side], m_recv.at[a, block, side], place.mate)

    def wait_z(a, block):
        mine = piece(a, block, model, strand)
        remote(mine, mine, z_send.at[a, 0, block], z_recv.at[a, block], place.side).wait_recv()

    def wait_x(a, block):
        mine = piece(a, block, 1 - model, strand)
        remote(mine, mine, x_send.at[a, block], x_recv.at[a, block], place.side).wait_recv()

    def wait_mate(a, block, side):
        mine = piece(a, block, side, 1 - strand)
        remote(
            mine, mine, m_send.at[a, block, side], m_recv.at[a, block, side], place.mate
        ).wait_recv()

    has_up, has_down = seq < peers - 1, seq > 0

    def launch_up(a):
        pl.when(has_up)(lambda: up(a, seq, own(a)).start())

    def launch_down(a):
        pl.when(has_down)(lambda: down(a, seq, own(a)).start())

    def local_copies():
        copies = []
        for a in range(2):
            rows = pl.ds(pl.multiple_of(seq * length, length), length)
            lanes = pl.ds(pl.multiple_of(model * features, features), features)
            copies.append(
                pltpu.make_async_copy(sources[a], fulls[a].at[rows, lanes], local_sem.at[a])
            )
        copies.append(
            pltpu.make_async_copy(packed.at[seq], w_block(seq, strand), local_sem.at[2])
        )
        copies.append(
            pltpu.make_async_copy(steps.at[seq], step_ref.at[2 * seq + strand], local_sem.at[3])
        )
        return copies

    def w_block(block, core):
        return w_ref.at[pl.ds(pl.multiple_of((2 * block + core) * shard, shard), shard), :]

    def w_piece(block, core, which):
        first = (2 * block + core) * shard + which * thin
        return w_ref.at[pl.ds(pl.multiple_of(first, thin), thin), :]

    def w_copies(t):
        rows = pl.ds(pl.multiple_of(part * thin, thin), thin)
        yield remote(
            packed.at[t, rows, :],
            w_piece(seq, strand, part),
            w_send.at[0, t],
            w_recv.at[0, seq],
            {"seq": t},
        )
        yield remote(
            steps.at[t],
            step_ref.at[2 * seq + strand],
            s_send.at[0, t],
            s_recv.at[0, seq],
            {"seq": t},
        )

    def own_to_mate():
        yield remote(
            packed.at[seq], w_block(seq, strand), w_send.at[0, seq], w_recv.at[0, seq], place.mate
        )
        yield remote(
            steps.at[seq],
            step_ref.at[2 * seq + strand],
            s_send.at[0, seq],
            s_recv.at[0, seq],
            place.mate,
        )

    def w_twin(t):
        mine = w_piece(t, strand, part)
        return remote(mine, mine, w_send.at[1, t], w_recv.at[1, t], place.twin)

    def w_mate(t, which):
        mine = w_piece(t, strand, which)
        return remote(mine, mine, w_send.at[2 + which, t], w_recv.at[2 + which, t], place.mate)

    def s_mate(t):
        mine = step_ref.at[2 * t + strand]
        return remote(mine, mine, s_send.at[1, t], s_recv.at[1, t], place.mate)

    def wait_w(t):
        mine = w_piece(t, strand, part)
        remote(mine, mine, w_send.at[0, t], w_recv.at[0, t], place.mate).wait_recv()
        mine = step_ref.at[2 * t + strand]
        remote(mine, mine, s_send.at[0, t], s_recv.at[0, t], place.mate).wait_recv()

    def wait_w_twin(t):
        mine = w_piece(t, strand, 1 - part)
        remote(mine, mine, w_send.at[1, t], w_recv.at[1, t], place.twin).wait_recv()

    def wait_w_mate(t):
        for which in range(2):
            mine = w_piece(t, 1 - strand, which)
            remote(
                mine, mine, w_send.at[2 + which, t], w_recv.at[2 + which, t], place.mate
            ).wait_recv()
        mine = step_ref.at[2 * t + 1 - strand]
        remote(mine, mine, s_send.at[1, t], s_recv.at[1, t], place.mate).wait_recv()

    def wait_w_own():
        mine = w_block(seq, 1 - strand)
        remote(mine, mine, w_send.at[0, seq], w_recv.at[0, seq], place.mate).wait_recv()
        mine = step_ref.at[2 * seq + 1 - strand]
        remote(mine, mine, s_send.at[0, seq], s_recv.at[0, seq], place.mate).wait_recv()

    def relay(a, d):
        def below():
            block = seq - d
            wait_z(a, block)
            pl.when(has_up)(lambda: up(a, block, piece(a, block, model, strand)).start())
            across(a, block, piece(a, block, model, strand)).start()
            to_mate(a, block, model).start()

        def above():
            block = seq + d
            wait_z(a, block)
            pl.when(has_down)(lambda: down(a, block, piece(a, block, model, strand)).start())
            across(a, block, piece(a, block, model, strand)).start()
            to_mate(a, block, model).start()

        pl.when(seq >= d)(below)
        pl.when(seq + d < peers)(above)

    def near(d, action):
        if d == 0:
            action(seq)
        else:
            pl.when(seq >= d)(lambda: action(seq - d))
            pl.when(seq + d < peers)(lambda: action(seq + d))

    def from_side(a):
        def action(block):
            wait_x(a, block)
            to_mate(a, block, 1 - model).start()

        return action

    launch_up(0)
    launch_down(0)
    across(0, seq, own(0)).start()
    for t in place.others:
        for copy in w_copies(t):
            copy.start()
    for copy in own_to_mate():
        copy.start()
    locals_ = local_copies()
    for copy in locals_:
        copy.start()

    def next_up(d):
        pl.when(seq == d)(lambda: launch_up(1))
        pl.when(peers - 1 - seq == d)(lambda: launch_down(1))

    next_up(0)
    for d in range(1, peers):
        relay(0, d)
        next_up(d)
        near(d - 1, from_side(0))
    across(1, seq, own(1)).start()
    for t in place.others:
        wait_w(t)
        w_twin(t).start()
        w_mate(t, part).start()
        s_mate(t).start()
    near(peers - 1, from_side(0))
    for t in place.others:
        wait_w_twin(t)
        w_mate(t, 1 - part).start()
    for d in range(1, peers):
        relay(1, d)
        near(d - 1, from_side(1))
    near(peers - 1, from_side(1))

    for a in range(2):
        for d in range(peers):

            def arrivals(block, a=a, d=d):
                if d:
                    wait_mate(a, block, model)
                wait_mate(a, block, 1 - model)

            near(d, arrivals)
    for t in place.others:
        wait_w_mate(t)
    wait_w_own()
    for copy in locals_:
        copy.wait()

    for a in range(2):
        for d in range(peers):

            def sent(block, a=a, d=d):
                mine = piece(a, block, model, strand)
                across(a, block, mine).wait_send()
                if d:
                    to_mate(a, block, model).wait_send()
                to_mate(a, block, 1 - model).wait_send()
                pl.when(jnp.logical_and(has_up, block <= seq))(
                    lambda: up(a, block, mine).wait_send()
                )
                pl.when(jnp.logical_and(has_down, block >= seq))(
                    lambda: down(a, block, mine).wait_send()
                )

            near(d, sent)
    for t in place.others:
        for copy in w_copies(t):
            copy.wait_send()
        w_twin(t).wait_send()
        for which in range(2):
            w_mate(t, which).wait_send()
        s_mate(t).wait_send()
    for copy in own_to_mate():
        copy.wait_send()


def collect(hidden, cotangent, packed, steps):
    peers, models = lax.axis_size("seq"), lax.axis_size("mp")
    anywhere = pl.BlockSpec(memory_space=pl.ANY)
    dma = pltpu.SemaphoreType.DMA
    full = (hidden.shape[0] * peers, hidden.shape[1] * models)
    return pl.pallas_call(
        partial(collect_kernel, peers),
        out_shape=(
            jax.ShapeDtypeStruct(full, hidden.dtype),
            jax.ShapeDtypeStruct(full, hidden.dtype),
            jax.ShapeDtypeStruct((2 * peers * packed.shape[1], packed.shape[2]), packed.dtype),
            jax.ShapeDtypeStruct((2 * peers,) + steps.shape[1:], steps.dtype),
        ),
        in_specs=[anywhere] * 4,
        out_specs=(anywhere,) * 4,
        scratch_shapes=[
            dma((4,)),
            dma((2, 2, peers)),
            dma((2, peers)),
            dma((2, peers)),
            dma((2, peers)),
            dma((2, peers, 2)),
            dma((2, peers, 2)),
            dma((4, peers)),
            dma((4, peers)),
            dma((2, peers)),
            dma((2, peers)),
        ],
        compiler_params=pltpu.CompilerParams(collective_id=2, has_side_effects=True),
    )(hidden, cotangent, packed, steps)


def by_group(
    hidden,
    breaks,
    cotangent,
    input_weight,
    gate_weight,
    key_weight,
    query_weight,
    step_weight,
    output_weight,
    step_bias,
    decay_log,
    skip_gain,
):
    strand = lax.axis_index("strand")
    seq = lax.axis_index("seq")
    peers = lax.axis_size("seq")
    length = hidden.shape[0]
    shard = input_weight.shape[0]
    heads = step_bias.shape[0]
    mine = heads // peers

    def grouped(weight):
        return jnp.transpose(weight.reshape(shard, peers, -1), (1, 0, 2))

    packed = jnp.concatenate(
        [
            grouped(w)
            for w in (input_weight, gate_weight, key_weight, query_weight, output_weight)
        ],
        axis=2,
    )
    steps = jnp.pad(
        jnp.transpose(step_weight).reshape(peers, mine, shard), ((0, 0), (0, 16 - mine), (0, 0))
    )

    u, t, weights, step_rows = collect(hidden, cotangent, packed, steps)

    marks = jnp.broadcast_to(
        breaks.astype(F32).reshape(-1, 1, STRETCH), (breaks.shape[0] // STRETCH, 8, STRETCH)
    )

    def here(value):
        return lax.dynamic_slice_in_dim(value, seq * mine, mine)

    params = jnp.stack([here(step_bias), here(decay_log)])
    params = jnp.broadcast_to(
        jnp.pad(params, ((0, 0), (0, 8 - mine)))[..., None], (2, 8, 128)
    )
    skip = jnp.broadcast_to(jnp.repeat(here(skip_gain), HEAD_DIM)[None], (8, mine * HEAD_DIM))

    p, grads, grad_step = mix(u, t, weights, step_rows, marks, params, skip)

    def to_shards(value):
        value = value.reshape((peers, 2) + value.shape[1:])
        own = lax.dynamic_index_in_dim(value, strand, 1, keepdims=False)
        other = lax.dynamic_index_in_dim(value, 1 - strand, 1, keepdims=False)
        total = own.astype(F32) + swap(other, "strand").astype(F32)
        return lax.all_to_all(total.astype(BF16), "seq", 0, 0).astype(F32)

    full = to_shards(grads.reshape(2 * peers, shard, -1))
    step_full = to_shards(grad_step)

    def spread(value):
        return jnp.transpose(value, (1, 0, 2)).reshape(shard, -1)

    inner = mine * HEAD_DIM
    p = lax.psum_scatter(p.astype(BF16), "mp", scatter_dimension=1, tiled=True)
    p = lax.psum_scatter(p, "seq", scatter_dimension=0, tiled=True)
    combined = (p.astype(F32) + swap(p, "strand").astype(F32)).astype(BF16)
    return (
        combined,
        spread(full[:, :, :inner]),
        spread(full[:, :, inner : 2 * inner]),
        spread(full[:, :, 2 * inner : 2 * inner + STATE]),
        spread(full[:, :, 2 * inner + STATE : 3 * inner]),
        jnp.transpose(step_full[:, :mine], (2, 0, 1)).reshape(shard, heads),
        spread(full[:, :, 3 * inner :]),
    )


def solution(mesh):
    in_specs = (
        P(("parts", "seq"), "mp"),
        P("parts"),
        P(("parts", "seq"), "mp"),
        P(("seq", "strand"), "mp"),
        P(("seq", "strand"), "mp"),
        P(("seq", "strand"), "mp"),
        P(("seq", "strand"), "mp"),
        P(("seq", "strand"), "mp"),
        P(("seq", "strand"), "mp"),
        P("mp"),
        P("mp"),
        P("mp"),
    )
    out_specs = (
        P(("parts", "seq"), "mp"),
        P(("parts", "seq", "strand"), "mp"),
        P(("parts", "seq", "strand"), "mp"),
        P(("parts", "seq", "strand"), "mp"),
        P(("parts", "seq", "strand"), "mp"),
        P(("parts", "seq", "strand"), "mp"),
        P(("parts", "seq", "strand"), "mp"),
    )
    peers = mesh.shape["seq"]

    def each(*args):
        groups = args[5].shape[1] // STATE
        heads = args[9].shape[0]
        fits = peers == groups and heads == 4 * groups and mesh.shape["mp"] == 2
        return (by_group if fits else on_device)(*args)

    return jax.shard_map(
        each, mesh=mesh, in_specs=in_specs, out_specs=out_specs, check_vma=False
    )
```

```python
from functools import partial

import jax
import jax.numpy as jnp
from jax import lax
from jax.experimental import pallas as pl
from jax.experimental.pallas import tpu as pltpu
from jax.sharding import PartitionSpec as P

HEAD_DIM = 64
STATE = 128
STRETCH = 256


KEEP_LOG = -0.35667494393873245
EPSILON = 1e-05
HIGHEST = lax.Precision.HIGHEST


def swap(value, axis):
    size = lax.axis_size(axis)
    return lax.ppermute(value, axis, [(i, size - 1 - i) for i in range(size)])


def earlier_than(count, backward):
    row = lax.broadcasted_iota(jnp.int32, (count, count), 0)
    column = lax.broadcasted_iota(jnp.int32, (count, count), 1)
    return jnp.where(backward, column > row, column < row)


def chain_weights(before, logs):
    steps = before.astype(jnp.float32)
    between = steps[:, None, :] * jnp.transpose(steps)[None, :, :]
    spans = jnp.sum(between[..., None] * logs[None, None], axis=2)
    return jnp.where(before[..., None], jnp.exp(spans), 0.0)


def block_terms(
    backward, step_bias, decay_log, break_marks, inner_vals, key_vals, query_vals, step_raw
):
    length = inner_vals.shape[0]
    blocks = length // STRETCH
    head_count = inner_vals.shape[1]
    groups = key_vals.shape[1]
    per_group = head_count // groups
    before = earlier_than(STRETCH, backward)
    row = lax.broadcasted_iota(jnp.int32, (STRETCH, STRETCH), 0)
    column = lax.broadcasted_iota(jnp.int32, (STRETCH, STRETCH), 1)
    causal = before | (row == column)
    step_size = jax.nn.softplus(step_raw + step_bias)
    log_rates = -jnp.exp(decay_log) * step_size + KEEP_LOG * break_marks[:, None]
    rate_rows = jnp.transpose(log_rates.reshape(blocks, STRETCH, head_count), (0, 2, 1))
    step_rows = jnp.transpose(step_size.reshape(blocks, STRETCH, head_count), (0, 2, 1))
    log_rows = jnp.einsum("chj,ij->chi", rate_rows, causal.astype(jnp.float32), precision=HIGHEST)
    ends = jnp.sum(rate_rows, axis=-1)
    end_rows = jnp.exp(ends[..., None] - log_rows) * step_rows
    log_decay = jnp.transpose(log_rows, (0, 2, 1))
    key_blocks = key_vals.reshape(blocks, STRETCH, groups, -1)
    query_blocks = query_vals.reshape(blocks, STRETCH, groups, -1)
    inner_blocks = inner_vals.reshape(blocks, STRETCH, groups, per_group, -1)
    scores = jnp.einsum(
        "cqgn,ckgn->cgqk", query_blocks, key_blocks, preferred_element_type=jnp.float32
    )
    decay_rows = log_rows.reshape(blocks, groups, per_group, STRETCH)
    step_heads = step_rows.reshape(blocks, groups, per_group, STRETCH)
    spread = decay_rows[..., :, None] - decay_rows[..., None, :]
    within = jnp.where(causal, jnp.exp(jnp.where(causal, spread, 0.0)), 0.0)
    mixing = (scores[:, :, None] * within * step_heads[..., None, :]).astype(jnp.bfloat16)
    local_out = jnp.einsum(
        "cghqk,ckghp->cqghp", mixing, inner_blocks, preferred_element_type=jnp.float32
    )
    to_end = jnp.transpose(end_rows, (0, 2, 1)).reshape(blocks, STRETCH, groups, per_group)
    weighted = (inner_blocks * to_end[..., None]).astype(jnp.bfloat16)
    block_states = jnp.einsum(
        "cqghp,cqgn->cghpn", weighted, key_blocks, preferred_element_type=jnp.float32
    )
    order = earlier_than(blocks, backward)
    head_shape = (groups, per_group)
    weights = chain_weights(order, ends).reshape((blocks, blocks) + head_shape)
    prior_state = jnp.stack(
        [
            sum(
                weights[c, k][..., None, None] * block_states[k] for k in range(blocks) if k != c
            )
            if blocks > 1
            else jnp.zeros_like(block_states[0])
            for c in range(blocks)
        ]
    )
    order_f = order.astype(jnp.float32)
    prior_logs = jnp.sum(order_f[:, :, None] * ends[None], axis=1)
    later_logs = jnp.sum(jnp.transpose(order_f)[:, :, None] * ends[None], axis=1)
    prior_decay = jnp.exp(prior_logs).reshape((blocks,) + head_shape)
    later_decay = jnp.exp(later_logs).reshape((blocks,) + head_shape)
    total_state = sum(later_decay[c][..., None, None] * block_states[c] for c in range(blocks))
    total_log = jnp.sum(ends, axis=0)
    return (local_out, prior_state, prior_decay, log_decay, total_log, total_state)


def finish_terms(
    skip_gain,
    local_out,
    prior_state,
    prior_decay,
    log_decay,
    query_vals,
    inner_vals,
    entering,
):
    blocks = log_decay.shape[0]
    groups = query_vals.shape[1]
    per_group = inner_vals.shape[1] // groups
    states = prior_state + prior_decay[..., None, None] * entering
    query_full = query_vals.reshape(blocks, STRETCH, groups, -1).astype(jnp.float32)
    carried = jnp.einsum("cqgn,cghpn->cqghp", query_full, states, precision=HIGHEST)
    growth = jnp.exp(log_decay).reshape(blocks, STRETCH, groups, per_group)
    inner_full = inner_vals.reshape(blocks, STRETCH, groups, per_group, -1).astype(jnp.float32)
    mixer_out = (
        local_out
        + growth[..., None] * carried
        + skip_gain.reshape(groups, per_group)[:, :, None] * inner_full
    )
    return mixer_out.reshape(blocks * STRETCH, groups, -1)


def gate_terms(mixer_out, gate_vals):
    product = mixer_out * jax.nn.silu(gate_vals.astype(jnp.float32))
    scaled = product * lax.rsqrt(jnp.mean(product * product, axis=-1, keepdims=True) + EPSILON)
    return scaled.astype(jnp.bfloat16)


def gather_kernel(peers, halves, *refs):
    shards, rows, fulls, all_rows = refs[:2], refs[2], refs[3:5], refs[5]
    local_sem, z_send, z_recv, y_send, y_recv, s_send, s_recv, o_send, o_recv, x_send, x_recv = refs[6:]
    part = lax.axis_index("parts")
    seq = lax.axis_index("seq")
    strand = lax.axis_index("strand")
    model = lax.axis_index("mp")
    twin = {"parts": 1 - part}
    mate = {"strand": 1 - strand}
    others = [lax.rem(seq + d, peers) for d in range(1, peers)]
    models = [lax.rem(model + d, halves) for d in range(1, halves)]

    def remote(source, target, send, receive, device):
        return pltpu.make_async_remote_copy(
            src_ref=source,
            dst_ref=target,
            send_sem=send,
            recv_sem=receive,
            device_id=device,
            device_id_type=pl.DeviceIdType.MESH,
        )

    barrier = pltpu.get_barrier_semaphore()
    targets = [{"seq": t} for t in others] + [{"mp": m} for m in models] + [twin, mate]
    for target in targets:
        pl.semaphore_signal(
            barrier, inc=1, device_id=target, device_id_type=pl.DeviceIdType.MESH
        )
    pl.semaphore_wait(barrier, len(targets))

    sends = []
    locals_ = []

    def go(copy):
        copy.start()
        sends.append(copy)

    for w in range(2):
        for d, t in enumerate(others):
            go(
                remote(
                    shards[w].at[part],
                    fulls[w].at[0, seq, part],
                    z_send.at[w, d],
                    z_recv.at[w, seq],
                    {"seq": t},
                )
            )
    for d, m in enumerate(models):
        go(remote(rows, all_rows.at[model], x_send.at[d], x_recv.at[model], {"mp": m}))
    for w in range(2):
        go(remote(shards[w], fulls[w].at[1, seq], o_send.at[w], o_recv.at[w], mate))
        copy = pltpu.make_async_copy(shards[w], fulls[w].at[0, seq], local_sem.at[w])
        copy.start()
        locals_.append(copy)
    copy = pltpu.make_async_copy(rows, all_rows.at[model], local_sem.at[2])
    copy.start()
    locals_.append(copy)

    for w in range(2):
        full = fulls[w]
        for d, t in enumerate(others):
            mine = full.at[0, t, part]
            remote(mine, mine, z_send.at[w, d], z_recv.at[w, t], {"seq": t}).wait_recv()
            go(remote(mine, mine, y_send.at[w, d], y_recv.at[w, t], twin))
            go(remote(mine, full.at[1, t, part], s_send.at[w, d, 0], s_recv.at[w, t, part], mate))
    for w in range(2):
        full = fulls[w]
        for d, t in enumerate(others):
            theirs = full.at[0, t, 1 - part]
            remote(theirs, theirs, y_send.at[w, d], y_recv.at[w, t], twin).wait_recv()
            go(
                remote(
                    theirs,
                    full.at[1, t, 1 - part],
                    s_send.at[w, d, 1],
                    s_recv.at[w, t, 1 - part],
                    mate,
                )
            )
    for w in range(2):
        full = fulls[w]
        own = full.at[1, seq]
        remote(own, own, o_send.at[w], o_recv.at[w], mate).wait_recv()
        for d, t in enumerate(others):
            for h in range(2):
                block = full.at[1, t, h]
                remote(block, block, s_send.at[w, d, h], s_recv.at[w, t, h], mate).wait_recv()
    for d, m in enumerate(models):
        block = all_rows.at[m]
        remote(block, block, x_send.at[d], x_recv.at[m], {"mp": m}).wait_recv()
    for copy in sends:
        copy.wait_send()
    for copy in locals_:
        copy.wait()


def gather_all(first, second, rows):
    peers, halves = (lax.axis_size("seq"), lax.axis_size("mp"))
    depth = first.shape[0] // 2
    shards = tuple(a.reshape(2, depth, -1) for a in (first, second))
    anywhere = pl.BlockSpec(memory_space=pl.ANY)
    dma = pltpu.SemaphoreType.DMA
    out = pl.pallas_call(
        partial(gather_kernel, peers, halves),
        out_shape=tuple(
            jax.ShapeDtypeStruct((2, peers) + a.shape, a.dtype) for a in shards
        )
        + (jax.ShapeDtypeStruct((halves,) + rows.shape, rows.dtype),),
        in_specs=[anywhere] * 3,
        out_specs=(anywhere,) * 3,
        scratch_shapes=[
            dma((3,)),
            dma((2, peers)),
            dma((2, peers)),
            dma((2, peers)),
            dma((2, peers)),
            dma((2, peers, 2)),
            dma((2, peers, 2)),
            dma((2,)),
            dma((2,)),
            dma((halves,)),
            dma((halves,)),
        ],
        compiler_params=pltpu.CompilerParams(collective_id=0, has_side_effects=True),
    )(*shards, rows)
    return (
        out[0].reshape(4 * peers * depth, -1),
        out[1].reshape(4 * peers * depth, -1),
        out[2],
    )


def exchange_kernel(peers, count, *refs):
    sources, targets = refs[:count], refs[count : 2 * count]
    local_sem, send_sem, recv_sem = refs[2 * count :]
    seq = lax.axis_index("seq")
    others = [lax.rem(seq + d, peers) for d in range(1, peers)]

    barrier = pltpu.get_barrier_semaphore()
    for t in others:
        pl.semaphore_signal(
            barrier, inc=1, device_id={"seq": t}, device_id_type=pl.DeviceIdType.MESH
        )
    pl.semaphore_wait(barrier, len(others))

    started = []
    for w in range(count):
        for d, t in enumerate(others):
            copy = pltpu.make_async_remote_copy(
                src_ref=sources[w].at[t],
                dst_ref=targets[w].at[seq],
                send_sem=send_sem.at[w, d],
                recv_sem=recv_sem.at[w, seq],
                device_id={"seq": t},
                device_id_type=pl.DeviceIdType.MESH,
            )
            copy.start()
            started.append(copy)
    own = [
        pltpu.make_async_copy(sources[w].at[seq], targets[w].at[seq], local_sem.at[w])
        for w in range(count)
    ]
    for copy in own:
        copy.start()
    for w in range(count):
        for d, t in enumerate(others):
            block = targets[w].at[t]
            pltpu.make_async_remote_copy(
                src_ref=block,
                dst_ref=block,
                send_sem=send_sem.at[w, d],
                recv_sem=recv_sem.at[w, t],
                device_id={"seq": t},
                device_id_type=pl.DeviceIdType.MESH,
            ).wait_recv()
    for copy in started:
        copy.wait_send()
    for copy in own:
        copy.wait()


def exchange(values):
    peers = lax.axis_size("seq")
    count = len(values)
    blocks = tuple(v.reshape(peers, v.shape[0] // peers, -1) for v in values)
    anywhere = pl.BlockSpec(memory_space=pl.ANY)
    dma = pltpu.SemaphoreType.DMA
    arrived = pl.pallas_call(
        partial(exchange_kernel, peers, count),
        out_shape=tuple(jax.ShapeDtypeStruct(v.shape, v.dtype) for v in blocks),
        in_specs=[anywhere] * count,
        out_specs=(anywhere,) * count,
        scratch_shapes=[dma((count,)), dma((count, peers)), dma((count, peers))],
        compiler_params=pltpu.CompilerParams(collective_id=1, has_side_effects=True),
    )(*blocks)
    return tuple(jnp.sum(v.astype(jnp.float32), axis=0) for v in arrived)


def core_sum(own, other):
    arrived = swap(other, "strand")
    return (own.astype(jnp.float32) + arrived.astype(jnp.float32)).astype(jnp.bfloat16)


def share_sum(own, other):
    return lax.psum_scatter(core_sum(own, other), "seq", scatter_dimension=0, tiled=True)


def on_device(
    hidden,
    breaks,
    cotangent,
    input_weight,
    gate_weight,
    key_weight,
    query_weight,
    step_weight,
    output_weight,
    step_bias,
    decay_log,
    skip_gain,
):
    strand = lax.axis_index("strand")
    backward = strand == 1
    seq_index = lax.axis_index("seq")
    length = hidden.shape[0]
    shard_rows = input_weight.shape[0]
    peers = lax.axis_size("seq")
    halves = lax.axis_size("mp")
    width = shard_rows * peers * 2
    half = shard_rows * peers
    part_width = hidden.shape[1]

    target = lax.broadcasted_iota(jnp.int32, (width, width), 1)
    source = lax.broadcasted_iota(jnp.int32, (width, width), 0)
    local = target % half
    side = jnp.where(target < half, strand, 1 - strand)
    feature = (local // shard_rows) * (2 * shard_rows) + side * shard_rows + local % shard_rows
    feature = jnp.where(backward, width - 1 - feature, feature)
    moves = (source == feature).astype(jnp.bfloat16)
    moves = lax.optimization_barrier(moves)

    key_width = key_weight.shape[1]
    inner_width = input_weight.shape[1]
    ahead = jnp.concatenate(
        (input_weight, gate_weight, key_weight, query_weight, step_weight), axis=1
    )
    ahead_full, out_full, everything = gather_all(
        ahead, output_weight, jnp.stack((hidden, cotangent))
    )

    def permuted(which):
        return sum(
            jnp.dot(
                everything[m, which],
                moves[m * part_width : (m + 1) * part_width],
                preferred_element_type=jnp.float32,
            )
            for m in range(halves)
        ).astype(jnp.bfloat16)

    inputs = permuted(0)
    grads_in = permuted(1)
    break_marks = lax.dynamic_slice_in_dim(breaks, seq_index * length, length).astype(jnp.float32)

    def project(start, size):
        return jnp.dot(
            inputs, ahead_full[:, start : start + size], preferred_element_type=jnp.float32
        )

    groups = key_width // STATE
    key_start = 2 * inner_width
    key_vals = project(key_start, key_width).astype(jnp.bfloat16).reshape(length, groups, STATE)
    query_vals = (
        project(key_start + key_width, key_width)
        .astype(jnp.bfloat16)
        .reshape(length, groups, STATE)
    )
    step_raw = project(key_start + 2 * key_width, step_weight.shape[1])
    inner_vals = project(0, inner_width).astype(jnp.bfloat16).reshape(length, -1, HEAD_DIM)
    gate_vals = project(inner_width, inner_width).astype(jnp.bfloat16).reshape(length, groups, -1)

    local_terms, local_pull = jax.vjp(
        partial(block_terms, backward, step_bias, decay_log, break_marks),
        inner_vals,
        key_vals,
        query_vals,
        step_raw,
    )
    total_log, total_state = local_terms[4:]
    head_shape = total_state.shape[:2]
    heads = total_log.shape[0]
    log_pieces = []
    rest = total_log
    for _ in range(3):
        piece = lax.reduce_precision(rest, 8, 7)
        log_pieces.append(piece)
        rest = rest - piece
    log_rows = jnp.pad(jnp.stack(log_pieces), ((0, 13), (0, STATE - heads)))
    sent = jnp.concatenate(
        (total_state.reshape(-1, STATE).astype(jnp.bfloat16), log_rows.astype(jnp.bfloat16))
    )
    arrived = lax.all_gather(sent, "seq")
    state_rows = heads * HEAD_DIM
    all_logs = jnp.sum(arrived[:, state_rows : state_rows + 3, :heads].astype(jnp.float32), axis=1)
    order = earlier_than(peers, backward)
    chain = chain_weights(order, all_logs)
    here = lax.dynamic_index_in_dim(chain, seq_index, 0, keepdims=False)
    there = lax.dynamic_index_in_dim(chain, seq_index, 1, keepdims=False)

    def chained(everything, weights):
        weights = weights.reshape((peers,) + head_shape)
        return sum(
            weights[k][..., None, None]
            * everything[k].reshape(total_state.shape).astype(jnp.float32)
            for k in range(peers)
        )

    entering = chained(arrived[:, :state_rows], here)
    mixer_out, finish_pull = jax.vjp(
        partial(finish_terms, skip_gain), *local_terms[:4], query_vals, inner_vals, entering
    )
    gated, gate_pull = jax.vjp(gate_terms, mixer_out, gate_vals)
    gated_flat = gated.reshape(length, -1)

    gated_back = jnp.dot(grads_in, out_full, preferred_element_type=jnp.float32).astype(jnp.bfloat16).reshape(gated.shape)
    mixer_back, gate_back = gate_pull(gated_back)
    finish_back = finish_pull(mixer_back)
    carried_back = chained(lax.all_gather(finish_back[6].astype(jnp.bfloat16), "seq"), there)

    contract_rows = (((1,), (1,)), ((), ()))
    head_terms = tuple(
        lax.dot_general(
            gated_flat, part, contract_rows, preferred_element_type=jnp.float32
        ).astype(jnp.bfloat16)
        for part in (out_full[:half], out_full[half:])
    )
    head_terms = jnp.stack(
        [
            sum(
                lax.dot_general(
                    head_terms[s],
                    moves[m * part_width : (m + 1) * part_width, s * half : (s + 1) * half],
                    contract_rows,
                    preferred_element_type=jnp.float32,
                )
                for s in range(2)
            ).astype(jnp.bfloat16)
            for m in range(halves)
        ]
    )
    reduced = lax.psum_scatter(head_terms, "mp", scatter_dimension=0)
    combined = (
        reduced.astype(jnp.float32) + swap(reduced, "strand").astype(jnp.float32)
    ).astype(jnp.bfloat16)

    contract = (((0,), (0,)), ((), ()))

    def grad_pair(left, right):
        return tuple(
            lax.dot_general(part, right, contract, preferred_element_type=jnp.float32).astype(
                jnp.bfloat16
            )
            for part in (left[:, :half], left[:, half:])
        )

    grad_output = share_sum(*grad_pair(grads_in, gated_flat)).astype(jnp.float32)
    grad_gate = share_sum(*grad_pair(inputs, gate_back.reshape(length, -1))).astype(jnp.float32)

    log_back = jnp.sum(carried_back * entering, axis=(-2, -1)).reshape(
        total_log.shape
    ) * jnp.exp(total_log)
    local_back = local_pull((*finish_back[:4], log_back, carried_back))
    inner_back = (local_back[0] + finish_back[5]).reshape(length, -1)
    key_back = local_back[1].reshape(length, -1)
    query_back = (local_back[2] + finish_back[4]).reshape(length, -1)
    step_back = local_back[3]

    input_terms = grad_pair(inputs, inner_back)
    small_terms = tuple(
        jnp.concatenate(
            (
                lax.dot_general(
                    part, key_back, contract, preferred_element_type=jnp.float32
                ).astype(jnp.bfloat16),
                lax.dot_general(
                    part, query_back, contract, preferred_element_type=jnp.float32
                ).astype(jnp.bfloat16),
                lax.dot_general(
                    part.astype(jnp.float32), step_back, contract, precision=HIGHEST
                ).astype(jnp.bfloat16),
            ),
            axis=1,
        )
        for part in (inputs[:, :half], inputs[:, half:])
    )
    grad_input, small_share = exchange((core_sum(*input_terms), core_sum(*small_terms)))
    return (
        combined,
        grad_input,
        grad_gate,
        small_share[:, :key_width],
        small_share[:, key_width : 2 * key_width],
        small_share[:, 2 * key_width :],
        grad_output,
    )


NN = (((1,), (0,)), ((), ()))
NT = (((1,), (1,)), ((), ()))
TN = (((0,), (0,)), ((), ()))
F32 = jnp.float32
BF16 = jnp.bfloat16


def mm(left, right, dims=NN, **options):
    return lax.dot_general(left, right, dims, preferred_element_type=F32, **options)


def iota(shape, axis):
    return lax.broadcasted_iota(jnp.int32, shape, axis)


def aligned(start, size, unit=None):
    return pl.ds(pl.multiple_of(start, unit or size), size)


def per_head(columns, first):
    low = iota((columns.shape[0], 128), 1) < HEAD_DIM
    parts = []
    for pair in range(2):
        at = first + 2 * pair
        wide = [
            jnp.broadcast_to(columns[:, at + i : at + i + 1], (columns.shape[0], 128))
            for i in range(2)
        ]
        parts.append(jnp.where(low, *wide))
    return jnp.concatenate(parts, axis=1)


def head_rows(value, select):
    high = value.astype(BF16)
    low = (value - high.astype(F32)).astype(BF16)
    return (mm(select, high, NT) + mm(select, low, NT))[:8]


def remote(source, target, send, receive, device):
    return pltpu.make_async_remote_copy(
        src_ref=source,
        dst_ref=target,
        send_sem=send,
        recv_sem=receive,
        device_id=device,
        device_id_type=pl.DeviceIdType.MESH,
    )


def mixer_kernel(peers, *refs):
    (
        hidden,
        cotangent,
        input_weight,
        key_weight,
        query_weight,
        gate_weight,
        output_weight,
        step_weight,
        marks_ref,
        bias_ref,
        decay_ref,
        gain_ref,
        combined,
        rg,
        rgs,
        u_ref,
        t_ref,
        w_ref,
        step_ref,
        steps,
        weff,
        seff,
        xbcz,
        dxbc,
        dz_ref,
        gated,
        y_ref,
        r_rows,
        dt_rows,
        k_rows,
        dr_rows,
        entering,
        state,
        p_ref,
        p_mate,
        acc,
        x_out,
        x_in,
        z_out,
        z_in,
        g_own,
        g_mate,
        g_out,
        gs_own,
        gs_mate,
        gs_out,
        local_sem,
        z_send,
        z_recv,
        x_send,
        x_recv,
        m_send,
        m_recv,
        w_send,
        w_recv,
        s_send,
        s_recv,
        p_send,
        p_recv,
        px_send,
        px_recv,
        pz_send,
        pz_recv,
        g_send,
        g_recv,
        gz_send,
        gz_recv,
        gs_send,
        gs_recv,
        c_sem,
    ) = refs
    part = lax.axis_index("parts")
    seq = lax.axis_index("seq")
    strand = lax.axis_index("strand")
    model = lax.axis_index("mp")
    backward = strand == 1
    twin = {"parts": 1 - part}
    mate = {"strand": 1 - strand}
    side = {"mp": 1 - model}
    others = [lax.rem(seq + d, peers) for d in range(1, peers)]
    has_up, has_down = seq < peers - 1, seq > 0

    length, features = hidden.shape
    half = length // 2
    shard = step_weight.shape[0]
    thin = shard // 2
    shards = 2 * peers
    positions, width = u_ref.shape
    blocks = positions // STRETCH
    heads = bias_ref.shape[0] // peers
    inner = heads * HEAD_DIM
    narrow = inner + 2 * STATE
    sources = (hidden, cotangent)
    fulls = (u_ref, t_ref)

    def mirrored(i, count):
        return jnp.where(backward, count - 1 - i, i)

    barrier = pltpu.get_barrier_semaphore()
    targets = [{"seq": t} for t in others] + [twin, mate, side]
    for target in targets:
        pl.semaphore_signal(
            barrier, inc=1, device_id=target, device_id_type=pl.DeviceIdType.MESH
        )
    pl.semaphore_wait(barrier, len(targets))

    def piece(a, block, which, core):
        return fulls[a].at[
            aligned(block * length + core * half, half), aligned(which * features, features)
        ]

    def own(a):
        return sources[a].at[aligned(strand * half, half), :]

    def up(a, block, source):
        return remote(
            source,
            piece(a, block, model, strand),
            z_send.at[a, 0, block],
            z_recv.at[a, block],
            {"seq": jnp.minimum(seq + 1, peers - 1)},
        )

    def down(a, block, source):
        return remote(
            source,
            piece(a, block, model, strand),
            z_send.at[a, 1, block],
            z_recv.at[a, block],
            {"seq": jnp.maximum(seq - 1, 0)},
        )

    def across(a, block, source):
        return remote(
            source,
            piece(a, block, model, strand),
            x_send.at[a, block],
            x_recv.at[a, block],
            side,
        )

    def to_mate(a, block, which):
        mine = piece(a, block, which, strand)
        return remote(mine, mine, m_send.at[a, block, which], m_recv.at[a, block, which], mate)

    def wait_z(a, block):
        mine = piece(a, block, model, strand)
        remote(mine, mine, z_send.at[a, 0, block], z_recv.at[a, block], side).wait_recv()

    def wait_x(a, block):
        mine = piece(a, block, 1 - model, strand)
        remote(mine, mine, x_send.at[a, block], x_recv.at[a, block], side).wait_recv()

    def wait_mate(a, block, which):
        mine = piece(a, block, which, 1 - strand)
        remote(
            mine, mine, m_send.at[a, block, which], m_recv.at[a, block, which], mate
        ).wait_recv()

    def launch_up(a):
        pl.when(has_up)(lambda: up(a, seq, own(a)).start())

    def launch_down(a):
        pl.when(has_down)(lambda: down(a, seq, own(a)).start())

    def near(d, action):
        if d == 0:
            action(seq)
        else:
            pl.when(seq >= d)(lambda: action(seq - d))
            pl.when(seq + d < peers)(lambda: action(seq + d))

    def relay(a, d):
        def pass_on(block, more, onward):
            mine = piece(a, block, model, strand)
            wait_z(a, block)
            pl.when(more)(lambda: onward(a, block, mine).start())
            across(a, block, mine).start()
            to_mate(a, block, model).start()

        pl.when(seq >= d)(lambda: pass_on(seq - d, has_up, up))
        pl.when(seq + d < peers)(lambda: pass_on(seq + d, has_down, down))

    def from_side(a):
        def action(block):
            wait_x(a, block)
            to_mate(a, block, 1 - model).start()

        return action

    def all_here(a):
        for d in range(peers):

            def arrivals(block, d=d):
                if d:
                    wait_mate(a, block, model)
                wait_mate(a, block, 1 - model)

            near(d, arrivals)

    def all_sent(a):
        for d in range(peers):

            def sent(block, d=d):
                mine = piece(a, block, model, strand)
                across(a, block, mine).wait_send()
                if d:
                    to_mate(a, block, model).wait_send()
                to_mate(a, block, 1 - model).wait_send()
                pl.when(jnp.logical_and(has_up, block <= seq))(
                    lambda: up(a, block, mine).wait_send()
                )
                pl.when(jnp.logical_and(has_down, block >= seq))(
                    lambda: down(a, block, mine).wait_send()
                )

            near(d, sent)

    def own_copy(a):
        target = fulls[a].at[
            aligned(seq * length, length), aligned(model * features, features)
        ]
        return pltpu.make_async_copy(sources[a], target, local_sem.at[a])

    weights = (input_weight, key_weight, query_weight, gate_weight, output_weight)
    starts = [0, inner, inner + STATE, narrow, narrow + inner, narrow + 2 * inner]

    def w_rows(block, core, which=None):
        first = (2 * block + core) * shard
        if which is None:
            return aligned(first, shard)
        return aligned(first + which * thin, thin)

    def w_sends(t):
        for weight, first, last in zip(weights, starts, starts[1:]):
            size = last - first
            yield remote(
                weight.at[aligned(part * thin, thin), aligned(t * size, size)],
                w_ref.at[w_rows(seq, strand, part), first:last],
                w_send.at[0, t],
                w_recv.at[0, seq],
                {"seq": t},
            )

    def s_sends(t):
        return remote(
            steps.at[t], step_ref.at[2 * seq + strand], s_send.at[0, t], s_recv.at[0, seq], {"seq": t}
        )

    def own_weights():
        for weight, first, last in zip(weights, starts, starts[1:]):
            size = last - first
            yield pltpu.make_async_copy(
                weight.at[:, aligned(seq * size, size)],
                w_ref.at[w_rows(seq, strand), first:last],
                local_sem.at[2],
            )

    def w_own_to_mate():
        mine = w_ref.at[w_rows(seq, strand), :]
        return remote(mine, mine, w_send.at[0, seq], w_recv.at[0, seq], mate)

    def s_own_to_mate():
        mine = step_ref.at[2 * seq + strand]
        return remote(mine, mine, s_send.at[0, seq], s_recv.at[0, seq], mate)

    def w_move(index, block, core, which, device):
        mine = w_ref.at[w_rows(block, core, which), :]
        return remote(mine, mine, w_send.at[index, block], w_recv.at[index, block], device)

    def s_move(index, block, core):
        mine = step_ref.at[2 * block + core]
        return remote(mine, mine, s_send.at[index, block], s_recv.at[index, block], mate)

    launch_up(0)
    launch_down(0)
    across(0, seq, own(0)).start()
    for t in others:
        for copy in w_sends(t):
            copy.start()
    for copy in own_weights():
        copy.start()
    for a in range(2):
        own_copy(a).start()
    pl.when(seq == 0)(lambda: launch_up(1))
    pl.when(seq == peers - 1)(lambda: launch_down(1))

    step_now = step_weight[...]
    for t in others + [seq]:
        taken = iota((16, heads * peers), 1) == iota((16, heads * peers), 0) + heads * t
        taken = jnp.logical_and(taken, iota((16, heads * peers), 0) < heads)
        turned = mm(jnp.where(taken, 1.0, 0.0).astype(BF16), step_now, NT).astype(BF16)
        if t is seq:
            step_ref[2 * seq + strand] = turned
            s_own_to_mate().start()
        else:
            steps[t] = turned
            s_sends(t).start()
    mine = w_ref.at[w_rows(seq, strand), :]
    pltpu.make_async_copy(mine, mine, local_sem.at[2]).wait()
    w_own_to_mate().start()

    for d in range(1, peers):
        relay(0, d)
        pl.when(seq == d)(lambda: launch_up(1))
        pl.when(peers - 1 - seq == d)(lambda: launch_down(1))
        near(d - 1, from_side(0))
    across(1, seq, own(1)).start()
    for t in others:
        w_move(0, t, strand, part, mate).wait_recv()
        w_move(1, t, strand, part, twin).start()
        w_move(2 + part, t, strand, part, mate).start()
        s_move(0, t, strand).wait_recv()
        s_move(1, t, strand).start()
    near(peers - 1, from_side(0))
    for t in others:
        w_move(1, t, strand, 1 - part, twin).wait_recv()
        w_move(3 - part, t, strand, 1 - part, mate).start()
    relay(1, 1)

    for t in others:
        for which in range(2):
            w_move(2 + which, t, 1 - strand, which, mate).wait_recv()
        s_move(1, t, 1 - strand).wait_recv()
    theirs = w_ref.at[w_rows(seq, 1 - strand), :]
    remote(theirs, theirs, w_send.at[0, seq], w_recv.at[0, seq], mate).wait_recv()
    s_move(0, seq, 1 - strand).wait_recv()

    row = iota((shard, shard), 0)
    column = iota((shard, shard), 1)
    other = jnp.where(backward, shard - 1 - column, column)
    moves = jnp.where(row == other, 1.0, 0.0).astype(BF16)
    for b in range(shards):
        source = mirrored(b, shards)
        weff[b * shard : (b + 1) * shard, :] = mm(
            moves, w_ref[aligned(source * shard, shard), :]
        ).astype(BF16)
        seff[:, b * shard : (b + 1) * shard] = mm(step_ref[source], moves).astype(BF16)

    lead = iota((STRETCH, STRETCH), 0) - iota((STRETCH, STRETCH), 1)
    lead = jnp.where(backward, -lead, lead)
    causal = lead >= 0
    sums_to = (lead <= 0).astype(F32)
    sums_from = (lead >= 0).astype(F32)
    sums_before = (lead < 0).astype(F32)
    low_lanes = iota((STRETCH, 128), 1) < HEAD_DIM
    select = jnp.where(
        iota((16, inner), 1) // HEAD_DIM == iota((16, inner), 0), 1.0, 0.0
    ).astype(BF16)
    bias = jnp.zeros((8, STRETCH), F32)
    rates = jnp.zeros((8, STRETCH), F32)
    skip = jnp.zeros((1, inner), F32)
    for h in range(heads):
        at_head = iota((8, STRETCH), 0) == h
        bias = jnp.where(at_head, bias_ref[seq * heads + h], bias)
        rates = jnp.where(at_head, decay_ref[seq * heads + h], rates)
        skip = jnp.where(iota((1, inner), 1) // HEAD_DIM == h, gain_ref[seq * heads + h], skip)
    rates = -jnp.exp(rates)
    filler = jnp.zeros((128 - 24, STRETCH), F32)

    def columns_of(k, a, dt):
        ends = jnp.broadcast_to(jnp.sum(a, axis=1, keepdims=True), a.shape)
        return jnp.transpose(jnp.concatenate((k, dt, ends, filler), axis=0))

    all_here(0)
    for a in range(2):
        own_copy(a).wait()
    state[...] = jnp.zeros_like(state)

    def p_to_mate(t):
        return remote(
            p_ref.at[aligned(t * length + (1 - strand) * half, half), :],
            p_mate.at[t],
            p_send.at[t],
            p_recv.at[t],
            mate,
        )

    def forward(c, carry):
        for d in range(peers):
            pl.when(c == 2 * d)(lambda d=d: near(d, from_side(1)))
            if d > 1:
                pl.when(c == 2 * d - 3)(lambda d=d: relay(1, d))
        blk = mirrored(c, blocks)
        at = aligned(blk * STRETCH, STRETCH)
        u = u_ref[at, :]
        projected = mm(u, weff[:, : narrow + inner]).astype(BF16)
        xbcz[at, :] = projected
        x = projected[:, :inner]
        b = projected[:, inner : inner + STATE]
        q = projected[:, inner + STATE : narrow]
        z = projected[:, narrow:].astype(F32)
        r = mm(seff[...], u, NT)[:8] + bias
        dt = jnp.maximum(r, 0.0) + jnp.log1p(jnp.exp(-jnp.abs(r)))
        marks = jnp.concatenate(
            [marks_ref[pl.ds(2 * blk + i, 1), :] for i in range(2)], axis=1
        ).astype(F32)
        a = rates * dt + KEEP_LOG * marks
        k = mm(a, sums_to, precision=HIGHEST)
        r_rows[blk] = r
        dt_rows[blk] = dt
        k_rows[blk] = jnp.concatenate((k, a), axis=0)
        cols = columns_of(k, a, dt)
        scores = mm(q, b, NT)
        parts = []
        for pair in range(2):
            outs = []
            for i in range(2):
                h = 2 * pair + i
                spread = jnp.where(causal, cols[:, h : h + 1] - k[h : h + 1, :], -1e30)
                mixing = (scores * jnp.exp(spread) * dt[h : h + 1, :]).astype(BF16)
                outs.append(mm(mixing, x[:, 128 * pair : 128 * (pair + 1)]))
            parts.append(jnp.where(low_lanes, *outs))
        y = jnp.concatenate(parts, axis=1)
        before = state[...]
        entering[blk] = before
        carried = mm(q, before.astype(BF16))
        wide_k = per_head(cols, 0)
        wide_dt = per_head(cols, 8)
        wide_end = per_head(cols, 16)
        xf = x.astype(F32)
        y = y + jnp.exp(wide_k) * carried + skip * xf
        e = (jnp.exp(wide_end - wide_k) * wide_dt * xf).astype(BF16)
        state[...] = jnp.exp(wide_end[0:1, :]) * before + mm(b, e, TN)
        y_ref[at, :] = y

        v = y * (z / (1.0 + jnp.exp(-z)))
        scale = lax.rsqrt(jnp.mean(v * v, axis=1, keepdims=True) + EPSILON)
        g = (v * scale).astype(BF16)
        gated[at, :] = g
        p_ref[at, :] = mm(g, weff[:, narrow + inner :], NT).astype(BF16)
        pl.when(lax.rem(c, 2) == 1)(lambda: p_to_mate(blk // 2).start())
        return carry

    lax.fori_loop(0, blocks, forward, 0)

    def turn(j):
        return lax.rem(seq + 1 + j, peers)

    def p_across(t):
        return remote(x_out.at[t], x_in.at[t], px_send.at[t], px_recv.at[t], side)

    def p_along(t):
        return remote(z_out.at[t], z_in.at[seq], pz_send.at[t], pz_recv.at[seq], {"seq": t})

    def add_core(j, carry):
        t = turn(j)
        p_to_mate(t).wait_recv()
        rows = aligned(t * length + strand * half, half)
        there = aligned((1 - model) * features, features)
        here = aligned(model * features, features)
        x_out[t] = (p_ref[rows, there].astype(F32) + p_mate[t, :, there].astype(F32)).astype(BF16)
        p_across(t).start()
        acc[t] = p_ref[rows, here].astype(F32) + p_mate[t, :, here].astype(F32)
        return carry

    def add_side(j, carry):
        t = turn(j)
        p_across(t).wait_recv()
        total = acc[t] + x_in[t].astype(F32)
        acc[t] = total

        def send():
            z_out[t] = total.astype(BF16)
            p_along(t).start()

        pl.when(j < peers - 1)(send)
        return carry

    lax.fori_loop(0, peers, add_core, 0)

    all_here(1)

    def gate_back(c, carry):
        at = aligned(c * STRETCH, STRETCH)
        z = xbcz[at, narrow:].astype(F32)
        y = y_ref[at, :]
        sig = 1.0 / (1.0 + jnp.exp(-z))
        silu = z * sig
        v = y * silu
        scale = lax.rsqrt(jnp.mean(v * v, axis=1, keepdims=True) + EPSILON)
        dg = mm(t_ref[at, :], weff[:, narrow + inner :]).astype(BF16).astype(F32)
        along = jnp.mean(dg * v, axis=1, keepdims=True)
        dv = scale * (dg - v * (scale * scale * along))
        y_ref[at, :] = dv * silu
        dz_ref[at, :] = (dv * y * (sig * (1.0 + z * (1.0 - sig)))).astype(BF16)
        return carry

    lax.fori_loop(0, blocks, gate_back, 0)
    lax.fori_loop(0, peers, add_side, 0)

    def g_to_mate(part_of, t):
        return remote(
            g_own.at[part_of, t],
            g_mate.at[part_of, t],
            g_send.at[part_of, t],
            g_recv.at[part_of, t],
            mate,
        )

    def g_along(part_of, t):
        return remote(
            g_out.at[part_of, t],
            rg.at[part_of, seq],
            gz_send.at[part_of, t],
            gz_recv.at[part_of, seq],
            {"seq": t},
        )

    def gs_to_mate(t):
        return remote(gs_own.at[t], gs_mate.at[t], gs_send.at[0, t], gs_recv.at[0, t], mate)

    def gs_along(t):
        return remote(gs_out.at[t], rgs.at[seq], gs_send.at[1, t], gs_recv.at[1, seq], {"seq": t})

    def lanes_of(block, core):
        return aligned(mirrored(2 * block + core, shards) * shard, shard)

    def early_terms(block, core):
        at = lanes_of(block, core)
        found = jnp.concatenate(
            (mm(u_ref[:, at], dz_ref[...], TN), mm(t_ref[:, at], gated[...], TN)), axis=1
        )
        return mm(moves, found.astype(BF16))

    def late_terms(block, core):
        return mm(moves, mm(u_ref[:, lanes_of(block, core)], dxbc[...], TN).astype(BF16))

    def weigh(part_of, terms):
        def for_mate(j, carry):
            t = turn(j)
            g_own[part_of, t] = terms(t, 1 - strand).astype(BF16)
            g_to_mate(part_of, t).start()
            return carry

        def for_owner(j, carry):
            t = turn(j)
            mine = terms(t, strand)
            g_to_mate(part_of, t).wait_recv()
            total = (mine + g_mate[part_of, t].astype(F32)).astype(BF16)

            def send():
                g_out[part_of, t] = total
                g_along(part_of, t).start()

            def keep():
                rg[part_of, t] = total

            pl.when(j < peers - 1)(send)
            pl.when(j == peers - 1)(keep)
            return carry

        lax.fori_loop(0, peers, for_mate, 0)
        lax.fori_loop(0, peers, for_owner, 0)

    weigh(0, early_terms)

    state[...] = jnp.zeros_like(state)

    def backwards(c, carry):
        blk = mirrored(blocks - 1 - c, blocks)
        at = aligned(blk * STRETCH, STRETCH)
        x = xbcz[at, :inner]
        b = xbcz[at, inner : inner + STATE]
        q = xbcz[at, inner + STATE : narrow]
        xf = x.astype(F32)
        dy = y_ref[at, :]
        dyb = dy.astype(BF16)
        dt = dt_rows[blk]
        k = k_rows[blk, :8]
        cols = columns_of(k, k_rows[blk, 8:], dt)
        wide_k = per_head(cols, 0)
        wide_dt = per_head(cols, 8)
        wide_end = per_head(cols, 16)
        before = entering[blk]
        before_b = before.astype(BF16)
        leaving = state[...]
        leaving_b = leaving.astype(BF16)

        keep = jnp.exp(wide_end - wide_k)
        keep_x = keep * xf
        de = mm(b, leaving_b)
        db = mm((keep_x * wide_dt).astype(BF16), leaving_b, NT)
        ddt = head_rows(de * keep_x, select)
        dx = de * (keep * wide_dt) + skip * dy

        grown = jnp.exp(wide_k) * dy
        grown_b = grown.astype(BF16)
        dq = mm(grown_b, before_b, NT)
        dk = head_rows(grown * mm(q, before_b), select)
        end_row = jnp.exp(wide_end[0:1, :])
        total = jnp.sum(before * leaving, axis=0, keepdims=True) * end_row
        total = head_rows(jnp.broadcast_to(total, (128, inner)), select)[:, 0:1]
        state[...] = end_row * leaving + mm(q, grown_b, TN)

        scores = mm(q, b, NT)
        dscores = jnp.zeros((STRETCH, STRETCH), F32)
        row_sums = jnp.zeros((STRETCH, 128), F32)
        lane = iota((STRETCH, 128), 1)
        dx_parts = []
        col_sums = []
        for pair in range(2):
            pair_at = slice(128 * pair, 128 * (pair + 1))
            outs = []
            for i in range(2):
                h = 2 * pair + i
                dt_row = dt[h : h + 1, :]
                spread = jnp.where(causal, cols[:, h : h + 1] - k[h : h + 1, :], -1e30)
                decay = jnp.exp(spread)
                mine = low_lanes if i == 0 else jnp.logical_not(low_lanes)
                dy_head = jnp.where(mine, dy[:, pair_at], 0.0).astype(BF16)
                dmix = mm(dy_head, x[:, pair_at], NT) * decay
                mixing = (scores * decay * dt_row).astype(BF16)
                outs.append(mm(mixing, dyb[:, pair_at], TN))
                dscores = dscores + dmix * dt_row
                dmix = dmix * scores
                col_sums.append(jnp.sum(dmix, axis=0, keepdims=True))
                summed = jnp.sum(dmix * dt_row, axis=1, keepdims=True)
                row_sums = jnp.where(lane == h, summed, row_sums)
            dx_parts.append(jnp.where(low_lanes, *outs))
        dx = dx + jnp.concatenate(dx_parts, axis=1)
        dscores_b = dscores.astype(BF16)
        dq = dq + mm(dscores_b, b)
        db = db + mm(dscores_b, q, TN)
        dxbc[at, :inner] = dx.astype(BF16)
        dxbc[at, inner : inner + STATE] = db.astype(BF16)
        dxbc[at, inner + STATE :] = dq.astype(BF16)

        columns = jnp.concatenate(col_sums + [jnp.zeros((4, STRETCH), F32)], axis=0)
        dk = dk + jnp.transpose(row_sums)[:8] - dt * columns
        da = mm(dk, sums_from, precision=HIGHEST)
        da = da + mm(dt * ddt, sums_before, precision=HIGHEST) + total
        ddt = ddt + columns + rates * da
        dr_rows[blk] = ddt / (1.0 + jnp.exp(-r_rows[blk]))
        return carry

    lax.fori_loop(0, blocks, backwards, 0)

    total = acc[seq]
    for t in others:
        remote(z_in.at[t], z_in.at[t], pz_send.at[t], pz_recv.at[t], {"seq": t}).wait_recv()
        total = total + z_in[t].astype(F32)
    mine = aligned(strand * half, half)
    combined[mine, :] = total.astype(BF16)
    rows = combined.at[mine, :]
    last = remote(rows, rows, c_sem.at[0], c_sem.at[1], mate)
    last.start()

    weigh(1, late_terms)
    dr = jnp.concatenate([dr_rows[i] for i in range(blocks)], axis=1)
    dr_high = dr.astype(BF16)
    dr_low = (dr - dr_high.astype(F32)).astype(BF16)
    dr_both = jnp.concatenate((dr_high, dr_low), axis=0)

    def step_terms(block, core):
        both = mm(dr_both, u_ref[:, lanes_of(block, core)])
        both = jnp.concatenate((both[:8] + both[8:], jnp.zeros((8, shard), F32)), axis=0)
        return mm(both.astype(BF16), moves)

    for t in others + [seq]:
        gs_own[t] = step_terms(t, 1 - strand).astype(BF16)
        gs_to_mate(t).start()
    for t in others + [seq]:
        mine = step_terms(t, strand)
        gs_to_mate(t).wait_recv()
        total = (mine + gs_mate[t].astype(F32)).astype(BF16)
        if t is seq:
            rgs[t] = total
        else:
            gs_out[t] = total
            gs_along(t).start()

    for t in others:
        for i in range(2):
            remote(
                rg.at[i, t], rg.at[i, t], gz_send.at[i, t], gz_recv.at[i, t], {"seq": t}
            ).wait_recv()
        remote(
            rgs.at[t], rgs.at[t], gs_send.at[1, t], gs_recv.at[1, t], {"seq": t}
        ).wait_recv()
    theirs = combined.at[aligned((1 - strand) * half, half), :]
    remote(theirs, theirs, c_sem.at[0], c_sem.at[1], mate).wait_recv()
    last.wait_send()
    for a in range(2):
        all_sent(a)
    for t in others:
        w_move(0, t, strand, part, mate).wait_send()
        w_move(1, t, strand, part, twin).wait_send()
        w_move(2 + part, t, strand, part, mate).wait_send()
        w_move(3 - part, t, strand, 1 - part, mate).wait_send()
        s_sends(t).wait_send()
        s_move(1, t, strand).wait_send()
        p_along(t).wait_send()
        gs_along(t).wait_send()
        for i in range(2):
            g_along(i, t).wait_send()
    w_own_to_mate().wait_send()
    s_own_to_mate().wait_send()
    for t in others + [seq]:
        p_to_mate(t).wait_send()
        p_across(t).wait_send()
        gs_to_mate(t).wait_send()
        for i in range(2):
            g_to_mate(i, t).wait_send()


def finish_kernel(heads, combined, rg, rgs, out, g_in, g_gate, g_key, g_query, g_step, g_out):
    peers = rg.shape[1]
    inner = g_in.shape[1] // peers
    out[...] = combined[...]
    total = jnp.zeros(g_step.shape, F32)
    for s in range(peers):
        early, late = rg[0, s].astype(F32), rg[1, s].astype(F32)
        wide = slice(s * inner, (s + 1) * inner)
        small = slice(s * STATE, (s + 1) * STATE)
        g_gate[:, wide] = early[:, :inner]
        g_out[:, wide] = early[:, inner:]
        g_in[:, wide] = late[:, :inner]
        g_key[:, small] = late[:, inner : inner + STATE]
        g_query[:, small] = late[:, inner + STATE :]
        taken = iota((16, heads * peers), 1) == iota((16, heads * peers), 0) + heads * s
        taken = jnp.logical_and(taken, iota((16, heads * peers), 0) < heads)
        total = total + mm(rgs[s], jnp.where(taken, 1.0, 0.0).astype(BF16), TN)
    g_step[...] = total


def by_group(
    hidden,
    breaks,
    cotangent,
    input_weight,
    gate_weight,
    key_weight,
    query_weight,
    step_weight,
    output_weight,
    step_bias,
    decay_log,
    skip_gain,
):
    peers, models = lax.axis_size("seq"), lax.axis_size("mp")
    length, features = hidden.shape
    half = length // 2
    shard = input_weight.shape[0]
    positions, width = length * peers, features * models
    blocks = positions // STRETCH
    heads = step_bias.shape[0] // peers
    inner = heads * HEAD_DIM
    narrow = inner + 2 * STATE
    columns = narrow + 2 * inner
    dma = pltpu.SemaphoreType.DMA
    anywhere = pl.BlockSpec(memory_space=pl.ANY)
    vmem = pl.BlockSpec(memory_space=pltpu.VMEM)
    smem = pl.BlockSpec(memory_space=pltpu.SMEM)
    strips = pltpu.VMEM((2, peers, shard, 2 * inner), BF16)
    steps = pltpu.VMEM((peers, 16, shard), BF16)
    rows8 = pltpu.VMEM((blocks, 8, STRETCH), F32)
    halves = pltpu.VMEM((peers, half, features), BF16)
    combined, rg, rgs = pl.pallas_call(
        partial(mixer_kernel, peers),
        out_shape=(
            jax.ShapeDtypeStruct((length, features), BF16),
            jax.ShapeDtypeStruct((2, peers, shard, 2 * inner), BF16),
            jax.ShapeDtypeStruct((peers, 16, shard), BF16),
        ),
        in_specs=[anywhere] * 7 + [vmem] * 2 + [smem] * 3,
        out_specs=(vmem,) * 3,
        scratch_shapes=[
            pltpu.VMEM((positions, width), BF16),
            pltpu.VMEM((positions, width), BF16),
            pltpu.VMEM((width, columns), BF16),
            pltpu.VMEM((2 * peers, 16, shard), BF16),
            steps,
            pltpu.VMEM((width, columns), BF16),
            pltpu.VMEM((16, width), BF16),
            pltpu.VMEM((positions, narrow + inner), BF16),
            pltpu.VMEM((positions, narrow), BF16),
            pltpu.VMEM((positions, inner), BF16),
            pltpu.VMEM((positions, inner), BF16),
            pltpu.VMEM((positions, inner), F32),
            rows8,
            rows8,
            pltpu.VMEM((blocks, 16, STRETCH), F32),
            rows8,
            pltpu.VMEM((blocks, STATE, inner), F32),
            pltpu.VMEM((STATE, inner), F32),
            pltpu.VMEM((positions, width), BF16),
            pltpu.VMEM((peers, half, width), BF16),
            pltpu.VMEM((peers, half, features), F32),
            halves,
            halves,
            halves,
            halves,
            strips,
            strips,
            strips,
            steps,
            steps,
            steps,
            dma((3,)),
            dma((2, 2, peers)),
            dma((2, peers)),
            dma((2, peers)),
            dma((2, peers)),
            dma((2, peers, 2)),
            dma((2, peers, 2)),
            dma((4, peers)),
            dma((4, peers)),
            dma((2, peers)),
            dma((2, peers)),
            dma((peers,)),
            dma((peers,)),
            dma((peers,)),
            dma((peers,)),
            dma((peers,)),
            dma((peers,)),
            dma((2, peers)),
            dma((2, peers)),
            dma((2, peers)),
            dma((2, peers)),
            dma((2, peers)),
            dma((2, peers)),
            dma((2,)),
        ],
        compiler_params=pltpu.CompilerParams(
            collective_id=2, has_side_effects=True, vmem_limit_bytes=60 * 1024 * 1024
        ),
    )(
        hidden,
        cotangent,
        input_weight,
        key_weight,
        query_weight,
        gate_weight,
        output_weight,
        step_weight,
        breaks.reshape(-1, 128),
        step_bias,
        decay_log,
        skip_gain,
    )

    wide = jax.ShapeDtypeStruct((shard, peers * inner), F32)
    small = jax.ShapeDtypeStruct((shard, peers * STATE), F32)
    return pl.pallas_call(
        partial(finish_kernel, heads),
        out_shape=(
            jax.ShapeDtypeStruct(combined.shape, BF16),
            wide,
            wide,
            small,
            small,
            jax.ShapeDtypeStruct((shard, peers * heads), F32),
            wide,
        ),
        in_specs=[vmem] * 3,
        out_specs=(vmem,) * 7,
        compiler_params=pltpu.CompilerParams(vmem_limit_bytes=32 * 1024 * 1024),
    )(combined, rg, rgs)


def solution(mesh):
    in_specs = (
        P(("parts", "seq"), "mp"),
        P("parts"),
        P(("parts", "seq"), "mp"),
        P(("seq", "strand"), "mp"),
        P(("seq", "strand"), "mp"),
        P(("seq", "strand"), "mp"),
        P(("seq", "strand"), "mp"),
        P(("seq", "strand"), "mp"),
        P(("seq", "strand"), "mp"),
        P("mp"),
        P("mp"),
        P("mp"),
    )
    out_specs = (
        P(("parts", "seq"), "mp"),
        P(("parts", "seq", "strand"), "mp"),
        P(("parts", "seq", "strand"), "mp"),
        P(("parts", "seq", "strand"), "mp"),
        P(("parts", "seq", "strand"), "mp"),
        P(("parts", "seq", "strand"), "mp"),
        P(("parts", "seq", "strand"), "mp"),
    )
    peers = mesh.shape["seq"]

    def each(*args):
        groups = args[5].shape[1] // STATE
        heads = args[9].shape[0]
        fits = peers == groups and heads == 4 * groups and mesh.shape["mp"] == 2
        return (by_group if fits else on_device)(*args)

    return jax.shard_map(
        each, mesh=mesh, in_specs=in_specs, out_specs=out_specs, check_vma=False
    )
```

```python
from functools import partial

import jax
import jax.numpy as jnp
from jax import lax
from jax.experimental import pallas as pl
from jax.experimental.pallas import tpu as pltpu
from jax.sharding import PartitionSpec as P

HEAD_DIM = 64
STATE = 128
STRETCH = 256


KEEP_LOG = -0.35667494393873245
EPSILON = 1e-05
HIGHEST = lax.Precision.HIGHEST


def swap(value, axis):
    size = lax.axis_size(axis)
    return lax.ppermute(value, axis, [(i, size - 1 - i) for i in range(size)])


def earlier_than(count, backward):
    row = lax.broadcasted_iota(jnp.int32, (count, count), 0)
    column = lax.broadcasted_iota(jnp.int32, (count, count), 1)
    return jnp.where(backward, column > row, column < row)


def chain_weights(before, logs):
    steps = before.astype(jnp.float32)
    between = steps[:, None, :] * jnp.transpose(steps)[None, :, :]
    spans = jnp.sum(between[..., None] * logs[None, None], axis=2)
    return jnp.where(before[..., None], jnp.exp(spans), 0.0)


def block_terms(
    backward, step_bias, decay_log, break_marks, inner_vals, key_vals, query_vals, step_raw
):
    length = inner_vals.shape[0]
    blocks = length // STRETCH
    head_count = inner_vals.shape[1]
    groups = key_vals.shape[1]
    per_group = head_count // groups
    before = earlier_than(STRETCH, backward)
    row = lax.broadcasted_iota(jnp.int32, (STRETCH, STRETCH), 0)
    column = lax.broadcasted_iota(jnp.int32, (STRETCH, STRETCH), 1)
    causal = before | (row == column)
    step_size = jax.nn.softplus(step_raw + step_bias)
    log_rates = -jnp.exp(decay_log) * step_size + KEEP_LOG * break_marks[:, None]
    rate_rows = jnp.transpose(log_rates.reshape(blocks, STRETCH, head_count), (0, 2, 1))
    step_rows = jnp.transpose(step_size.reshape(blocks, STRETCH, head_count), (0, 2, 1))
    log_rows = jnp.einsum("chj,ij->chi", rate_rows, causal.astype(jnp.float32), precision=HIGHEST)
    ends = jnp.sum(rate_rows, axis=-1)
    end_rows = jnp.exp(ends[..., None] - log_rows) * step_rows
    log_decay = jnp.transpose(log_rows, (0, 2, 1))
    key_blocks = key_vals.reshape(blocks, STRETCH, groups, -1)
    query_blocks = query_vals.reshape(blocks, STRETCH, groups, -1)
    inner_blocks = inner_vals.reshape(blocks, STRETCH, groups, per_group, -1)
    scores = jnp.einsum(
        "cqgn,ckgn->cgqk", query_blocks, key_blocks, preferred_element_type=jnp.float32
    )
    decay_rows = log_rows.reshape(blocks, groups, per_group, STRETCH)
    step_heads = step_rows.reshape(blocks, groups, per_group, STRETCH)
    spread = decay_rows[..., :, None] - decay_rows[..., None, :]
    within = jnp.where(causal, jnp.exp(jnp.where(causal, spread, 0.0)), 0.0)
    mixing = (scores[:, :, None] * within * step_heads[..., None, :]).astype(jnp.bfloat16)
    local_out = jnp.einsum(
        "cghqk,ckghp->cqghp", mixing, inner_blocks, preferred_element_type=jnp.float32
    )
    to_end = jnp.transpose(end_rows, (0, 2, 1)).reshape(blocks, STRETCH, groups, per_group)
    weighted = (inner_blocks * to_end[..., None]).astype(jnp.bfloat16)
    block_states = jnp.einsum(
        "cqghp,cqgn->cghpn", weighted, key_blocks, preferred_element_type=jnp.float32
    )
    order = earlier_than(blocks, backward)
    head_shape = (groups, per_group)
    weights = chain_weights(order, ends).reshape((blocks, blocks) + head_shape)
    prior_state = jnp.stack(
        [
            sum(
                weights[c, k][..., None, None] * block_states[k] for k in range(blocks) if k != c
            )
            if blocks > 1
            else jnp.zeros_like(block_states[0])
            for c in range(blocks)
        ]
    )
    order_f = order.astype(jnp.float32)
    prior_logs = jnp.sum(order_f[:, :, None] * ends[None], axis=1)
    later_logs = jnp.sum(jnp.transpose(order_f)[:, :, None] * ends[None], axis=1)
    prior_decay = jnp.exp(prior_logs).reshape((blocks,) + head_shape)
    later_decay = jnp.exp(later_logs).reshape((blocks,) + head_shape)
    total_state = sum(later_decay[c][..., None, None] * block_states[c] for c in range(blocks))
    total_log = jnp.sum(ends, axis=0)
    return (local_out, prior_state, prior_decay, log_decay, total_log, total_state)


def finish_terms(
    skip_gain,
    local_out,
    prior_state,
    prior_decay,
    log_decay,
    query_vals,
    inner_vals,
    entering,
):
    blocks = log_decay.shape[0]
    groups = query_vals.shape[1]
    per_group = inner_vals.shape[1] // groups
    states = prior_state + prior_decay[..., None, None] * entering
    query_full = query_vals.reshape(blocks, STRETCH, groups, -1).astype(jnp.float32)
    carried = jnp.einsum("cqgn,cghpn->cqghp", query_full, states, precision=HIGHEST)
    growth = jnp.exp(log_decay).reshape(blocks, STRETCH, groups, per_group)
    inner_full = inner_vals.reshape(blocks, STRETCH, groups, per_group, -1).astype(jnp.float32)
    mixer_out = (
        local_out
        + growth[..., None] * carried
        + skip_gain.reshape(groups, per_group)[:, :, None] * inner_full
    )
    return mixer_out.reshape(blocks * STRETCH, groups, -1)


def gate_terms(mixer_out, gate_vals):
    product = mixer_out * jax.nn.silu(gate_vals.astype(jnp.float32))
    scaled = product * lax.rsqrt(jnp.mean(product * product, axis=-1, keepdims=True) + EPSILON)
    return scaled.astype(jnp.bfloat16)


def gather_kernel(peers, halves, *refs):
    shards, rows, fulls, all_rows = refs[:2], refs[2], refs[3:5], refs[5]
    local_sem, z_send, z_recv, y_send, y_recv, s_send, s_recv, o_send, o_recv, x_send, x_recv = refs[6:]
    part = lax.axis_index("parts")
    seq = lax.axis_index("seq")
    strand = lax.axis_index("strand")
    model = lax.axis_index("mp")
    twin = {"parts": 1 - part}
    mate = {"strand": 1 - strand}
    others = [lax.rem(seq + d, peers) for d in range(1, peers)]
    models = [lax.rem(model + d, halves) for d in range(1, halves)]

    def remote(source, target, send, receive, device):
        return pltpu.make_async_remote_copy(
            src_ref=source,
            dst_ref=target,
            send_sem=send,
            recv_sem=receive,
            device_id=device,
            device_id_type=pl.DeviceIdType.MESH,
        )

    barrier = pltpu.get_barrier_semaphore()
    targets = [{"seq": t} for t in others] + [{"mp": m} for m in models] + [twin, mate]
    for target in targets:
        pl.semaphore_signal(
            barrier, inc=1, device_id=target, device_id_type=pl.DeviceIdType.MESH
        )
    pl.semaphore_wait(barrier, len(targets))

    sends = []
    locals_ = []

    def go(copy):
        copy.start()
        sends.append(copy)

    for w in range(2):
        for d, t in enumerate(others):
            go(
                remote(
                    shards[w].at[part],
                    fulls[w].at[0, seq, part],
                    z_send.at[w, d],
                    z_recv.at[w, seq],
                    {"seq": t},
                )
            )
    for d, m in enumerate(models):
        go(remote(rows, all_rows.at[model], x_send.at[d], x_recv.at[model], {"mp": m}))
    for w in range(2):
        go(remote(shards[w], fulls[w].at[1, seq], o_send.at[w], o_recv.at[w], mate))
        copy = pltpu.make_async_copy(shards[w], fulls[w].at[0, seq], local_sem.at[w])
        copy.start()
        locals_.append(copy)
    copy = pltpu.make_async_copy(rows, all_rows.at[model], local_sem.at[2])
    copy.start()
    locals_.append(copy)

    for w in range(2):
        full = fulls[w]
        for d, t in enumerate(others):
            mine = full.at[0, t, part]
            remote(mine, mine, z_send.at[w, d], z_recv.at[w, t], {"seq": t}).wait_recv()
            go(remote(mine, mine, y_send.at[w, d], y_recv.at[w, t], twin))
            go(remote(mine, full.at[1, t, part], s_send.at[w, d, 0], s_recv.at[w, t, part], mate))
    for w in range(2):
        full = fulls[w]
        for d, t in enumerate(others):
            theirs = full.at[0, t, 1 - part]
            remote(theirs, theirs, y_send.at[w, d], y_recv.at[w, t], twin).wait_recv()
            go(
                remote(
                    theirs,
                    full.at[1, t, 1 - part],
                    s_send.at[w, d, 1],
                    s_recv.at[w, t, 1 - part],
                    mate,
                )
            )
    for w in range(2):
        full = fulls[w]
        own = full.at[1, seq]
        remote(own, own, o_send.at[w], o_recv.at[w], mate).wait_recv()
        for d, t in enumerate(others):
            for h in range(2):
                block = full.at[1, t, h]
                remote(block, block, s_send.at[w, d, h], s_recv.at[w, t, h], mate).wait_recv()
    for d, m in enumerate(models):
        block = all_rows.at[m]
        remote(block, block, x_send.at[d], x_recv.at[m], {"mp": m}).wait_recv()
    for copy in sends:
        copy.wait_send()
    for copy in locals_:
        copy.wait()


def gather_all(first, second, rows):
    peers, halves = (lax.axis_size("seq"), lax.axis_size("mp"))
    depth = first.shape[0] // 2
    shards = tuple(a.reshape(2, depth, -1) for a in (first, second))
    anywhere = pl.BlockSpec(memory_space=pl.ANY)
    dma = pltpu.SemaphoreType.DMA
    out = pl.pallas_call(
        partial(gather_kernel, peers, halves),
        out_shape=tuple(
            jax.ShapeDtypeStruct((2, peers) + a.shape, a.dtype) for a in shards
        )
        + (jax.ShapeDtypeStruct((halves,) + rows.shape, rows.dtype),),
        in_specs=[anywhere] * 3,
        out_specs=(anywhere,) * 3,
        scratch_shapes=[
            dma((3,)),
            dma((2, peers)),
            dma((2, peers)),
            dma((2, peers)),
            dma((2, peers)),
            dma((2, peers, 2)),
            dma((2, peers, 2)),
            dma((2,)),
            dma((2,)),
            dma((halves,)),
            dma((halves,)),
        ],
        compiler_params=pltpu.CompilerParams(collective_id=0, has_side_effects=True),
    )(*shards, rows)
    return (
        out[0].reshape(4 * peers * depth, -1),
        out[1].reshape(4 * peers * depth, -1),
        out[2],
    )


def exchange_kernel(peers, count, *refs):
    sources, targets = refs[:count], refs[count : 2 * count]
    local_sem, send_sem, recv_sem = refs[2 * count :]
    seq = lax.axis_index("seq")
    others = [lax.rem(seq + d, peers) for d in range(1, peers)]

    barrier = pltpu.get_barrier_semaphore()
    for t in others:
        pl.semaphore_signal(
            barrier, inc=1, device_id={"seq": t}, device_id_type=pl.DeviceIdType.MESH
        )
    pl.semaphore_wait(barrier, len(others))

    started = []
    for w in range(count):
        for d, t in enumerate(others):
            copy = pltpu.make_async_remote_copy(
                src_ref=sources[w].at[t],
                dst_ref=targets[w].at[seq],
                send_sem=send_sem.at[w, d],
                recv_sem=recv_sem.at[w, seq],
                device_id={"seq": t},
                device_id_type=pl.DeviceIdType.MESH,
            )
            copy.start()
            started.append(copy)
    own = [
        pltpu.make_async_copy(sources[w].at[seq], targets[w].at[seq], local_sem.at[w])
        for w in range(count)
    ]
    for copy in own:
        copy.start()
    for w in range(count):
        for d, t in enumerate(others):
            block = targets[w].at[t]
            pltpu.make_async_remote_copy(
                src_ref=block,
                dst_ref=block,
                send_sem=send_sem.at[w, d],
                recv_sem=recv_sem.at[w, t],
                device_id={"seq": t},
                device_id_type=pl.DeviceIdType.MESH,
            ).wait_recv()
    for copy in started:
        copy.wait_send()
    for copy in own:
        copy.wait()


def exchange(values):
    peers = lax.axis_size("seq")
    count = len(values)
    blocks = tuple(v.reshape(peers, v.shape[0] // peers, -1) for v in values)
    anywhere = pl.BlockSpec(memory_space=pl.ANY)
    dma = pltpu.SemaphoreType.DMA
    arrived = pl.pallas_call(
        partial(exchange_kernel, peers, count),
        out_shape=tuple(jax.ShapeDtypeStruct(v.shape, v.dtype) for v in blocks),
        in_specs=[anywhere] * count,
        out_specs=(anywhere,) * count,
        scratch_shapes=[dma((count,)), dma((count, peers)), dma((count, peers))],
        compiler_params=pltpu.CompilerParams(collective_id=1, has_side_effects=True),
    )(*blocks)
    return tuple(jnp.sum(v.astype(jnp.float32), axis=0) for v in arrived)


def core_sum(own, other):
    arrived = swap(other, "strand")
    return (own.astype(jnp.float32) + arrived.astype(jnp.float32)).astype(jnp.bfloat16)


def share_sum(own, other):
    return lax.psum_scatter(core_sum(own, other), "seq", scatter_dimension=0, tiled=True)


def on_device(
    hidden,
    breaks,
    cotangent,
    input_weight,
    gate_weight,
    key_weight,
    query_weight,
    step_weight,
    output_weight,
    step_bias,
    decay_log,
    skip_gain,
):
    strand = lax.axis_index("strand")
    backward = strand == 1
    seq_index = lax.axis_index("seq")
    length = hidden.shape[0]
    shard_rows = input_weight.shape[0]
    peers = lax.axis_size("seq")
    halves = lax.axis_size("mp")
    width = shard_rows * peers * 2
    half = shard_rows * peers
    part_width = hidden.shape[1]

    target = lax.broadcasted_iota(jnp.int32, (width, width), 1)
    source = lax.broadcasted_iota(jnp.int32, (width, width), 0)
    local = target % half
    side = jnp.where(target < half, strand, 1 - strand)
    feature = (local // shard_rows) * (2 * shard_rows) + side * shard_rows + local % shard_rows
    feature = jnp.where(backward, width - 1 - feature, feature)
    moves = (source == feature).astype(jnp.bfloat16)
    moves = lax.optimization_barrier(moves)

    key_width = key_weight.shape[1]
    inner_width = input_weight.shape[1]
    ahead = jnp.concatenate(
        (input_weight, gate_weight, key_weight, query_weight, step_weight), axis=1
    )
    ahead_full, out_full, everything = gather_all(
        ahead, output_weight, jnp.stack((hidden, cotangent))
    )

    def permuted(which):
        return sum(
            jnp.dot(
                everything[m, which],
                moves[m * part_width : (m + 1) * part_width],
                preferred_element_type=jnp.float32,
            )
            for m in range(halves)
        ).astype(jnp.bfloat16)

    inputs = permuted(0)
    grads_in = permuted(1)
    break_marks = lax.dynamic_slice_in_dim(breaks, seq_index * length, length).astype(jnp.float32)

    def project(start, size):
        return jnp.dot(
            inputs, ahead_full[:, start : start + size], preferred_element_type=jnp.float32
        )

    groups = key_width // STATE
    key_start = 2 * inner_width
    key_vals = project(key_start, key_width).astype(jnp.bfloat16).reshape(length, groups, STATE)
    query_vals = (
        project(key_start + key_width, key_width)
        .astype(jnp.bfloat16)
        .reshape(length, groups, STATE)
    )
    step_raw = project(key_start + 2 * key_width, step_weight.shape[1])
    inner_vals = project(0, inner_width).astype(jnp.bfloat16).reshape(length, -1, HEAD_DIM)
    gate_vals = project(inner_width, inner_width).astype(jnp.bfloat16).reshape(length, groups, -1)

    local_terms, local_pull = jax.vjp(
        partial(block_terms, backward, step_bias, decay_log, break_marks),
        inner_vals,
        key_vals,
        query_vals,
        step_raw,
    )
    total_log, total_state = local_terms[4:]
    head_shape = total_state.shape[:2]
    heads = total_log.shape[0]
    log_pieces = []
    rest = total_log
    for _ in range(3):
        piece = lax.reduce_precision(rest, 8, 7)
        log_pieces.append(piece)
        rest = rest - piece
    log_rows = jnp.pad(jnp.stack(log_pieces), ((0, 13), (0, STATE - heads)))
    sent = jnp.concatenate(
        (total_state.reshape(-1, STATE).astype(jnp.bfloat16), log_rows.astype(jnp.bfloat16))
    )
    arrived = lax.all_gather(sent, "seq")
    state_rows = heads * HEAD_DIM
    all_logs = jnp.sum(arrived[:, state_rows : state_rows + 3, :heads].astype(jnp.float32), axis=1)
    order = earlier_than(peers, backward)
    chain = chain_weights(order, all_logs)
    here = lax.dynamic_index_in_dim(chain, seq_index, 0, keepdims=False)
    there = lax.dynamic_index_in_dim(chain, seq_index, 1, keepdims=False)

    def chained(everything, weights):
        weights = weights.reshape((peers,) + head_shape)
        return sum(
            weights[k][..., None, None]
            * everything[k].reshape(total_state.shape).astype(jnp.float32)
            for k in range(peers)
        )

    entering = chained(arrived[:, :state_rows], here)
    mixer_out, finish_pull = jax.vjp(
        partial(finish_terms, skip_gain), *local_terms[:4], query_vals, inner_vals, entering
    )
    gated, gate_pull = jax.vjp(gate_terms, mixer_out, gate_vals)
    gated_flat = gated.reshape(length, -1)

    gated_back = jnp.dot(grads_in, out_full, preferred_element_type=jnp.float32).astype(jnp.bfloat16).reshape(gated.shape)
    mixer_back, gate_back = gate_pull(gated_back)
    finish_back = finish_pull(mixer_back)
    carried_back = chained(lax.all_gather(finish_back[6].astype(jnp.bfloat16), "seq"), there)

    contract_rows = (((1,), (1,)), ((), ()))
    head_terms = tuple(
        lax.dot_general(
            gated_flat, part, contract_rows, preferred_element_type=jnp.float32
        ).astype(jnp.bfloat16)
        for part in (out_full[:half], out_full[half:])
    )
    head_terms = jnp.stack(
        [
            sum(
                lax.dot_general(
                    head_terms[s],
                    moves[m * part_width : (m + 1) * part_width, s * half : (s + 1) * half],
                    contract_rows,
                    preferred_element_type=jnp.float32,
                )
                for s in range(2)
            ).astype(jnp.bfloat16)
            for m in range(halves)
        ]
    )
    reduced = lax.psum_scatter(head_terms, "mp", scatter_dimension=0)
    combined = (
        reduced.astype(jnp.float32) + swap(reduced, "strand").astype(jnp.float32)
    ).astype(jnp.bfloat16)

    contract = (((0,), (0,)), ((), ()))

    def grad_pair(left, right):
        return tuple(
            lax.dot_general(part, right, contract, preferred_element_type=jnp.float32).astype(
                jnp.bfloat16
            )
            for part in (left[:, :half], left[:, half:])
        )

    grad_output = share_sum(*grad_pair(grads_in, gated_flat)).astype(jnp.float32)
    grad_gate = share_sum(*grad_pair(inputs, gate_back.reshape(length, -1))).astype(jnp.float32)

    log_back = jnp.sum(carried_back * entering, axis=(-2, -1)).reshape(
        total_log.shape
    ) * jnp.exp(total_log)
    local_back = local_pull((*finish_back[:4], log_back, carried_back))
    inner_back = (local_back[0] + finish_back[5]).reshape(length, -1)
    key_back = local_back[1].reshape(length, -1)
    query_back = (local_back[2] + finish_back[4]).reshape(length, -1)
    step_back = local_back[3]

    input_terms = grad_pair(inputs, inner_back)
    small_terms = tuple(
        jnp.concatenate(
            (
                lax.dot_general(
                    part, key_back, contract, preferred_element_type=jnp.float32
                ).astype(jnp.bfloat16),
                lax.dot_general(
                    part, query_back, contract, preferred_element_type=jnp.float32
                ).astype(jnp.bfloat16),
                lax.dot_general(
                    part.astype(jnp.float32), step_back, contract, precision=HIGHEST
                ).astype(jnp.bfloat16),
            ),
            axis=1,
        )
        for part in (inputs[:, :half], inputs[:, half:])
    )
    grad_input, small_share = exchange((core_sum(*input_terms), core_sum(*small_terms)))
    return (
        combined,
        grad_input,
        grad_gate,
        small_share[:, :key_width],
        small_share[:, key_width : 2 * key_width],
        small_share[:, 2 * key_width :],
        grad_output,
    )


NN = (((1,), (0,)), ((), ()))
NT = (((1,), (1,)), ((), ()))
TN = (((0,), (0,)), ((), ()))
F32 = jnp.float32
BF16 = jnp.bfloat16
CHUNKS = 2


def mm(left, right, dims=NN, **options):
    return lax.dot_general(left, right, dims, preferred_element_type=F32, **options)


def iota(shape, axis):
    return lax.broadcasted_iota(jnp.int32, shape, axis)


def aligned(start, size, unit=None):
    return pl.ds(pl.multiple_of(start, unit or size), size)


def remote(source, target, send, receive, device):
    return pltpu.make_async_remote_copy(
        src_ref=source,
        dst_ref=target,
        send_sem=send,
        recv_sem=receive,
        device_id=device,
        device_id_type=pl.DeviceIdType.MESH,
    )


def mixer_kernel(peers, *refs):
    (
        hidden,
        cotangent,
        input_weight,
        key_weight,
        query_weight,
        gate_weight,
        output_weight,
        step_weight,
        marks_ref,
        bias_ref,
        decay_ref,
        gain_ref,
        combined,
        rg,
        rgs,
        u_ref,
        t_ref,
        w_ref,
        step_ref,
        steps,
        wt,
        seff,
        xbcz,
        dxbc,
        dz_ref,
        gated,
        y_ref,
        r_rows,
        dt_rows,
        k_rows,
        entering,
        state,
        p_ref,
        p_mate,
        acc,
        x_out,
        x_in,
        z_out,
        z_in,
        g_own,
        g_mine,
        g_mate,
        g_out,
        gs_own,
        gs_mine,
        gs_mate,
        gs_out,
        local_sem,
        z_send,
        z_recv,
        x_send,
        x_recv,
        m_send,
        m_recv,
        w_send,
        w_recv,
        s_send,
        s_recv,
        p_send,
        p_recv,
        px_send,
        px_recv,
        pz_send,
        pz_recv,
        g_send,
        g_recv,
        gz_send,
        gz_recv,
        gs_send,
        gs_recv,
        c_sem,
    ) = refs
    part = lax.axis_index("parts")
    seq = lax.axis_index("seq")
    strand = lax.axis_index("strand")
    model = lax.axis_index("mp")
    backward = strand == 1
    twin = {"parts": 1 - part}
    mate = {"strand": 1 - strand}
    side = {"mp": 1 - model}
    others = [lax.rem(seq + d, peers) for d in range(1, peers)]
    has_up, has_down = seq < peers - 1, seq > 0

    length, features = hidden.shape
    half = length // 2
    shard = step_weight.shape[1]
    thin = shard // 2
    shards = 2 * peers
    positions, width = u_ref.shape
    blocks = positions // STRETCH
    heads = bias_ref.shape[0] // peers
    inner = heads * HEAD_DIM
    narrow = inner + 2 * STATE
    per = [slice(h * HEAD_DIM, (h + 1) * HEAD_DIM) for h in range(heads)]
    sources = (hidden, cotangent)
    fulls = (u_ref, t_ref)

    def mirrored(i, count):
        return jnp.where(backward, count - 1 - i, i)

    barrier = pltpu.get_barrier_semaphore()
    targets = [{"seq": t} for t in others] + [twin, mate, side]
    for target in targets:
        pl.semaphore_signal(
            barrier, inc=1, device_id=target, device_id_type=pl.DeviceIdType.MESH
        )
    pl.semaphore_wait(barrier, len(targets))

    chunk = half // CHUNKS

    def piece(a, block, which, core, k):
        return fulls[a].at[
            aligned(block * length + core * half + k * chunk, chunk),
            aligned(which * features, features),
        ]

    def own(a, k):
        return sources[a].at[aligned(strand * half + k * chunk, chunk), :]

    def up(a, block, k, source):
        return remote(
            source,
            piece(a, block, model, strand, k),
            z_send.at[a, 0, block, k],
            z_recv.at[a, block, k],
            {"seq": jnp.minimum(seq + 1, peers - 1)},
        )

    def down(a, block, k, source):
        return remote(
            source,
            piece(a, block, model, strand, k),
            z_send.at[a, 1, block, k],
            z_recv.at[a, block, k],
            {"seq": jnp.maximum(seq - 1, 0)},
        )

    def across(a, block, k, source):
        return remote(
            source,
            piece(a, block, model, strand, k),
            x_send.at[a, block, k],
            x_recv.at[a, block, k],
            side,
        )

    def to_mate(a, block, which, k, core=strand):
        mine = piece(a, block, which, core, k)
        return remote(
            mine, mine, m_send.at[a, block, which, k], m_recv.at[a, block, which, k], mate
        )

    def wait_z(a, block, k):
        mine = piece(a, block, model, strand, k)
        remote(mine, mine, z_send.at[a, 0, block, k], z_recv.at[a, block, k], side).wait_recv()

    def wait_x(a, block, k):
        mine = piece(a, block, 1 - model, strand, k)
        remote(mine, mine, x_send.at[a, block, k], x_recv.at[a, block, k], side).wait_recv()

    def launch_up(a):
        def action():
            for k in range(CHUNKS):
                up(a, seq, k, own(a, k)).start()

        pl.when(has_up)(action)

    def launch_down(a):
        def action():
            for k in range(CHUNKS):
                down(a, seq, k, own(a, k)).start()

        pl.when(has_down)(action)

    def launch_across(a):
        for k in range(CHUNKS):
            across(a, seq, k, own(a, k)).start()

    def near(d, action):
        if d == 0:
            action(seq)
        else:
            pl.when(seq >= d)(lambda: action(seq - d))
            pl.when(seq + d < peers)(lambda: action(seq + d))

    def relay(a, d):
        def pass_on(block, k, more, onward):
            mine = piece(a, block, model, strand, k)
            wait_z(a, block, k)
            pl.when(more)(lambda: onward(a, block, k, mine).start())
            across(a, block, k, mine).start()
            to_mate(a, block, model, k).start()

        for k in range(CHUNKS):
            pl.when(seq >= d)(lambda: pass_on(seq - d, k, has_up, up))
            pl.when(seq + d < peers)(lambda: pass_on(seq + d, k, has_down, down))

    def from_side(a):
        def action(block):
            for k in range(CHUNKS):
                wait_x(a, block, k)
                to_mate(a, block, 1 - model, k).start()

        return action

    def all_here(a):
        for d in range(peers):

            def arrivals(block, d=d):
                for k in range(CHUNKS):
                    if d:
                        to_mate(a, block, model, k, 1 - strand).wait_recv()
                    to_mate(a, block, 1 - model, k, 1 - strand).wait_recv()

            near(d, arrivals)

    def all_sent(a):
        def sent_chunk(block, d, k):
            mine = piece(a, block, model, strand, k)
            across(a, block, k, mine).wait_send()
            if d:
                to_mate(a, block, model, k).wait_send()
            to_mate(a, block, 1 - model, k).wait_send()
            pl.when(jnp.logical_and(has_up, block <= seq))(
                lambda: up(a, block, k, mine).wait_send()
            )
            pl.when(jnp.logical_and(has_down, block >= seq))(
                lambda: down(a, block, k, mine).wait_send()
            )

        for d in range(peers):

            def sent(block, d=d):
                for k in range(CHUNKS):
                    sent_chunk(block, d, k)

            near(d, sent)

    def own_copy(a):
        target = fulls[a].at[
            aligned(seq * length, length), aligned(model * features, features)
        ]
        return pltpu.make_async_copy(sources[a], target, local_sem.at[a])

    weights = (input_weight, key_weight, query_weight, gate_weight, output_weight)
    starts = [0, inner, inner + STATE, narrow, narrow + inner, narrow + 2 * inner]

    def w_rows(block, core, which=None):
        first = (2 * block + core) * shard
        if which is None:
            return aligned(first, shard)
        return aligned(first + which * thin, thin)

    def w_sends(t):
        for weight, first, last in zip(weights, starts, starts[1:]):
            size = last - first
            yield remote(
                weight.at[aligned(part * thin, thin), aligned(t * size, size)],
                w_ref.at[w_rows(seq, strand, part), first:last],
                w_send.at[0, t],
                w_recv.at[0, seq],
                {"seq": t},
            )

    def s_sends(t):
        return remote(
            steps.at[t], step_ref.at[2 * seq + strand], s_send.at[0, t], s_recv.at[0, seq], {"seq": t}
        )

    def own_weights():
        for weight, first, last in zip(weights, starts, starts[1:]):
            size = last - first
            yield pltpu.make_async_copy(
                weight.at[:, aligned(seq * size, size)],
                w_ref.at[w_rows(seq, strand), first:last],
                local_sem.at[2],
            )

    def w_own_to_mate():
        mine = w_ref.at[w_rows(seq, strand), :]
        return remote(mine, mine, w_send.at[0, seq], w_recv.at[0, seq], mate)

    def s_own_to_mate():
        mine = step_ref.at[2 * seq + strand]
        return remote(mine, mine, s_send.at[0, seq], s_recv.at[0, seq], mate)

    def w_move(index, block, core, which, device):
        mine = w_ref.at[w_rows(block, core, which), :]
        return remote(mine, mine, w_send.at[index, block], w_recv.at[index, block], device)

    def s_move(index, block, core):
        mine = step_ref.at[2 * block + core]
        return remote(mine, mine, s_send.at[index, block], s_recv.at[index, block], mate)

    launch_up(0)
    launch_down(0)
    launch_across(0)
    launch_across(1)
    for t in others:
        for copy in w_sends(t):
            copy.start()
    for copy in own_weights():
        copy.start()
    for a in range(2):
        own_copy(a).start()
    pl.when(seq == 0)(lambda: launch_up(1))
    pl.when(seq == peers - 1)(lambda: launch_down(1))

    step_now = step_weight[...]
    for t in others + [seq]:
        taken = iota((16, heads * peers), 1) == iota((16, heads * peers), 0) + heads * t
        taken = jnp.logical_and(taken, iota((16, heads * peers), 0) < heads)
        turned = mm(jnp.where(taken, 1.0, 0.0).astype(BF16), step_now).astype(BF16)
        if t is seq:
            step_ref[2 * seq + strand] = turned
            s_own_to_mate().start()
        else:
            steps[t] = turned
            s_sends(t).start()
    mine = w_ref.at[w_rows(seq, strand), :]
    pltpu.make_async_copy(mine, mine, local_sem.at[2]).wait()
    w_own_to_mate().start()

    def weights_in():
        for t in others:
            w_move(0, t, strand, part, mate).wait_recv()
            w_move(1, t, strand, part, twin).start()
            w_move(2 + part, t, strand, part, mate).start()
            s_move(0, t, strand).wait_recv()
            s_move(1, t, strand).start()

    def weights_twin():
        for t in others:
            w_move(1, t, strand, 1 - part, twin).wait_recv()
            w_move(3 - part, t, strand, 1 - part, mate).start()

    for d in range(1, peers):
        relay(0, d)
        pl.when(seq == d)(lambda: launch_up(1))
        pl.when(peers - 1 - seq == d)(lambda: launch_down(1))
        if d == peers - 1:
            relay(1, 1)
        near(d - 1, from_side(0))
        if d == min(2, peers - 1):
            weights_in()
    weights_twin()
    near(peers - 1, from_side(0))
    near(0, from_side(1))

    for t in others:
        for which in range(2):
            w_move(2 + which, t, 1 - strand, which, mate).wait_recv()
        s_move(1, t, 1 - strand).wait_recv()
    theirs = w_ref.at[w_rows(seq, 1 - strand), :]
    remote(theirs, theirs, w_send.at[0, seq], w_recv.at[0, seq], mate).wait_recv()
    s_move(0, seq, 1 - strand).wait_recv()

    row = iota((shard, shard), 0)
    column = iota((shard, shard), 1)
    other = jnp.where(backward, shard - 1 - column, column)
    moves = jnp.where(row == other, 1.0, 0.0).astype(BF16)
    for b in range(shards):
        source = mirrored(b, shards)
        wt[:, b * shard : (b + 1) * shard] = mm(
            w_ref[aligned(source * shard, shard), :], moves, TN
        ).astype(BF16)
        seff[:, b * shard : (b + 1) * shard] = mm(step_ref[source], moves).astype(BF16)

    lead = iota((STRETCH, STRETCH), 0) - iota((STRETCH, STRETCH), 1)
    lead = jnp.where(backward, -lead, lead)
    causal = lead >= 0
    sums_to = (lead <= 0).astype(F32)
    sums_from = (lead >= 0).astype(F32)
    sums_before = (lead < 0).astype(F32)
    bias = jnp.zeros((8, STRETCH), F32)
    rates = jnp.zeros((8, STRETCH), F32)
    for h in range(heads):
        at_head = iota((8, STRETCH), 0) == h
        bias = jnp.where(at_head, bias_ref[seq * heads + h], bias)
        rates = jnp.where(at_head, decay_ref[seq * heads + h], rates)
    rates = -jnp.exp(rates)
    filler = jnp.zeros((128 - 8, STRETCH), F32)
    gains = [gain_ref[seq * heads + h] for h in range(heads)]

    def stacked(parts):
        return jnp.concatenate(parts, axis=0)

    def row(value, h):
        return value[h : h + 1, :]

    def decay_of(cols, k, h):
        return jnp.exp(jnp.where(causal, cols[:, h : h + 1] - row(k, h), -1e30))

    all_here(0)
    for a in range(2):
        own_copy(a).wait()
    state[...] = jnp.zeros_like(state)

    def p_to_mate(t):
        return remote(
            p_ref.at[aligned(t * length + (1 - strand) * half, half), :],
            p_mate.at[t],
            p_send.at[t],
            p_recv.at[t],
            mate,
        )

    inside, outside = range(1, peers - 1), (0, peers - 1)

    def turn(j):
        return lax.rem(seq + 1 + j, peers)

    def p_across(t):
        return remote(x_out.at[t], x_in.at[t], px_send.at[t], px_recv.at[t], side)

    def p_along(t):
        return remote(z_out.at[t], z_in.at[seq], pz_send.at[t], pz_recv.at[seq], {"seq": t})

    def add_core(t):
        p_to_mate(t).wait_recv()
        rows = aligned(t * length + strand * half, half)
        there = aligned((1 - model) * features, features)
        here = aligned(model * features, features)
        x_out[t] = (p_ref[rows, there].astype(F32) + p_mate[t, :, there].astype(F32)).astype(BF16)
        p_across(t).start()
        acc[t] = p_ref[rows, here].astype(F32) + p_mate[t, :, here].astype(F32)

    def add_side(t):
        p_across(t).wait_recv()
        total = acc[t] + x_in[t].astype(F32)
        acc[t] = total

        def send():
            z_out[t] = total.astype(BF16)
            p_along(t).start()

        pl.when(t != seq)(send)

    def forward(c, carry):
        for d in range(1, peers - 1):
            pl.when(c == 3 * d - 3)(lambda d=d: relay(1, d + 1))
            pl.when(c == 3 * d - 1)(lambda d=d: near(d, from_side(1)))
        blk = mirrored(c, blocks)
        at = aligned(blk * STRETCH, STRETCH)
        lanes = aligned(blk * STRETCH, STRETCH)
        u = u_ref[at, :]
        projected = mm(wt[: narrow + inner, :], u, NT).astype(BF16)
        xbcz[:, lanes] = projected
        x = projected[:inner]
        b = projected[inner : inner + STATE]
        q = projected[inner + STATE : narrow]
        z = projected[narrow:].astype(F32)
        r = mm(seff[...], u, NT)[:8] + bias
        dt = jnp.maximum(r, 0.0) + jnp.log1p(jnp.exp(-jnp.abs(r)))
        marks = jnp.concatenate(
            [marks_ref[pl.ds(2 * blk + i, 1), :] for i in range(2)], axis=1
        ).astype(F32)
        a = rates * dt + KEEP_LOG * marks
        k = mm(a, sums_to, precision=HIGHEST)
        end = jnp.sum(a, axis=1, keepdims=True)
        r_rows[blk] = r
        dt_rows[blk] = dt
        k_rows[blk] = stacked((k, jnp.broadcast_to(end, k.shape)))
        cols = jnp.transpose(stacked((k, filler)))
        scores = mm(q, b, TN)
        grow = jnp.exp(k)
        weight = jnp.exp(end - k) * dt
        keep_all = jnp.exp(end)
        before = state[...]
        entering[blk] = before
        carried = mm(before.astype(BF16), q)
        xf = x.astype(F32)
        ys, es, kept = [], [], []
        for h in range(heads):
            mixing = (scores * decay_of(cols, k, h) * row(dt, h)).astype(BF16)
            y_h = mm(x[per[h]], mixing, NT)
            ys.append(y_h + row(grow, h) * carried[per[h]] + gains[h] * xf[per[h]])
            es.append((row(weight, h) * xf[per[h]]).astype(BF16))
            kept.append(row(keep_all, h) * before[per[h]])
        state[...] = stacked(kept) + mm(stacked(es), b, NT)
        y = stacked(ys)
        y_ref[:, lanes] = y

        v = y * (z / (1.0 + jnp.exp(-z)))
        scale = lax.rsqrt(jnp.mean(v * v, axis=0, keepdims=True) + EPSILON)
        g = (v * scale).astype(BF16)
        gated[:, lanes] = g
        p_ref[at, :] = mm(g, wt[narrow + inner :, :], TN).astype(BF16)
        pl.when(lax.rem(c, 2) == 1)(lambda: p_to_mate(blk // 2).start())
        for i, t in enumerate(inside):
            pl.when(c == blocks - 2 + i)(lambda t=t: add_core(t))
        return carry

    lax.fori_loop(0, blocks, forward, 0)

    for t in outside:
        add_core(t)
    near(peers - 1, from_side(1))

    all_here(1)

    def gate_back(c, carry):
        at = aligned(c * STRETCH, STRETCH)
        z = xbcz[narrow:, at].astype(F32)
        y = y_ref[:, at]
        sig = 1.0 / (1.0 + jnp.exp(-z))
        silu = z * sig
        v = y * silu
        scale = lax.rsqrt(jnp.mean(v * v, axis=0, keepdims=True) + EPSILON)
        dg = mm(wt[narrow + inner :, :], t_ref[at, :], NT).astype(BF16).astype(F32)
        along = jnp.mean(dg * v, axis=0, keepdims=True)
        dv = scale * (dg - v * (scale * scale * along))
        y_ref[:, at] = dv * silu
        dz_ref[:, at] = (dv * y * (sig * (1.0 + z * (1.0 - sig)))).astype(BF16)
        return carry

    lax.fori_loop(0, blocks, gate_back, 0)

    def g_to_mate(part_of, t):
        return remote(
            g_own.at[part_of, t],
            g_mate.at[part_of, t],
            g_send.at[part_of, t],
            g_recv.at[part_of, t],
            mate,
        )

    def g_along(part_of, t):
        return remote(
            g_out.at[part_of, t],
            rg.at[part_of, seq],
            gz_send.at[part_of, t],
            gz_recv.at[part_of, seq],
            {"seq": t},
        )

    def gs_to_mate(t):
        return remote(gs_own.at[t], gs_mate.at[t], gs_send.at[0, t], gs_recv.at[0, t], mate)

    def gs_along(t):
        return remote(gs_out.at[t], rgs.at[seq], gs_send.at[1, t], gs_recv.at[1, seq], {"seq": t})

    def columns_at(t):
        return aligned(mirrored(t, peers) * 2 * shard, 2 * shard)

    def early_terms(t):
        at = columns_at(t)
        return stacked((mm(dz_ref[...], u_ref[:, at]), mm(gated[...], t_ref[:, at]))).astype(BF16)

    def late_terms(t):
        found = mm(dxbc[...], u_ref[:, columns_at(t)])
        steps_found = found[narrow : narrow + 8] + found[narrow + 8 :]
        steps_found = stacked((steps_found, jnp.zeros_like(steps_found))).astype(BF16)
        gs_own[t] = mm(steps_found[:, shard:], moves).astype(BF16)
        gs_mine[t] = mm(steps_found[:, :shard], moves)
        gs_to_mate(t).start()
        return found[:narrow].astype(BF16)

    def weigh(part_of, terms):
        def first(j, carry):
            t = turn(j)
            found = terms(t)
            g_own[part_of, t] = mm(moves, found[:, shard:], NT).astype(BF16)
            g_to_mate(part_of, t).start()
            g_mine[t] = mm(moves, found[:, :shard], NT)
            return carry

        def second(j, carry):
            t = turn(j)
            g_to_mate(part_of, t).wait_recv()
            total = (g_mine[t] + g_mate[part_of, t].astype(F32)).astype(BF16)
            if part_of:
                gs_to_mate(t).wait_recv()
                steps_total = (gs_mine[t] + gs_mate[t].astype(F32)).astype(BF16)

            def send():
                g_out[part_of, t] = total
                g_along(part_of, t).start()
                if part_of:
                    gs_out[t] = steps_total
                    gs_along(t).start()

            def keep():
                rg[part_of, t] = total
                if part_of:
                    rgs[t] = steps_total

            pl.when(j < peers - 1)(send)
            pl.when(j == peers - 1)(keep)
            return carry

        lax.fori_loop(0, peers, first, 0)
        lax.fori_loop(0, peers, second, 0)

    state[...] = jnp.zeros_like(state)

    weigh(0, early_terms)
    sides = (*inside, *outside)
    add_side(sides[0])

    def backwards(c, carry):
        for i, t in enumerate(sides[1:]):
            pl.when(c == 3 * i)(lambda t=t: add_side(t))
        blk = mirrored(blocks - 1 - c, blocks)
        at = aligned(blk * STRETCH, STRETCH)
        x = xbcz[:inner, at]
        b = xbcz[inner : inner + STATE, at]
        q = xbcz[inner + STATE : narrow, at]
        xf = x.astype(F32)
        dy = y_ref[:, at]
        dyb = dy.astype(BF16)
        dt = dt_rows[blk]
        k = k_rows[blk, :8]
        end = k_rows[blk, 8:]
        cols = jnp.transpose(stacked((k, filler)))
        before = entering[blk]
        leaving = state[...]
        before_b = before.astype(BF16)
        leaving_b = leaving.astype(BF16)
        before_t = jnp.transpose(before).astype(BF16)
        leaving_t = jnp.transpose(leaving).astype(BF16)
        keep = jnp.exp(end - k)
        weight = keep * dt
        grow = jnp.exp(k)
        keep_all = jnp.exp(end[:, :STATE])

        de = mm(leaving_b, b)
        carried = mm(before_b, q)
        scores = mm(q, b, TN)
        dscores = jnp.zeros((STRETCH, STRETCH), F32)
        row_sums = jnp.zeros((STRETCH, 128), F32)
        lane = iota((STRETCH, 128), 1)
        none = jnp.zeros((8 - heads, STRETCH), F32)
        dxs, es, growns, kept, ddts, dks, columns, totals = [], [], [], [], [], [], [], []
        for h in range(heads):
            x_h, de_h, dy_h = xf[per[h]], de[per[h]], dy[per[h]]
            ddts.append(jnp.sum(de_h * x_h, axis=0, keepdims=True) * row(keep, h))
            es.append((x_h * row(weight, h)).astype(BF16))
            grown = row(grow, h) * dy_h
            growns.append(grown.astype(BF16))
            dks.append(jnp.sum(grown * carried[per[h]], axis=0, keepdims=True))
            held = row(keep_all, h) * leaving[per[h]]
            kept.append(held)
            totals.append(jnp.sum(before[per[h]] * held, axis=0, keepdims=True))

            decay = decay_of(cols, k, h)
            dmix = mm(dyb[per[h]], x[per[h]], TN) * decay
            mixing = (scores * decay * row(dt, h)).astype(BF16)
            dx_h = mm(dyb[per[h]], mixing)
            dxs.append((dx_h + de_h * row(weight, h) + gains[h] * dy_h).astype(BF16))
            scaled = dmix * row(dt, h)
            dscores = dscores + scaled
            columns.append(jnp.sum(dmix * scores, axis=0, keepdims=True))
            summed = jnp.sum(scaled * scores, axis=1, keepdims=True)
            row_sums = jnp.where(lane == h, summed, row_sums)
        grown = stacked(growns)
        dscores_b = dscores.astype(BF16)
        dq = mm(before_t, grown) + mm(b, dscores_b, NT)
        db = mm(leaving_t, stacked(es)) + mm(q, dscores_b)
        state[...] = stacked(kept) + mm(grown, q, NT)
        dxbc[:inner, at] = stacked(dxs)
        dxbc[inner : inner + STATE, at] = db.astype(BF16)
        dxbc[inner + STATE : narrow, at] = dq.astype(BF16)

        ddt = stacked(ddts + [none])
        columns = stacked(columns + [none])
        total = jnp.sum(stacked(totals + [none[:, :STATE]]), axis=1, keepdims=True)
        dk = stacked(dks + [none]) + jnp.transpose(row_sums)[:8] - dt * columns
        da = mm(dk, sums_from, precision=HIGHEST)
        da = da + mm(dt * ddt, sums_before, precision=HIGHEST) + total
        ddt = ddt + columns + rates * da
        dr = ddt / (1.0 + jnp.exp(-r_rows[blk]))
        high = dr.astype(BF16).astype(F32)
        dxbc[narrow:, at] = stacked((high, dr - high)).astype(BF16)
        return carry

    lax.fori_loop(0, blocks, backwards, 0)

    weigh(1, late_terms)

    total = acc[seq]
    for t in others:
        remote(z_in.at[t], z_in.at[t], pz_send.at[t], pz_recv.at[t], {"seq": t}).wait_recv()
        total = total + z_in[t].astype(F32)
    mine = aligned(strand * half, half)
    combined[mine, :] = total.astype(BF16)
    rows = combined.at[mine, :]
    last = remote(rows, rows, c_sem.at[0], c_sem.at[1], mate)
    last.start()

    for t in others:
        for i in range(2):
            remote(
                rg.at[i, t], rg.at[i, t], gz_send.at[i, t], gz_recv.at[i, t], {"seq": t}
            ).wait_recv()
        remote(
            rgs.at[t], rgs.at[t], gs_send.at[1, t], gs_recv.at[1, t], {"seq": t}
        ).wait_recv()
    theirs = combined.at[aligned((1 - strand) * half, half), :]
    remote(theirs, theirs, c_sem.at[0], c_sem.at[1], mate).wait_recv()
    last.wait_send()
    for a in range(2):
        all_sent(a)
    for t in others:
        w_move(0, t, strand, part, mate).wait_send()
        w_move(1, t, strand, part, twin).wait_send()
        w_move(2 + part, t, strand, part, mate).wait_send()
        w_move(3 - part, t, strand, 1 - part, mate).wait_send()
        s_sends(t).wait_send()
        s_move(1, t, strand).wait_send()
        p_along(t).wait_send()
        gs_along(t).wait_send()
        for i in range(2):
            g_along(i, t).wait_send()
    w_own_to_mate().wait_send()
    s_own_to_mate().wait_send()
    for t in others + [seq]:
        p_to_mate(t).wait_send()
        p_across(t).wait_send()
        gs_to_mate(t).wait_send()
        for i in range(2):
            g_to_mate(i, t).wait_send()


def finish_kernel(
    heads, combined, rg, rgs, out, g_in, g_gate, g_key, g_query, g_step, g_out, here, here_s, sems
):
    peers = rg.shape[1]
    inner = g_in.shape[1] // peers
    copies = [pltpu.make_async_copy(rgs, here_s, sems.at[0])]
    for s in range(peers):
        copies.append(pltpu.make_async_copy(rg.at[:, s], here.at[:, s], sems.at[2 + s]))
    last = pltpu.make_async_copy(combined, out, sems.at[1])
    for copy in copies + [last]:
        copy.start()
    copies[0].wait()
    for s in range(peers):
        g_step[heads * s : heads * (s + 1), :] = here_s[s].astype(F32)[:heads]
    for s in range(peers):
        copies[1 + s].wait()
        early, late = here[0, s].astype(F32), here[1, s].astype(F32)
        wide = slice(s * inner, (s + 1) * inner)
        small = slice(s * STATE, (s + 1) * STATE)
        g_gate[:, wide] = early[:, :inner]
        g_out[:, wide] = early[:, inner:]
        g_in[:, wide] = late[:, :inner]
        g_key[:, small] = late[:, inner : inner + STATE]
        g_query[:, small] = late[:, inner + STATE :]
    last.wait()


def by_group(
    hidden,
    breaks,
    cotangent,
    input_weight,
    gate_weight,
    key_weight,
    query_weight,
    step_weight,
    output_weight,
    step_bias,
    decay_log,
    skip_gain,
):
    peers, models = lax.axis_size("seq"), lax.axis_size("mp")
    length, features = hidden.shape
    half = length // 2
    shard = input_weight.shape[0]
    positions, width = length * peers, features * models
    blocks = positions // STRETCH
    heads = step_bias.shape[0] // peers
    inner = heads * HEAD_DIM
    narrow = inner + 2 * STATE
    columns = narrow + 2 * inner
    dma = pltpu.SemaphoreType.DMA
    anywhere = pl.BlockSpec(memory_space=pl.ANY)
    vmem = pl.BlockSpec(memory_space=pltpu.VMEM)
    smem = pl.BlockSpec(memory_space=pltpu.SMEM)
    strips = pltpu.VMEM((2, peers, shard, 2 * inner), BF16)
    steps = pltpu.VMEM((peers, 16, shard), BF16)
    rows8 = pltpu.VMEM((blocks, 8, STRETCH), F32)
    halves = pltpu.VMEM((peers, half, features), BF16)
    combined, rg, rgs = pl.pallas_call(
        partial(mixer_kernel, peers),
        out_shape=(
            jax.ShapeDtypeStruct((length, features), BF16),
            jax.ShapeDtypeStruct((2, peers, shard, 2 * inner), BF16),
            jax.ShapeDtypeStruct((peers, 16, shard), BF16),
        ),
        in_specs=[anywhere] * 7 + [vmem] * 2 + [smem] * 3,
        out_specs=(vmem,) * 3,
        scratch_shapes=[
            pltpu.VMEM((positions, width), BF16),
            pltpu.VMEM((positions, width), BF16),
            pltpu.VMEM((width, columns), BF16),
            pltpu.VMEM((2 * peers, 16, shard), BF16),
            steps,
            pltpu.VMEM((columns, width), BF16),
            pltpu.VMEM((16, width), BF16),
            pltpu.VMEM((narrow + inner, positions), BF16),
            pltpu.VMEM((narrow + 16, positions), BF16),
            pltpu.VMEM((inner, positions), BF16),
            pltpu.VMEM((inner, positions), BF16),
            pltpu.VMEM((inner, positions), F32),
            rows8,
            rows8,
            pltpu.VMEM((blocks, 16, STRETCH), F32),
            pltpu.VMEM((blocks, inner, STATE), F32),
            pltpu.VMEM((inner, STATE), F32),
            pltpu.VMEM((positions, width), BF16),
            pltpu.VMEM((peers, half, width), BF16),
            pltpu.VMEM((peers, half, features), F32),
            halves,
            halves,
            halves,
            halves,
            strips,
            pltpu.VMEM((peers, shard, narrow), F32),
            strips,
            strips,
            steps,
            pltpu.VMEM((peers, 16, shard), F32),
            steps,
            steps,
            dma((3,)),
            dma((2, 2, peers, CHUNKS)),
            dma((2, peers, CHUNKS)),
            dma((2, peers, CHUNKS)),
            dma((2, peers, CHUNKS)),
            dma((2, peers, 2, CHUNKS)),
            dma((2, peers, 2, CHUNKS)),
            dma((4, peers)),
            dma((4, peers)),
            dma((2, peers)),
            dma((2, peers)),
            dma((peers,)),
            dma((peers,)),
            dma((peers,)),
            dma((peers,)),
            dma((peers,)),
            dma((peers,)),
            dma((2, peers)),
            dma((2, peers)),
            dma((2, peers)),
            dma((2, peers)),
            dma((2, peers)),
            dma((2, peers)),
            dma((2,)),
        ],
        compiler_params=pltpu.CompilerParams(
            collective_id=2, has_side_effects=True, vmem_limit_bytes=60 * 1024 * 1024
        ),
    )(
        hidden,
        cotangent,
        input_weight,
        key_weight,
        query_weight,
        gate_weight,
        output_weight,
        jnp.transpose(step_weight),
        breaks.reshape(-1, 128),
        step_bias,
        decay_log,
        skip_gain,
    )

    wide = jax.ShapeDtypeStruct((shard, peers * inner), F32)
    small = jax.ShapeDtypeStruct((shard, peers * STATE), F32)
    out, g_in, g_gate, g_key, g_query, g_step, g_out = pl.pallas_call(
        partial(finish_kernel, heads),
        out_shape=(
            jax.ShapeDtypeStruct(combined.shape, BF16),
            wide,
            wide,
            small,
            small,
            jax.ShapeDtypeStruct((peers * heads, shard), F32),
            wide,
        ),
        in_specs=[anywhere] * 3,
        out_specs=(vmem,) * 7,
        scratch_shapes=[
            pltpu.VMEM(rg.shape, BF16),
            pltpu.VMEM(rgs.shape, BF16),
            dma((2 + peers,)),
        ],
        compiler_params=pltpu.CompilerParams(vmem_limit_bytes=60 * 1024 * 1024),
    )(combined, rg, rgs)
    return out, g_in, g_gate, g_key, g_query, jnp.transpose(g_step), g_out


def solution(mesh):
    in_specs = (
        P(("parts", "seq"), "mp"),
        P("parts"),
        P(("parts", "seq"), "mp"),
        P(("seq", "strand"), "mp"),
        P(("seq", "strand"), "mp"),
        P(("seq", "strand"), "mp"),
        P(("seq", "strand"), "mp"),
        P(("seq", "strand"), "mp"),
        P(("seq", "strand"), "mp"),
        P("mp"),
        P("mp"),
        P("mp"),
    )
    out_specs = (
        P(("parts", "seq"), "mp"),
        P(("parts", "seq", "strand"), "mp"),
        P(("parts", "seq", "strand"), "mp"),
        P(("parts", "seq", "strand"), "mp"),
        P(("parts", "seq", "strand"), "mp"),
        P(("parts", "seq", "strand"), "mp"),
        P(("parts", "seq", "strand"), "mp"),
    )
    peers = mesh.shape["seq"]

    def each(*args):
        groups = args[5].shape[1] // STATE
        heads = args[9].shape[0]
        fits = peers == groups and heads == 4 * groups and mesh.shape["mp"] == 2
        return (by_group if fits else on_device)(*args)

    return jax.shard_map(
        each, mesh=mesh, in_specs=in_specs, out_specs=out_specs, check_vma=False
    )
```

```python
from functools import partial

import jax
import jax.numpy as jnp
from jax import lax
from jax.experimental import pallas as pl
from jax.experimental.pallas import tpu as pltpu
from jax.sharding import PartitionSpec as P

HEAD_DIM = 64
STATE = 128
STRETCH = 256


KEEP_LOG = -0.35667494393873245
EPSILON = 1e-05
HIGHEST = lax.Precision.HIGHEST


def swap(value, axis):
    size = lax.axis_size(axis)
    return lax.ppermute(value, axis, [(i, size - 1 - i) for i in range(size)])


def earlier_than(count, backward):
    row = lax.broadcasted_iota(jnp.int32, (count, count), 0)
    column = lax.broadcasted_iota(jnp.int32, (count, count), 1)
    return jnp.where(backward, column > row, column < row)


def chain_weights(before, logs):
    steps = before.astype(jnp.float32)
    between = steps[:, None, :] * jnp.transpose(steps)[None, :, :]
    spans = jnp.sum(between[..., None] * logs[None, None], axis=2)
    return jnp.where(before[..., None], jnp.exp(spans), 0.0)


def block_terms(
    backward, step_bias, decay_log, break_marks, inner_vals, key_vals, query_vals, step_raw
):
    length = inner_vals.shape[0]
    blocks = length // STRETCH
    head_count = inner_vals.shape[1]
    groups = key_vals.shape[1]
    per_group = head_count // groups
    before = earlier_than(STRETCH, backward)
    row = lax.broadcasted_iota(jnp.int32, (STRETCH, STRETCH), 0)
    column = lax.broadcasted_iota(jnp.int32, (STRETCH, STRETCH), 1)
    causal = before | (row == column)
    step_size = jax.nn.softplus(step_raw + step_bias)
    log_rates = -jnp.exp(decay_log) * step_size + KEEP_LOG * break_marks[:, None]
    rate_rows = jnp.transpose(log_rates.reshape(blocks, STRETCH, head_count), (0, 2, 1))
    step_rows = jnp.transpose(step_size.reshape(blocks, STRETCH, head_count), (0, 2, 1))
    log_rows = jnp.einsum("chj,ij->chi", rate_rows, causal.astype(jnp.float32), precision=HIGHEST)
    ends = jnp.sum(rate_rows, axis=-1)
    end_rows = jnp.exp(ends[..., None] - log_rows) * step_rows
    log_decay = jnp.transpose(log_rows, (0, 2, 1))
    key_blocks = key_vals.reshape(blocks, STRETCH, groups, -1)
    query_blocks = query_vals.reshape(blocks, STRETCH, groups, -1)
    inner_blocks = inner_vals.reshape(blocks, STRETCH, groups, per_group, -1)
    scores = jnp.einsum(
        "cqgn,ckgn->cgqk", query_blocks, key_blocks, preferred_element_type=jnp.float32
    )
    decay_rows = log_rows.reshape(blocks, groups, per_group, STRETCH)
    step_heads = step_rows.reshape(blocks, groups, per_group, STRETCH)
    spread = decay_rows[..., :, None] - decay_rows[..., None, :]
    within = jnp.where(causal, jnp.exp(jnp.where(causal, spread, 0.0)), 0.0)
    mixing = (scores[:, :, None] * within * step_heads[..., None, :]).astype(jnp.bfloat16)
    local_out = jnp.einsum(
        "cghqk,ckghp->cqghp", mixing, inner_blocks, preferred_element_type=jnp.float32
    )
    to_end = jnp.transpose(end_rows, (0, 2, 1)).reshape(blocks, STRETCH, groups, per_group)
    weighted = (inner_blocks * to_end[..., None]).astype(jnp.bfloat16)
    block_states = jnp.einsum(
        "cqghp,cqgn->cghpn", weighted, key_blocks, preferred_element_type=jnp.float32
    )
    order = earlier_than(blocks, backward)
    head_shape = (groups, per_group)
    weights = chain_weights(order, ends).reshape((blocks, blocks) + head_shape)
    prior_state = jnp.stack(
        [
            sum(
                weights[c, k][..., None, None] * block_states[k] for k in range(blocks) if k != c
            )
            if blocks > 1
            else jnp.zeros_like(block_states[0])
            for c in range(blocks)
        ]
    )
    order_f = order.astype(jnp.float32)
    prior_logs = jnp.sum(order_f[:, :, None] * ends[None], axis=1)
    later_logs = jnp.sum(jnp.transpose(order_f)[:, :, None] * ends[None], axis=1)
    prior_decay = jnp.exp(prior_logs).reshape((blocks,) + head_shape)
    later_decay = jnp.exp(later_logs).reshape((blocks,) + head_shape)
    total_state = sum(later_decay[c][..., None, None] * block_states[c] for c in range(blocks))
    total_log = jnp.sum(ends, axis=0)
    return (local_out, prior_state, prior_decay, log_decay, total_log, total_state)


def finish_terms(
    skip_gain,
    local_out,
    prior_state,
    prior_decay,
    log_decay,
    query_vals,
    inner_vals,
    entering,
):
    blocks = log_decay.shape[0]
    groups = query_vals.shape[1]
    per_group = inner_vals.shape[1] // groups
    states = prior_state + prior_decay[..., None, None] * entering
    query_full = query_vals.reshape(blocks, STRETCH, groups, -1).astype(jnp.float32)
    carried = jnp.einsum("cqgn,cghpn->cqghp", query_full, states, precision=HIGHEST)
    growth = jnp.exp(log_decay).reshape(blocks, STRETCH, groups, per_group)
    inner_full = inner_vals.reshape(blocks, STRETCH, groups, per_group, -1).astype(jnp.float32)
    mixer_out = (
        local_out
        + growth[..., None] * carried
        + skip_gain.reshape(groups, per_group)[:, :, None] * inner_full
    )
    return mixer_out.reshape(blocks * STRETCH, groups, -1)


def gate_terms(mixer_out, gate_vals):
    product = mixer_out * jax.nn.silu(gate_vals.astype(jnp.float32))
    scaled = product * lax.rsqrt(jnp.mean(product * product, axis=-1, keepdims=True) + EPSILON)
    return scaled.astype(jnp.bfloat16)


def gather_kernel(peers, halves, *refs):
    shards, rows, fulls, all_rows = refs[:2], refs[2], refs[3:5], refs[5]
    local_sem, z_send, z_recv, y_send, y_recv, s_send, s_recv, o_send, o_recv, x_send, x_recv = refs[6:]
    part = lax.axis_index("parts")
    seq = lax.axis_index("seq")
    strand = lax.axis_index("strand")
    model = lax.axis_index("mp")
    twin = {"parts": 1 - part}
    mate = {"strand": 1 - strand}
    others = [lax.rem(seq + d, peers) for d in range(1, peers)]
    models = [lax.rem(model + d, halves) for d in range(1, halves)]

    def remote(source, target, send, receive, device):
        return pltpu.make_async_remote_copy(
            src_ref=source,
            dst_ref=target,
            send_sem=send,
            recv_sem=receive,
            device_id=device,
            device_id_type=pl.DeviceIdType.MESH,
        )

    barrier = pltpu.get_barrier_semaphore()
    targets = [{"seq": t} for t in others] + [{"mp": m} for m in models] + [twin, mate]
    for target in targets:
        pl.semaphore_signal(
            barrier, inc=1, device_id=target, device_id_type=pl.DeviceIdType.MESH
        )
    pl.semaphore_wait(barrier, len(targets))

    sends = []
    locals_ = []

    def go(copy):
        copy.start()
        sends.append(copy)

    for w in range(2):
        for d, t in enumerate(others):
            go(
                remote(
                    shards[w].at[part],
                    fulls[w].at[0, seq, part],
                    z_send.at[w, d],
                    z_recv.at[w, seq],
                    {"seq": t},
                )
            )
    for d, m in enumerate(models):
        go(remote(rows, all_rows.at[model], x_send.at[d], x_recv.at[model], {"mp": m}))
    for w in range(2):
        go(remote(shards[w], fulls[w].at[1, seq], o_send.at[w], o_recv.at[w], mate))
        copy = pltpu.make_async_copy(shards[w], fulls[w].at[0, seq], local_sem.at[w])
        copy.start()
        locals_.append(copy)
    copy = pltpu.make_async_copy(rows, all_rows.at[model], local_sem.at[2])
    copy.start()
    locals_.append(copy)

    for w in range(2):
        full = fulls[w]
        for d, t in enumerate(others):
            mine = full.at[0, t, part]
            remote(mine, mine, z_send.at[w, d], z_recv.at[w, t], {"seq": t}).wait_recv()
            go(remote(mine, mine, y_send.at[w, d], y_recv.at[w, t], twin))
            go(remote(mine, full.at[1, t, part], s_send.at[w, d, 0], s_recv.at[w, t, part], mate))
    for w in range(2):
        full = fulls[w]
        for d, t in enumerate(others):
            theirs = full.at[0, t, 1 - part]
            remote(theirs, theirs, y_send.at[w, d], y_recv.at[w, t], twin).wait_recv()
            go(
                remote(
                    theirs,
                    full.at[1, t, 1 - part],
                    s_send.at[w, d, 1],
                    s_recv.at[w, t, 1 - part],
                    mate,
                )
            )
    for w in range(2):
        full = fulls[w]
        own = full.at[1, seq]
        remote(own, own, o_send.at[w], o_recv.at[w], mate).wait_recv()
        for d, t in enumerate(others):
            for h in range(2):
                block = full.at[1, t, h]
                remote(block, block, s_send.at[w, d, h], s_recv.at[w, t, h], mate).wait_recv()
    for d, m in enumerate(models):
        block = all_rows.at[m]
        remote(block, block, x_send.at[d], x_recv.at[m], {"mp": m}).wait_recv()
    for copy in sends:
        copy.wait_send()
    for copy in locals_:
        copy.wait()


def gather_all(first, second, rows):
    peers, halves = (lax.axis_size("seq"), lax.axis_size("mp"))
    depth = first.shape[0] // 2
    shards = tuple(a.reshape(2, depth, -1) for a in (first, second))
    anywhere = pl.BlockSpec(memory_space=pl.ANY)
    dma = pltpu.SemaphoreType.DMA
    out = pl.pallas_call(
        partial(gather_kernel, peers, halves),
        out_shape=tuple(
            jax.ShapeDtypeStruct((2, peers) + a.shape, a.dtype) for a in shards
        )
        + (jax.ShapeDtypeStruct((halves,) + rows.shape, rows.dtype),),
        in_specs=[anywhere] * 3,
        out_specs=(anywhere,) * 3,
        scratch_shapes=[
            dma((3,)),
            dma((2, peers)),
            dma((2, peers)),
            dma((2, peers)),
            dma((2, peers)),
            dma((2, peers, 2)),
            dma((2, peers, 2)),
            dma((2,)),
            dma((2,)),
            dma((halves,)),
            dma((halves,)),
        ],
        compiler_params=pltpu.CompilerParams(collective_id=0, has_side_effects=True),
    )(*shards, rows)
    return (
        out[0].reshape(4 * peers * depth, -1),
        out[1].reshape(4 * peers * depth, -1),
        out[2],
    )


def exchange_kernel(peers, count, *refs):
    sources, targets = refs[:count], refs[count : 2 * count]
    local_sem, send_sem, recv_sem = refs[2 * count :]
    seq = lax.axis_index("seq")
    others = [lax.rem(seq + d, peers) for d in range(1, peers)]

    barrier = pltpu.get_barrier_semaphore()
    for t in others:
        pl.semaphore_signal(
            barrier, inc=1, device_id={"seq": t}, device_id_type=pl.DeviceIdType.MESH
        )
    pl.semaphore_wait(barrier, len(others))

    started = []
    for w in range(count):
        for d, t in enumerate(others):
            copy = pltpu.make_async_remote_copy(
                src_ref=sources[w].at[t],
                dst_ref=targets[w].at[seq],
                send_sem=send_sem.at[w, d],
                recv_sem=recv_sem.at[w, seq],
                device_id={"seq": t},
                device_id_type=pl.DeviceIdType.MESH,
            )
            copy.start()
            started.append(copy)
    own = [
        pltpu.make_async_copy(sources[w].at[seq], targets[w].at[seq], local_sem.at[w])
        for w in range(count)
    ]
    for copy in own:
        copy.start()
    for w in range(count):
        for d, t in enumerate(others):
            block = targets[w].at[t]
            pltpu.make_async_remote_copy(
                src_ref=block,
                dst_ref=block,
                send_sem=send_sem.at[w, d],
                recv_sem=recv_sem.at[w, t],
                device_id={"seq": t},
                device_id_type=pl.DeviceIdType.MESH,
            ).wait_recv()
    for copy in started:
        copy.wait_send()
    for copy in own:
        copy.wait()


def exchange(values):
    peers = lax.axis_size("seq")
    count = len(values)
    blocks = tuple(v.reshape(peers, v.shape[0] // peers, -1) for v in values)
    anywhere = pl.BlockSpec(memory_space=pl.ANY)
    dma = pltpu.SemaphoreType.DMA
    arrived = pl.pallas_call(
        partial(exchange_kernel, peers, count),
        out_shape=tuple(jax.ShapeDtypeStruct(v.shape, v.dtype) for v in blocks),
        in_specs=[anywhere] * count,
        out_specs=(anywhere,) * count,
        scratch_shapes=[dma((count,)), dma((count, peers)), dma((count, peers))],
        compiler_params=pltpu.CompilerParams(collective_id=1, has_side_effects=True),
    )(*blocks)
    return tuple(jnp.sum(v.astype(jnp.float32), axis=0) for v in arrived)


def core_sum(own, other):
    arrived = swap(other, "strand")
    return (own.astype(jnp.float32) + arrived.astype(jnp.float32)).astype(jnp.bfloat16)


def share_sum(own, other):
    return lax.psum_scatter(core_sum(own, other), "seq", scatter_dimension=0, tiled=True)


def on_device(
    hidden,
    breaks,
    cotangent,
    input_weight,
    gate_weight,
    key_weight,
    query_weight,
    step_weight,
    output_weight,
    step_bias,
    decay_log,
    skip_gain,
):
    strand = lax.axis_index("strand")
    backward = strand == 1
    seq_index = lax.axis_index("seq")
    length = hidden.shape[0]
    shard_rows = input_weight.shape[0]
    peers = lax.axis_size("seq")
    halves = lax.axis_size("mp")
    width = shard_rows * peers * 2
    half = shard_rows * peers
    part_width = hidden.shape[1]

    target = lax.broadcasted_iota(jnp.int32, (width, width), 1)
    source = lax.broadcasted_iota(jnp.int32, (width, width), 0)
    local = target % half
    side = jnp.where(target < half, strand, 1 - strand)
    feature = (local // shard_rows) * (2 * shard_rows) + side * shard_rows + local % shard_rows
    feature = jnp.where(backward, width - 1 - feature, feature)
    moves = (source == feature).astype(jnp.bfloat16)
    moves = lax.optimization_barrier(moves)

    key_width = key_weight.shape[1]
    inner_width = input_weight.shape[1]
    ahead = jnp.concatenate(
        (input_weight, gate_weight, key_weight, query_weight, step_weight), axis=1
    )
    ahead_full, out_full, everything = gather_all(
        ahead, output_weight, jnp.stack((hidden, cotangent))
    )

    def permuted(which):
        return sum(
            jnp.dot(
                everything[m, which],
                moves[m * part_width : (m + 1) * part_width],
                preferred_element_type=jnp.float32,
            )
            for m in range(halves)
        ).astype(jnp.bfloat16)

    inputs = permuted(0)
    grads_in = permuted(1)
    break_marks = lax.dynamic_slice_in_dim(breaks, seq_index * length, length).astype(jnp.float32)

    def project(start, size):
        return jnp.dot(
            inputs, ahead_full[:, start : start + size], preferred_element_type=jnp.float32
        )

    groups = key_width // STATE
    key_start = 2 * inner_width
    key_vals = project(key_start, key_width).astype(jnp.bfloat16).reshape(length, groups, STATE)
    query_vals = (
        project(key_start + key_width, key_width)
        .astype(jnp.bfloat16)
        .reshape(length, groups, STATE)
    )
    step_raw = project(key_start + 2 * key_width, step_weight.shape[1])
    inner_vals = project(0, inner_width).astype(jnp.bfloat16).reshape(length, -1, HEAD_DIM)
    gate_vals = project(inner_width, inner_width).astype(jnp.bfloat16).reshape(length, groups, -1)

    local_terms, local_pull = jax.vjp(
        partial(block_terms, backward, step_bias, decay_log, break_marks),
        inner_vals,
        key_vals,
        query_vals,
        step_raw,
    )
    total_log, total_state = local_terms[4:]
    head_shape = total_state.shape[:2]
    heads = total_log.shape[0]
    log_pieces = []
    rest = total_log
    for _ in range(3):
        piece = lax.reduce_precision(rest, 8, 7)
        log_pieces.append(piece)
        rest = rest - piece
    log_rows = jnp.pad(jnp.stack(log_pieces), ((0, 13), (0, STATE - heads)))
    sent = jnp.concatenate(
        (total_state.reshape(-1, STATE).astype(jnp.bfloat16), log_rows.astype(jnp.bfloat16))
    )
    arrived = lax.all_gather(sent, "seq")
    state_rows = heads * HEAD_DIM
    all_logs = jnp.sum(arrived[:, state_rows : state_rows + 3, :heads].astype(jnp.float32), axis=1)
    order = earlier_than(peers, backward)
    chain = chain_weights(order, all_logs)
    here = lax.dynamic_index_in_dim(chain, seq_index, 0, keepdims=False)
    there = lax.dynamic_index_in_dim(chain, seq_index, 1, keepdims=False)

    def chained(everything, weights):
        weights = weights.reshape((peers,) + head_shape)
        return sum(
            weights[k][..., None, None]
            * everything[k].reshape(total_state.shape).astype(jnp.float32)
            for k in range(peers)
        )

    entering = chained(arrived[:, :state_rows], here)
    mixer_out, finish_pull = jax.vjp(
        partial(finish_terms, skip_gain), *local_terms[:4], query_vals, inner_vals, entering
    )
    gated, gate_pull = jax.vjp(gate_terms, mixer_out, gate_vals)
    gated_flat = gated.reshape(length, -1)

    gated_back = jnp.dot(grads_in, out_full, preferred_element_type=jnp.float32).astype(jnp.bfloat16).reshape(gated.shape)
    mixer_back, gate_back = gate_pull(gated_back)
    finish_back = finish_pull(mixer_back)
    carried_back = chained(lax.all_gather(finish_back[6].astype(jnp.bfloat16), "seq"), there)

    contract_rows = (((1,), (1,)), ((), ()))
    head_terms = tuple(
        lax.dot_general(
            gated_flat, part, contract_rows, preferred_element_type=jnp.float32
        ).astype(jnp.bfloat16)
        for part in (out_full[:half], out_full[half:])
    )
    head_terms = jnp.stack(
        [
            sum(
                lax.dot_general(
                    head_terms[s],
                    moves[m * part_width : (m + 1) * part_width, s * half : (s + 1) * half],
                    contract_rows,
                    preferred_element_type=jnp.float32,
                )
                for s in range(2)
            ).astype(jnp.bfloat16)
            for m in range(halves)
        ]
    )
    reduced = lax.psum_scatter(head_terms, "mp", scatter_dimension=0)
    combined = (
        reduced.astype(jnp.float32) + swap(reduced, "strand").astype(jnp.float32)
    ).astype(jnp.bfloat16)

    contract = (((0,), (0,)), ((), ()))

    def grad_pair(left, right):
        return tuple(
            lax.dot_general(part, right, contract, preferred_element_type=jnp.float32).astype(
                jnp.bfloat16
            )
            for part in (left[:, :half], left[:, half:])
        )

    grad_output = share_sum(*grad_pair(grads_in, gated_flat)).astype(jnp.float32)
    grad_gate = share_sum(*grad_pair(inputs, gate_back.reshape(length, -1))).astype(jnp.float32)

    log_back = jnp.sum(carried_back * entering, axis=(-2, -1)).reshape(
        total_log.shape
    ) * jnp.exp(total_log)
    local_back = local_pull((*finish_back[:4], log_back, carried_back))
    inner_back = (local_back[0] + finish_back[5]).reshape(length, -1)
    key_back = local_back[1].reshape(length, -1)
    query_back = (local_back[2] + finish_back[4]).reshape(length, -1)
    step_back = local_back[3]

    input_terms = grad_pair(inputs, inner_back)
    small_terms = tuple(
        jnp.concatenate(
            (
                lax.dot_general(
                    part, key_back, contract, preferred_element_type=jnp.float32
                ).astype(jnp.bfloat16),
                lax.dot_general(
                    part, query_back, contract, preferred_element_type=jnp.float32
                ).astype(jnp.bfloat16),
                lax.dot_general(
                    part.astype(jnp.float32), step_back, contract, precision=HIGHEST
                ).astype(jnp.bfloat16),
            ),
            axis=1,
        )
        for part in (inputs[:, :half], inputs[:, half:])
    )
    grad_input, small_share = exchange((core_sum(*input_terms), core_sum(*small_terms)))
    return (
        combined,
        grad_input,
        grad_gate,
        small_share[:, :key_width],
        small_share[:, key_width : 2 * key_width],
        small_share[:, 2 * key_width :],
        grad_output,
    )


NN = (((1,), (0,)), ((), ()))
NT = (((1,), (1,)), ((), ()))
TN = (((0,), (0,)), ((), ()))
F32 = jnp.float32
BF16 = jnp.bfloat16
CHUNKS = 2


def mm(left, right, dims=NN, **options):
    return lax.dot_general(left, right, dims, preferred_element_type=F32, **options)


def iota(shape, axis):
    return lax.broadcasted_iota(jnp.int32, shape, axis)


def aligned(start, size, unit=None):
    return pl.ds(pl.multiple_of(start, unit or size), size)


def remote(source, target, send, receive, device):
    return pltpu.make_async_remote_copy(
        src_ref=source,
        dst_ref=target,
        send_sem=send,
        recv_sem=receive,
        device_id=device,
        device_id_type=pl.DeviceIdType.MESH,
    )


def mixer_kernel(peers, *refs):
    (
        hidden,
        cotangent,
        input_weight,
        key_weight,
        query_weight,
        gate_weight,
        output_weight,
        step_weight,
        marks_ref,
        bias_ref,
        decay_ref,
        gain_ref,
        combined,
        rg,
        rgs,
        u_ref,
        t_ref,
        w_ref,
        step_ref,
        steps,
        wt,
        seff,
        xbcz,
        dxbc,
        dz_ref,
        gated,
        y_ref,
        r_rows,
        dt_rows,
        k_rows,
        entering,
        state,
        p_ref,
        p_mate,
        acc,
        x_out,
        x_in,
        z_out,
        z_in,
        g_own,
        g_mine,
        g_mate,
        g_out,
        gs_own,
        gs_mine,
        gs_mate,
        gs_out,
        local_sem,
        z_send,
        z_recv,
        x_send,
        x_recv,
        m_send,
        m_recv,
        w_send,
        w_recv,
        s_send,
        s_recv,
        p_send,
        p_recv,
        px_send,
        px_recv,
        pz_send,
        pz_recv,
        g_send,
        g_recv,
        gz_send,
        gz_recv,
        gs_send,
        gs_recv,
        c_sem,
    ) = refs
    part = lax.axis_index("parts")
    seq = lax.axis_index("seq")
    strand = lax.axis_index("strand")
    model = lax.axis_index("mp")
    backward = strand == 1
    twin = {"parts": 1 - part}
    mate = {"strand": 1 - strand}
    side = {"mp": 1 - model}
    others = [lax.rem(seq + d, peers) for d in range(1, peers)]
    has_up, has_down = seq < peers - 1, seq > 0

    length, features = hidden.shape
    half = length // 2
    shard = step_weight.shape[1]
    thin = shard // 2
    shards = 2 * peers
    positions, width = u_ref.shape
    blocks = positions // STRETCH
    heads = bias_ref.shape[0] // peers
    inner = heads * HEAD_DIM
    narrow = inner + 2 * STATE
    per = [slice(h * HEAD_DIM, (h + 1) * HEAD_DIM) for h in range(heads)]
    sources = (hidden, cotangent)
    fulls = (u_ref, t_ref)

    def mirrored(i, count):
        return jnp.where(backward, count - 1 - i, i)

    barrier = pltpu.get_barrier_semaphore()
    targets = [{"seq": t} for t in others] + [twin, mate, side]
    for target in targets:
        pl.semaphore_signal(
            barrier, inc=1, device_id=target, device_id_type=pl.DeviceIdType.MESH
        )
    pl.semaphore_wait(barrier, len(targets))

    chunk = half // CHUNKS

    def piece(a, block, which, core, k):
        return fulls[a].at[
            aligned(block * length + core * half + k * chunk, chunk),
            aligned(which * features, features),
        ]

    def own(a, k):
        return sources[a].at[aligned(strand * half + k * chunk, chunk), :]

    def up(a, block, k, source):
        return remote(
            source,
            piece(a, block, model, strand, k),
            z_send.at[a, 0, block, k],
            z_recv.at[a, block, k],
            {"seq": jnp.minimum(seq + 1, peers - 1)},
        )

    def down(a, block, k, source):
        return remote(
            source,
            piece(a, block, model, strand, k),
            z_send.at[a, 1, block, k],
            z_recv.at[a, block, k],
            {"seq": jnp.maximum(seq - 1, 0)},
        )

    def across(a, block, k, source):
        return remote(
            source,
            piece(a, block, model, strand, k),
            x_send.at[a, block, k],
            x_recv.at[a, block, k],
            side,
        )

    def to_mate(a, block, which, k, core=strand):
        mine = piece(a, block, which, core, k)
        return remote(
            mine, mine, m_send.at[a, block, which, k], m_recv.at[a, block, which, k], mate
        )

    def wait_z(a, block, k):
        mine = piece(a, block, model, strand, k)
        remote(mine, mine, z_send.at[a, 0, block, k], z_recv.at[a, block, k], side).wait_recv()

    def wait_x(a, block, k):
        mine = piece(a, block, 1 - model, strand, k)
        remote(mine, mine, x_send.at[a, block, k], x_recv.at[a, block, k], side).wait_recv()

    def launch_up(a):
        def action():
            for k in range(CHUNKS):
                up(a, seq, k, own(a, k)).start()

        pl.when(has_up)(action)

    def launch_down(a):
        def action():
            for k in range(CHUNKS):
                down(a, seq, k, own(a, k)).start()

        pl.when(has_down)(action)

    def launch_across(a):
        for k in range(CHUNKS):
            across(a, seq, k, own(a, k)).start()

    def near(d, action):
        if d == 0:
            action(seq)
        else:
            pl.when(seq >= d)(lambda: action(seq - d))
            pl.when(seq + d < peers)(lambda: action(seq + d))

    def relay(a, d):
        def pass_on(block, k, more, onward):
            mine = piece(a, block, model, strand, k)
            wait_z(a, block, k)
            pl.when(more)(lambda: onward(a, block, k, mine).start())
            across(a, block, k, mine).start()
            to_mate(a, block, model, k).start()

        for k in range(CHUNKS):
            pl.when(seq >= d)(lambda: pass_on(seq - d, k, has_up, up))
            pl.when(seq + d < peers)(lambda: pass_on(seq + d, k, has_down, down))

    def from_side(a):
        def action(block):
            for k in range(CHUNKS):
                wait_x(a, block, k)
                to_mate(a, block, 1 - model, k).start()

        return action

    def all_here(a):
        for d in range(peers):

            def arrivals(block, d=d):
                for k in range(CHUNKS):
                    if d:
                        to_mate(a, block, model, k, 1 - strand).wait_recv()
                    to_mate(a, block, 1 - model, k, 1 - strand).wait_recv()

            near(d, arrivals)

    def all_sent(a):
        def sent_chunk(block, d, k):
            mine = piece(a, block, model, strand, k)
            across(a, block, k, mine).wait_send()
            if d:
                to_mate(a, block, model, k).wait_send()
            to_mate(a, block, 1 - model, k).wait_send()
            pl.when(jnp.logical_and(has_up, block <= seq))(
                lambda: up(a, block, k, mine).wait_send()
            )
            pl.when(jnp.logical_and(has_down, block >= seq))(
                lambda: down(a, block, k, mine).wait_send()
            )

        for d in range(peers):

            def sent(block, d=d):
                for k in range(CHUNKS):
                    sent_chunk(block, d, k)

            near(d, sent)

    def own_copy(a):
        target = fulls[a].at[
            aligned(seq * length, length), aligned(model * features, features)
        ]
        return pltpu.make_async_copy(sources[a], target, local_sem.at[a])

    weights = (input_weight, key_weight, query_weight, gate_weight, output_weight)
    starts = [0, inner, inner + STATE, narrow, narrow + inner, narrow + 2 * inner]

    def w_rows(block, core, which=None):
        first = (2 * block + core) * shard
        if which is None:
            return aligned(first, shard)
        return aligned(first + which * thin, thin)

    def w_sends(t):
        for weight, first, last in zip(weights, starts, starts[1:]):
            size = last - first
            yield remote(
                weight.at[aligned(part * thin, thin), aligned(t * size, size)],
                w_ref.at[w_rows(seq, strand, part), first:last],
                w_send.at[0, t],
                w_recv.at[0, seq],
                {"seq": t},
            )

    def s_sends(t):
        return remote(
            steps.at[t], step_ref.at[2 * seq + strand], s_send.at[0, t], s_recv.at[0, seq], {"seq": t}
        )

    def own_weights():
        for weight, first, last in zip(weights, starts, starts[1:]):
            size = last - first
            yield pltpu.make_async_copy(
                weight.at[:, aligned(seq * size, size)],
                w_ref.at[w_rows(seq, strand), first:last],
                local_sem.at[2],
            )

    def w_own_to_mate():
        mine = w_ref.at[w_rows(seq, strand), :]
        return remote(mine, mine, w_send.at[0, seq], w_recv.at[0, seq], mate)

    def s_own_to_mate():
        mine = step_ref.at[2 * seq + strand]
        return remote(mine, mine, s_send.at[0, seq], s_recv.at[0, seq], mate)

    def w_move(index, block, core, which, device):
        mine = w_ref.at[w_rows(block, core, which), :]
        return remote(mine, mine, w_send.at[index, block], w_recv.at[index, block], device)

    def s_move(index, block, core):
        mine = step_ref.at[2 * block + core]
        return remote(mine, mine, s_send.at[index, block], s_recv.at[index, block], mate)

    launch_up(0)
    launch_down(0)
    launch_across(0)
    launch_across(1)
    for t in others:
        for copy in w_sends(t):
            copy.start()
    for copy in own_weights():
        copy.start()
    for a in range(2):
        own_copy(a).start()
    pl.when(seq == 0)(lambda: launch_up(1))
    pl.when(seq == peers - 1)(lambda: launch_down(1))

    step_now = step_weight[...]
    for t in others + [seq]:
        taken = iota((16, heads * peers), 1) == iota((16, heads * peers), 0) + heads * t
        taken = jnp.logical_and(taken, iota((16, heads * peers), 0) < heads)
        turned = mm(jnp.where(taken, 1.0, 0.0).astype(BF16), step_now).astype(BF16)
        if t is seq:
            step_ref[2 * seq + strand] = turned
            s_own_to_mate().start()
        else:
            steps[t] = turned
            s_sends(t).start()
    mine = w_ref.at[w_rows(seq, strand), :]
    pltpu.make_async_copy(mine, mine, local_sem.at[2]).wait()
    w_own_to_mate().start()

    def weights_in():
        for t in others:
            w_move(0, t, strand, part, mate).wait_recv()
            w_move(1, t, strand, part, twin).start()
            w_move(2 + part, t, strand, part, mate).start()
            s_move(0, t, strand).wait_recv()
            s_move(1, t, strand).start()

    def weights_twin():
        for t in others:
            w_move(1, t, strand, 1 - part, twin).wait_recv()
            w_move(3 - part, t, strand, 1 - part, mate).start()

    for d in range(1, peers):
        relay(0, d)
        pl.when(seq == d)(lambda: launch_up(1))
        pl.when(peers - 1 - seq == d)(lambda: launch_down(1))
        if d == peers - 1:
            relay(1, 1)
        near(d - 1, from_side(0))
        if d == min(2, peers - 1):
            weights_in()
    weights_twin()

    for t in others:
        for which in range(2):
            w_move(2 + which, t, 1 - strand, which, mate).wait_recv()
        s_move(1, t, 1 - strand).wait_recv()
    theirs = w_ref.at[w_rows(seq, 1 - strand), :]
    remote(theirs, theirs, w_send.at[0, seq], w_recv.at[0, seq], mate).wait_recv()
    s_move(0, seq, 1 - strand).wait_recv()

    row = iota((shard, shard), 0)
    column = iota((shard, shard), 1)
    other = jnp.where(backward, shard - 1 - column, column)
    moves = jnp.where(row == other, 1.0, 0.0).astype(BF16)
    for b in range(shards):
        source = mirrored(b, shards)
        wt[:, b * shard : (b + 1) * shard] = mm(
            w_ref[aligned(source * shard, shard), :], moves, TN
        ).astype(BF16)
        seff[:, b * shard : (b + 1) * shard] = mm(step_ref[source], moves).astype(BF16)

    near(peers - 1, from_side(0))
    near(0, from_side(1))

    lead = iota((STRETCH, STRETCH), 0) - iota((STRETCH, STRETCH), 1)
    lead = jnp.where(backward, -lead, lead)
    causal = lead >= 0
    sums_to = (lead <= 0).astype(F32)
    sums_from = (lead >= 0).astype(F32)
    sums_before = (lead < 0).astype(F32)
    bias = jnp.zeros((8, STRETCH), F32)
    rates = jnp.zeros((8, STRETCH), F32)
    for h in range(heads):
        at_head = iota((8, STRETCH), 0) == h
        bias = jnp.where(at_head, bias_ref[seq * heads + h], bias)
        rates = jnp.where(at_head, decay_ref[seq * heads + h], rates)
    rates = -jnp.exp(rates)
    filler = jnp.zeros((128 - 8, STRETCH), F32)
    gains = [gain_ref[seq * heads + h] for h in range(heads)]

    def stacked(parts):
        return jnp.concatenate(parts, axis=0)

    def row(value, h):
        return value[h : h + 1, :]

    def decay_of(cols, k, h):
        return jnp.exp(jnp.where(causal, cols[:, h : h + 1] - row(k, h), -1e30))

    all_here(0)
    for a in range(2):
        own_copy(a).wait()
    state[...] = jnp.zeros_like(state)

    def p_to_mate(t):
        return remote(
            p_ref.at[aligned(t * length + (1 - strand) * half, half), :],
            p_mate.at[t],
            p_send.at[t],
            p_recv.at[t],
            mate,
        )

    def far_first(n):
        t = 0
        for s in range(peers):
            order = sorted(range(peers), key=lambda b: (-abs(b - s), -b if s < peers / 2 else b))
            t = jnp.where(seq == s, order[n], t)
        return t


    def turn(j):
        return lax.rem(seq + 1 + j, peers)

    def p_across(t):
        return remote(x_out.at[t], x_in.at[t], px_send.at[t], px_recv.at[t], side)

    def p_along(t, upward):
        return remote(
            z_out.at[t],
            z_in.at[0 if upward else 1, t],
            pz_send.at[t],
            pz_recv.at[0 if upward else 1, t],
            {"seq": jnp.minimum(seq + 1, peers - 1) if upward else jnp.maximum(seq - 1, 0)},
        )

    def pass_sum(slot):
        def one(t, upward, more):
            came = 0 if upward else 1

            def both():
                p_along(t, upward).wait_recv()
                z_out[t] = (acc[t] + z_in[came, t].astype(F32)).astype(BF16)

            def alone():
                z_out[t] = acc[t].astype(BF16)

            pl.when(more)(both)
            pl.when(jnp.logical_not(more))(alone)
            p_along(t, upward).start()

        pl.when(seq <= slot)(lambda: one(peers - 1 + seq - slot, True, has_down))
        pl.when(peers - 1 - seq <= slot)(lambda: one(slot - (peers - 1 - seq), False, has_up))

    def add_core(t):
        p_to_mate(t).wait_recv()
        rows = aligned(t * length + strand * half, half)
        there = aligned((1 - model) * features, features)
        here = aligned(model * features, features)
        x_out[t] = (p_ref[rows, there].astype(F32) + p_mate[t, :, there].astype(F32)).astype(BF16)
        p_across(t).start()
        acc[t] = p_ref[rows, here].astype(F32) + p_mate[t, :, here].astype(F32)

    def add_side(t):
        p_across(t).wait_recv()
        acc[t] = acc[t] + x_in[t].astype(F32)

    def forward(c, carry):
        for d in range(1, peers - 1):
            pl.when(c == 3 * d - 3)(lambda d=d: relay(1, d + 1))
            pl.when(c == 3 * d - 1)(lambda d=d: near(d, from_side(1)))
        blk = mirrored(c, blocks)
        at = aligned(blk * STRETCH, STRETCH)
        lanes = aligned(blk * STRETCH, STRETCH)
        u = u_ref[at, :]
        projected = mm(wt[: narrow + inner, :], u, NT).astype(BF16)
        xbcz[:, lanes] = projected
        x = projected[:inner]
        b = projected[inner : inner + STATE]
        q = projected[inner + STATE : narrow]
        z = projected[narrow:].astype(F32)
        r = mm(seff[...], u, NT)[:8] + bias
        dt = jnp.maximum(r, 0.0) + jnp.log1p(jnp.exp(-jnp.abs(r)))
        marks = jnp.concatenate(
            [marks_ref[pl.ds(2 * blk + i, 1), :] for i in range(2)], axis=1
        ).astype(F32)
        a = rates * dt + KEEP_LOG * marks
        k = mm(a, sums_to, precision=HIGHEST)
        end = jnp.sum(a, axis=1, keepdims=True)
        r_rows[blk] = r
        dt_rows[blk] = dt
        k_rows[blk] = stacked((k, jnp.broadcast_to(end, k.shape)))
        cols = jnp.transpose(stacked((k, filler)))
        scores = mm(q, b, TN)
        grow = jnp.exp(k)
        weight = jnp.exp(end - k) * dt
        keep_all = jnp.exp(end)
        before = state[...]
        entering[blk] = before
        carried = mm(before.astype(BF16), q)
        xf = x.astype(F32)
        ys, es, kept = [], [], []
        for h in range(heads):
            mixing = (scores * decay_of(cols, k, h) * row(dt, h)).astype(BF16)
            y_h = mm(x[per[h]], mixing, NT)
            ys.append(y_h + row(grow, h) * carried[per[h]] + gains[h] * xf[per[h]])
            es.append((row(weight, h) * xf[per[h]]).astype(BF16))
            kept.append(row(keep_all, h) * before[per[h]])
        state[...] = stacked(kept) + mm(stacked(es), b, NT)
        y = stacked(ys)
        y_ref[:, lanes] = y

        v = y * (z / (1.0 + jnp.exp(-z)))
        scale = lax.rsqrt(jnp.mean(v * v, axis=0, keepdims=True) + EPSILON)
        g = (v * scale).astype(BF16)
        gated[:, lanes] = g
        p_ref[at, :] = mm(g, wt[narrow + inner :, :], TN).astype(BF16)
        pl.when(lax.rem(c, 2) == 1)(lambda: p_to_mate(blk // 2).start())
        return carry

    lax.fori_loop(0, blocks, forward, 0)

    near(peers - 1, from_side(1))
    add_core(far_first(0))

    def sums(slot):
        add_side(far_first(slot))
        pass_sum(slot)

    all_here(1)

    def gate_back(c, carry):
        at = aligned(c * STRETCH, STRETCH)
        z = xbcz[narrow:, at].astype(F32)
        y = y_ref[:, at]
        sig = 1.0 / (1.0 + jnp.exp(-z))
        silu = z * sig
        v = y * silu
        scale = lax.rsqrt(jnp.mean(v * v, axis=0, keepdims=True) + EPSILON)
        dg = mm(wt[narrow + inner :, :], t_ref[at, :], NT).astype(BF16).astype(F32)
        along = jnp.mean(dg * v, axis=0, keepdims=True)
        dv = scale * (dg - v * (scale * scale * along))
        y_ref[:, at] = dv * silu
        dz_ref[:, at] = (dv * y * (sig * (1.0 + z * (1.0 - sig)))).astype(BF16)
        return carry

    lax.fori_loop(0, blocks, gate_back, 0)
    add_core(far_first(1))
    sums(0)

    def g_to_mate(part_of, t):
        return remote(
            g_own.at[part_of, t],
            g_mate.at[part_of, t],
            g_send.at[part_of, t],
            g_recv.at[part_of, t],
            mate,
        )

    def g_along(part_of, t):
        return remote(
            g_out.at[part_of, t],
            rg.at[part_of, seq],
            gz_send.at[part_of, t],
            gz_recv.at[part_of, seq],
            {"seq": t},
        )

    def gs_to_mate(t):
        return remote(gs_own.at[t], gs_mate.at[t], gs_send.at[0, t], gs_recv.at[0, t], mate)

    def gs_along(t):
        return remote(gs_out.at[t], rgs.at[seq], gs_send.at[1, t], gs_recv.at[1, seq], {"seq": t})

    def columns_at(t):
        return aligned(mirrored(t, peers) * 2 * shard, 2 * shard)

    def early_terms(t):
        at = columns_at(t)
        return stacked((mm(dz_ref[...], u_ref[:, at]), mm(gated[...], t_ref[:, at]))).astype(BF16)

    def late_terms(t):
        found = mm(dxbc[...], u_ref[:, columns_at(t)])
        steps_found = found[narrow : narrow + 8] + found[narrow + 8 :]
        steps_found = stacked((steps_found, jnp.zeros_like(steps_found))).astype(BF16)
        gs_own[t] = mm(steps_found[:, shard:], moves).astype(BF16)
        gs_mine[t] = mm(steps_found[:, :shard], moves)
        gs_to_mate(t).start()
        return found[:narrow].astype(BF16)

    def weigh(part_of, terms):
        def first(j, carry):
            t = turn(j)
            found = terms(t)
            g_own[part_of, t] = mm(moves, found[:, shard:], NT).astype(BF16)
            g_to_mate(part_of, t).start()
            g_mine[t] = mm(moves, found[:, :shard], NT)
            return carry

        def second(j, carry):
            t = turn(j)
            g_to_mate(part_of, t).wait_recv()
            total = (g_mine[t] + g_mate[part_of, t].astype(F32)).astype(BF16)
            if part_of:
                gs_to_mate(t).wait_recv()
                steps_total = (gs_mine[t] + gs_mate[t].astype(F32)).astype(BF16)

            def send():
                g_out[part_of, t] = total
                g_along(part_of, t).start()
                if part_of:
                    gs_out[t] = steps_total
                    gs_along(t).start()

            def keep():
                rg[part_of, t] = total
                if part_of:
                    rgs[t] = steps_total

            pl.when(j < peers - 1)(send)
            pl.when(j == peers - 1)(keep)
            return carry

        def both(j, carry):
            return second(j - 1, first(j, carry))

        first(0, 0)
        lax.fori_loop(1, peers, both, 0)
        second(peers - 1, 0)

    state[...] = jnp.zeros_like(state)

    weigh(0, early_terms)

    add_core(far_first(2))

    def backwards(c, carry):
        for n in range(3, peers):
            pl.when(c == n - 2)(lambda n=n: add_core(far_first(n)))
        for slot in range(1, peers - 1):
            pl.when(c == min(5 * slot - 3, blocks - 1))(lambda slot=slot: sums(slot))
        blk = mirrored(blocks - 1 - c, blocks)
        at = aligned(blk * STRETCH, STRETCH)
        x = xbcz[:inner, at]
        b = xbcz[inner : inner + STATE, at]
        q = xbcz[inner + STATE : narrow, at]
        xf = x.astype(F32)
        dy = y_ref[:, at]
        dyb = dy.astype(BF16)
        dt = dt_rows[blk]
        k = k_rows[blk, :8]
        end = k_rows[blk, 8:]
        cols = jnp.transpose(stacked((k, filler)))
        before = entering[blk]
        leaving = state[...]
        before_b = before.astype(BF16)
        leaving_b = leaving.astype(BF16)
        before_t = jnp.transpose(before).astype(BF16)
        leaving_t = jnp.transpose(leaving).astype(BF16)
        keep = jnp.exp(end - k)
        weight = keep * dt
        grow = jnp.exp(k)
        keep_all = jnp.exp(end[:, :STATE])

        de = mm(leaving_b, b)
        carried = mm(before_b, q)
        scores = mm(q, b, TN)
        dscores = jnp.zeros((STRETCH, STRETCH), F32)
        row_sums = jnp.zeros((STRETCH, 128), F32)
        lane = iota((STRETCH, 128), 1)
        none = jnp.zeros((8 - heads, STRETCH), F32)
        dxs, es, growns, kept, ddts, dks, columns, totals = [], [], [], [], [], [], [], []
        for h in range(heads):
            x_h, de_h, dy_h = xf[per[h]], de[per[h]], dy[per[h]]
            ddts.append(jnp.sum(de_h * x_h, axis=0, keepdims=True) * row(keep, h))
            es.append((x_h * row(weight, h)).astype(BF16))
            grown = row(grow, h) * dy_h
            growns.append(grown.astype(BF16))
            dks.append(jnp.sum(grown * carried[per[h]], axis=0, keepdims=True))
            held = row(keep_all, h) * leaving[per[h]]
            kept.append(held)
            totals.append(jnp.sum(before[per[h]] * held, axis=0, keepdims=True))

            decay = decay_of(cols, k, h)
            dmix = mm(dyb[per[h]], x[per[h]], TN) * decay
            mixing = (scores * decay * row(dt, h)).astype(BF16)
            dx_h = mm(dyb[per[h]], mixing)
            dxs.append((dx_h + de_h * row(weight, h) + gains[h] * dy_h).astype(BF16))
            scaled = dmix * row(dt, h)
            dscores = dscores + scaled
            columns.append(jnp.sum(dmix * scores, axis=0, keepdims=True))
            summed = jnp.sum(scaled * scores, axis=1, keepdims=True)
            row_sums = jnp.where(lane == h, summed, row_sums)
        grown = stacked(growns)
        dscores_b = dscores.astype(BF16)
        dq = mm(before_t, grown) + mm(b, dscores_b, NT)
        db = mm(leaving_t, stacked(es)) + mm(q, dscores_b)
        state[...] = stacked(kept) + mm(grown, q, NT)
        dxbc[:inner, at] = stacked(dxs)
        dxbc[inner : inner + STATE, at] = db.astype(BF16)
        dxbc[inner + STATE : narrow, at] = dq.astype(BF16)

        ddt = stacked(ddts + [none])
        columns = stacked(columns + [none])
        total = jnp.sum(stacked(totals + [none[:, :STATE]]), axis=1, keepdims=True)
        dk = stacked(dks + [none]) + jnp.transpose(row_sums)[:8] - dt * columns
        da = mm(dk, sums_from, precision=HIGHEST)
        da = da + mm(dt * ddt, sums_before, precision=HIGHEST) + total
        ddt = ddt + columns + rates * da
        dr = ddt / (1.0 + jnp.exp(-r_rows[blk]))
        high = dr.astype(BF16).astype(F32)
        dxbc[narrow:, at] = stacked((high, dr - high)).astype(BF16)
        return carry

    lax.fori_loop(0, blocks, backwards, 0)

    weigh(1, late_terms)

    add_side(far_first(peers - 1))

    def add_along(upward):
        p_along(seq, upward).wait_recv()
        acc[seq] = acc[seq] + z_in[0 if upward else 1, seq].astype(F32)

    pl.when(has_down)(lambda: add_along(True))
    pl.when(has_up)(lambda: add_along(False))
    total = acc[seq]
    mine = aligned(strand * half, half)
    combined[mine, :] = total.astype(BF16)
    rows = combined.at[mine, :]
    last = remote(rows, rows, c_sem.at[0], c_sem.at[1], mate)
    last.start()

    for t in others:
        for i in range(2):
            remote(
                rg.at[i, t], rg.at[i, t], gz_send.at[i, t], gz_recv.at[i, t], {"seq": t}
            ).wait_recv()
        remote(
            rgs.at[t], rgs.at[t], gs_send.at[1, t], gs_recv.at[1, t], {"seq": t}
        ).wait_recv()
    theirs = combined.at[aligned((1 - strand) * half, half), :]
    remote(theirs, theirs, c_sem.at[0], c_sem.at[1], mate).wait_recv()
    last.wait_send()
    for a in range(2):
        all_sent(a)
    for t in others:
        w_move(0, t, strand, part, mate).wait_send()
        w_move(1, t, strand, part, twin).wait_send()
        w_move(2 + part, t, strand, part, mate).wait_send()
        w_move(3 - part, t, strand, 1 - part, mate).wait_send()
        s_sends(t).wait_send()
        s_move(1, t, strand).wait_send()
        p_along(t, True).wait_send()
        gs_along(t).wait_send()
        for i in range(2):
            g_along(i, t).wait_send()
    w_own_to_mate().wait_send()
    s_own_to_mate().wait_send()
    for t in others + [seq]:
        p_to_mate(t).wait_send()
        p_across(t).wait_send()
        gs_to_mate(t).wait_send()
        for i in range(2):
            g_to_mate(i, t).wait_send()


def finish_kernel(
    heads, combined, rg, rgs, out, g_in, g_gate, g_key, g_query, g_step, g_out, here, here_s, sems
):
    peers = rg.shape[1]
    inner = g_in.shape[1] // peers
    copies = [pltpu.make_async_copy(rgs, here_s, sems.at[0])]
    for s in range(peers):
        copies.append(pltpu.make_async_copy(rg.at[:, s], here.at[:, s], sems.at[2 + s]))
    last = pltpu.make_async_copy(combined, out, sems.at[1])
    for copy in copies + [last]:
        copy.start()
    copies[0].wait()
    for s in range(peers):
        g_step[heads * s : heads * (s + 1), :] = here_s[s].astype(F32)[:heads]
    for s in range(peers):
        copies[1 + s].wait()
        early, late = here[0, s].astype(F32), here[1, s].astype(F32)
        wide = slice(s * inner, (s + 1) * inner)
        small = slice(s * STATE, (s + 1) * STATE)
        g_gate[:, wide] = early[:, :inner]
        g_out[:, wide] = early[:, inner:]
        g_in[:, wide] = late[:, :inner]
        g_key[:, small] = late[:, inner : inner + STATE]
        g_query[:, small] = late[:, inner + STATE :]
    last.wait()


def by_group(
    hidden,
    breaks,
    cotangent,
    input_weight,
    gate_weight,
    key_weight,
    query_weight,
    step_weight,
    output_weight,
    step_bias,
    decay_log,
    skip_gain,
):
    peers, models = lax.axis_size("seq"), lax.axis_size("mp")
    length, features = hidden.shape
    half = length // 2
    shard = input_weight.shape[0]
    positions, width = length * peers, features * models
    blocks = positions // STRETCH
    heads = step_bias.shape[0] // peers
    inner = heads * HEAD_DIM
    narrow = inner + 2 * STATE
    columns = narrow + 2 * inner
    dma = pltpu.SemaphoreType.DMA
    anywhere = pl.BlockSpec(memory_space=pl.ANY)
    vmem = pl.BlockSpec(memory_space=pltpu.VMEM)
    smem = pl.BlockSpec(memory_space=pltpu.SMEM)
    strips = pltpu.VMEM((2, peers, shard, 2 * inner), BF16)
    steps = pltpu.VMEM((peers, 16, shard), BF16)
    rows8 = pltpu.VMEM((blocks, 8, STRETCH), F32)
    halves = pltpu.VMEM((peers, half, features), BF16)
    combined, rg, rgs = pl.pallas_call(
        partial(mixer_kernel, peers),
        out_shape=(
            jax.ShapeDtypeStruct((length, features), BF16),
            jax.ShapeDtypeStruct((2, peers, shard, 2 * inner), BF16),
            jax.ShapeDtypeStruct((peers, 16, shard), BF16),
        ),
        in_specs=[anywhere] * 7 + [vmem] * 2 + [smem] * 3,
        out_specs=(vmem,) * 3,
        scratch_shapes=[
            pltpu.VMEM((positions, width), BF16),
            pltpu.VMEM((positions, width), BF16),
            pltpu.VMEM((width, columns), BF16),
            pltpu.VMEM((2 * peers, 16, shard), BF16),
            steps,
            pltpu.VMEM((columns, width), BF16),
            pltpu.VMEM((16, width), BF16),
            pltpu.VMEM((narrow + inner, positions), BF16),
            pltpu.VMEM((narrow + 16, positions), BF16),
            pltpu.VMEM((inner, positions), BF16),
            pltpu.VMEM((inner, positions), BF16),
            pltpu.VMEM((inner, positions), F32),
            rows8,
            rows8,
            pltpu.VMEM((blocks, 16, STRETCH), F32),
            pltpu.VMEM((blocks, inner, STATE), F32),
            pltpu.VMEM((inner, STATE), F32),
            pltpu.VMEM((positions, width), BF16),
            pltpu.VMEM((peers, half, width), BF16),
            pltpu.VMEM((peers, half, features), F32),
            halves,
            halves,
            halves,
            pltpu.VMEM((2, peers, half, features), BF16),
            strips,
            pltpu.VMEM((peers, shard, narrow), F32),
            strips,
            strips,
            steps,
            pltpu.VMEM((peers, 16, shard), F32),
            steps,
            steps,
            dma((3,)),
            dma((2, 2, peers, CHUNKS)),
            dma((2, peers, CHUNKS)),
            dma((2, peers, CHUNKS)),
            dma((2, peers, CHUNKS)),
            dma((2, peers, 2, CHUNKS)),
            dma((2, peers, 2, CHUNKS)),
            dma((4, peers)),
            dma((4, peers)),
            dma((2, peers)),
            dma((2, peers)),
            dma((peers,)),
            dma((peers,)),
            dma((peers,)),
            dma((peers,)),
            dma((peers,)),
            dma((2, peers)),
            dma((2, peers)),
            dma((2, peers)),
            dma((2, peers)),
            dma((2, peers)),
            dma((2, peers)),
            dma((2, peers)),
            dma((2,)),
        ],
        compiler_params=pltpu.CompilerParams(
            collective_id=2, has_side_effects=True, vmem_limit_bytes=60 * 1024 * 1024
        ),
    )(
        hidden,
        cotangent,
        input_weight,
        key_weight,
        query_weight,
        gate_weight,
        output_weight,
        jnp.transpose(step_weight),
        breaks.reshape(-1, 128),
        step_bias,
        decay_log,
        skip_gain,
    )

    wide = jax.ShapeDtypeStruct((shard, peers * inner), F32)
    small = jax.ShapeDtypeStruct((shard, peers * STATE), F32)
    out, g_in, g_gate, g_key, g_query, g_step, g_out = pl.pallas_call(
        partial(finish_kernel, heads),
        out_shape=(
            jax.ShapeDtypeStruct(combined.shape, BF16),
            wide,
            wide,
            small,
            small,
            jax.ShapeDtypeStruct((peers * heads, shard), F32),
            wide,
        ),
        in_specs=[anywhere] * 3,
        out_specs=(vmem,) * 7,
        scratch_shapes=[
            pltpu.VMEM(rg.shape, BF16),
            pltpu.VMEM(rgs.shape, BF16),
            dma((2 + peers,)),
        ],
        compiler_params=pltpu.CompilerParams(vmem_limit_bytes=60 * 1024 * 1024),
    )(combined, rg, rgs)
    return out, g_in, g_gate, g_key, g_query, jnp.transpose(g_step), g_out


def solution(mesh):
    in_specs = (
        P(("parts", "seq"), "mp"),
        P("parts"),
        P(("parts", "seq"), "mp"),
        P(("seq", "strand"), "mp"),
        P(("seq", "strand"), "mp"),
        P(("seq", "strand"), "mp"),
        P(("seq", "strand"), "mp"),
        P(("seq", "strand"), "mp"),
        P(("seq", "strand"), "mp"),
        P("mp"),
        P("mp"),
        P("mp"),
    )
    out_specs = (
        P(("parts", "seq"), "mp"),
        P(("parts", "seq", "strand"), "mp"),
        P(("parts", "seq", "strand"), "mp"),
        P(("parts", "seq", "strand"), "mp"),
        P(("parts", "seq", "strand"), "mp"),
        P(("parts", "seq", "strand"), "mp"),
        P(("parts", "seq", "strand"), "mp"),
    )
    peers = mesh.shape["seq"]

    def each(*args):
        groups = args[5].shape[1] // STATE
        heads = args[9].shape[0]
        fits = peers == groups == 4 and heads == 4 * groups and mesh.shape["mp"] == 2
        return (by_group if fits else on_device)(*args)

    return jax.shard_map(
        each, mesh=mesh, in_specs=in_specs, out_specs=out_specs, check_vma=False
    )
```
